32 devices in a mesh: dp: 8 (over z, y), seq: 4 (over x, core).
Axes of the slice: x: 2, y: 2, z: 4, core: 2. Of those that a mesh axis runs over, the one named last changes fastest.
Arguments:
- layer_in: bfloat16 [16, 832, 768], P('dp', 'seq'), may hold values from -6 to 6
- out_grad: bfloat16 [16, 832, 768], P('dp', 'seq'), may hold values from -6 to 6
- pre_gain: float32 [768], replicated, may hold values from 0.5 to 1.5
- pre_bias: float32 [768], replicated, may hold values from -1.75 to 1.75
- query_key_value_weight: bfloat16 [768, 2304], replicated, may hold values from -0.3125 to 0.3125
- q_bias: float32 [768], replicated, may hold values from -3 to 3
- v_bias: float32 [768], replicated, may hold values from -3 to 3
- output_weight: bfloat16 [768, 768], replicated, may hold values from -1.75 to 1.75
- attention_output_bias: float32 [768], replicated, may hold values from -1.75 to 1.75
- mid_gain: float32 [768], replicated, may hold values from 0.5 to 1.5
- mid_bias: float32 [768], replicated, may hold values from -1.75 to 1.75
- up_weight: bfloat16 [768, 3072], replicated, may hold values from -0.21875 to 0.21875
- input_ffn_bias: float32 [3072], replicated, may hold values from -3 to 3
- down_weight: bfloat16 [3072, 768], replicated, may hold values from -0.109375 to 0.109375
- output_ffn_bias: float32 [768], replicated, may hold values from -1.75 to 1.75
- patch_keep: int32 [16, 196], P('dp'), may hold values 0 or 1
- text_len: int32 [16], P('dp'), may hold values from 1 to 512
Outputs:
- layer_out: bfloat16 [16, 832, 768], P('dp', 'seq')
- in_grad: bfloat16 [16, 832, 768], P('dp', 'seq')
- d_pregain: float32 [768], P(('dp', 'seq'))
- d_prebias: float32 [768], P(('dp', 'seq'))
- d_qkv: float32 [768, 2304], P(('dp', 'seq'))
- d_qbias: float32 [768], P(('dp', 'seq'))
- d_vbias: float32 [768], P(('dp', 'seq'))
- d_wout: float32 [768, 768], P(('dp', 'seq'))
- d_outbias: float32 [768], P(('dp', 'seq'))
- d_midgain: float32 [768], P(('dp', 'seq'))
- d_midbias: float32 [768], P(('dp', 'seq'))
- d_wup: float32 [768, 3072], P(('dp', 'seq'))
- d_upbias: float32 [3072], P(('dp', 'seq'))
- d_wdown: float32 [3072, 768], P(('dp', 'seq'))
- d_downbias: float32 [768], P(('dp', 'seq'))
The draws below stay inside these ranges and needn't reach their ends.
All inputs are finite; a program needn't handle non-finite values. No bound on the sum of `patch_keep` on one device may be relied on, other than what follows from the above.
Results may differ from the reference program's by a relative error of at most 0.015.
Values may be sent and summed in bfloat16 or wider, within the bound.
A program may use at most 192 MiB of HBM per device.

```python
import math
import jax
import jax.numpy as jnp
from jax import lax

D = 768
FF = 3072
HEADS = 12
HEAD_DIM = 64
PATCHES = 196
TEXT = 512
L = 832
SEQS = 16


def touch_ends(array, own_key, low, top_value):
    place = [jax.random.randint(jax.random.fold_in(own_key, axis), (), 0, length) for axis, length in enumerate(array.shape)]
    main_axis = array.shape.index(max(array.shape))
    neighbour = place[:main_axis] + [(place[main_axis] + 1) % array.shape[main_axis]] + place[main_axis + 1:]
    return array.at[tuple(place)].set(low).at[tuple(neighbour)].set(top_value)


def steps_of(rng, dims, cuts, least, high):
    loudness, own = 1.0, jax.random.fold_in(rng, 6)
    for position, parts in cuts:
        draws = jnp.exp(jax.random.uniform(jax.random.fold_in(own, position), (parts,), jnp.float32, least / len(cuts), high / len(cuts)))
        loudness = loudness * jnp.repeat(draws, dims[position] // parts).reshape([-1 if axis == position else 1 for axis in range(len(dims))])
    return loudness


def bell_draw(own_key, extent, scale, bound, split=(), kind=jnp.bfloat16):
    values = scale * jax.random.normal(own_key, extent, jnp.float32)
    if split:
        values = values * steps_of(own_key, extent, split, -0.22, 0.18)
    return jnp.clip(values, -bound, bound).astype(kind)


def setup_inputs(seed: int = 0) -> dict:
    keys = jax.random.split(jax.random.key(seed), 18)
    layer_in = bell_draw(keys[0], (SEQS, L, D), 1.0, 6.0, ((0, 8), (1, 4)))
    out_grad = bell_draw(keys[1], (SEQS, L, D), 1.0, 6.0, ((0, 8), (1, 4)))
    pre_gain = jnp.clip(1.0 + 0.1 * jax.random.normal(keys[2], (D,), jnp.float32), 0.5, 1.5)
    pre_bias = bell_draw(keys[3], (D,), 0.3, 1.75, (), jnp.float32)
    query_key_value_weight = bell_draw(keys[4], (D, 3 * D), (D // 2) ** -0.5, 0.3125)
    q_bias = bell_draw(keys[5], (D,), 0.5, 3.0, (), jnp.float32)
    v_bias = bell_draw(keys[6], (D,), 0.5, 3.0, (), jnp.float32)
    output_weight = bell_draw(keys[7], (D, D), (D // 64) ** -0.5, 1.75)
    attention_output_bias = bell_draw(keys[8], (D,), 0.3, 1.75, (), jnp.float32)
    mid_gain = jnp.clip(1.0 + 0.1 * jax.random.normal(keys[9], (D,), jnp.float32), 0.5, 1.5)
    mid_bias = bell_draw(keys[10], (D,), 0.3, 1.75, (), jnp.float32)
    up_weight = bell_draw(keys[11], (D, FF), D ** -0.5, 0.21875)
    input_ffn_bias = bell_draw(keys[12], (FF,), 0.5, 3.0, (), jnp.float32)
    down_weight = bell_draw(keys[13], (FF, D), FF ** -0.5, 0.109375)
    output_ffn_bias = bell_draw(keys[14], (D,), 0.3, 1.75, (), jnp.float32)
    patch_keep = touch_ends((jax.random.randint(keys[15], (SEQS, PATCHES), 0, 5) < 3).astype(jnp.int32), jax.random.fold_in(keys[15], 1), 0, 1)
    text_len = touch_ends(jax.random.randint(keys[16], (SEQS,), 1, TEXT + 1), jax.random.fold_in(keys[16], 1), 1, TEXT).astype(jnp.int32)
    return dict(layer_in=layer_in, out_grad=out_grad, pre_gain=pre_gain, pre_bias=pre_bias, query_key_value_weight=query_key_value_weight, q_bias=q_bias, v_bias=v_bias, output_weight=output_weight, attention_output_bias=attention_output_bias, mid_gain=mid_gain, mid_bias=mid_bias, up_weight=up_weight, input_ffn_bias=input_ffn_bias, down_weight=down_weight, output_ffn_bias=output_ffn_bias, patch_keep=patch_keep, text_len=text_len)


@jax.custom_vjp
def low(v):
    return lax.optimization_barrier(v.astype(jnp.bfloat16)).astype(jnp.float32)

@jax.custom_vjp
def reduced_backward(v):
    return v

def low_keep(v):
    return (low(v), None)

def low_pass(kept, grad):
    return (grad,)

def back_keep(v):
    return (v, None)

def back_low(kept, grad):
    return (low(grad),)
low.defvjp(low_keep, low_pass)
reduced_backward.defvjp(back_keep, back_low)
precise_setting = lax.Precision.HIGHEST

def layer_norm(values, gain_vec, shift_vec):
    center = values - lax.optimization_barrier(jnp.mean(values, axis=-1, keepdims=True))
    spread = lax.optimization_barrier(jnp.mean(center * center, axis=-1, keepdims=True))
    return center * lax.rsqrt(spread + 1e-06) * gain_vec + shift_vec

def key_valid(patch_keep, text_len, full_len):
    seq_count = patch_keep.shape[0]
    tokens = (jnp.arange(TEXT, dtype=jnp.int32)[None, :] < text_len[:, None]).astype(jnp.int32)
    pieces = [jnp.ones((seq_count, 2), jnp.int32), patch_keep.astype(jnp.int32), jnp.ones((seq_count, 1), jnp.int32), tokens, jnp.zeros((seq_count, full_len - 3 - PATCHES - TEXT), jnp.int32)]
    return jnp.concatenate(pieces, axis=1) > 0

def forward(layer_inputs, weights, key_mask):
    pre_gain, pre_bias, query_key_value_weight, q_bias, v_bias, output_weight, attention_output_bias, mid_gain, mid_bias, up_weight, input_ffn_bias, down_weight, output_ffn_bias = weights
    model_width = layer_inputs.shape[-1]
    head_shape = layer_inputs.shape[:2] + (HEADS, HEAD_DIM)
    first_normed = low(layer_norm(layer_inputs, pre_gain, pre_bias))
    projected_output = reduced_backward(jnp.einsum('kom,mj->koj', first_normed, query_key_value_weight, precision=precise_setting))
    queries = low((projected_output[..., :model_width] + q_bias) * 0.125)
    key_rows = low(projected_output[..., model_width:2 * model_width])
    value_rows = low(projected_output[..., 2 * model_width:] + v_bias)
    scores = reduced_backward(jnp.einsum('sqhc,skhc->shqk', queries.reshape(head_shape), key_rows.reshape(head_shape), precision=precise_setting))
    masked = jnp.where(key_mask[:, None, None, :], scores, -1e+30)
    top_score = lax.optimization_barrier(jnp.max(masked, axis=-1, keepdims=True))
    exponent = jnp.exp(masked - top_score)
    attention = exponent / lax.optimization_barrier(jnp.sum(exponent, axis=-1, keepdims=True))
    attended_context = jnp.einsum('shqk,skhc->sqhc', low(attention), value_rows.reshape(head_shape), precision=precise_setting).reshape(layer_inputs.shape)
    attended_context = reduced_backward(low(attended_context))
    middle_state = layer_inputs + reduced_backward(jnp.einsum('kom,mj->koj', attended_context, output_weight, precision=precise_setting)) + attention_output_bias
    second_normed = low(layer_norm(middle_state, mid_gain, mid_bias))
    preactivation = reduced_backward(jnp.einsum('tzq,qb->tzb', second_normed, up_weight, precision=precise_setting)) + input_ffn_bias
    hidden_state = low(jax.nn.gelu(preactivation, approximate=False))
    return middle_state + jnp.einsum('qzb,bo->qzo', hidden_state, down_weight, precision=precise_setting) + output_ffn_bias

def reference(layer_in, out_grad, pre_gain, pre_bias, query_key_value_weight, q_bias, v_bias, output_weight, attention_output_bias, mid_gain, mid_bias, up_weight, input_ffn_bias, down_weight, output_ffn_bias, patch_keep, text_len):
    params = tuple((member.astype(jnp.float32) for member in (pre_gain, pre_bias, query_key_value_weight, q_bias, v_bias, output_weight, attention_output_bias, mid_gain, mid_bias, up_weight, input_ffn_bias, down_weight, output_ffn_bias)))
    key_mask = key_valid(patch_keep, text_len, L)
    group_size = 4 if SEQS % 4 == 0 else 1
    blocks = SEQS // group_size

    def regroup(values_in):
        return values_in.reshape((blocks, group_size) + values_in.shape[1:])

    def group_step(totals, block_data):
        layer_inputs, cotangent, mask_rows = block_data

        def apply_layer(layer_rows, *weights):
            return forward(layer_rows, weights, mask_rows)
        result, pullback = jax.vjp(apply_layer, layer_inputs, *params)
        gradients = pullback(cotangent)
        totals = tuple((first + second for first, second in zip(totals, gradients[1:])))
        return (totals, (result.astype(jnp.bfloat16), gradients[0].astype(jnp.bfloat16)))
    initial = tuple((jnp.zeros_like(member) for member in params))
    totals, (layer_outs, in_grads) = lax.scan(group_step, initial, (regroup(layer_in.astype(jnp.float32)), regroup(out_grad.astype(jnp.float32)), regroup(key_mask)))
    factor = 1.0 / math.sqrt(SEQS * L)
    return (layer_outs.reshape(SEQS, L, -1), in_grads.reshape(SEQS, L, -1), totals[0] * factor, totals[1] * factor, totals[2] * factor, totals[3] * factor, totals[4] * factor, totals[5] * factor, totals[6] * factor, totals[7] * factor, totals[8] * factor, totals[9] * factor, totals[10] * factor, totals[11] * factor, totals[12] * factor)
```

```python
import functools
import math

import jax
import jax.numpy as jnp
from jax import lax
from jax.experimental import pallas as pl
from jax.experimental.pallas import tpu as pltpu
from jax.sharding import PartitionSpec as P

HEADS = 12
HEAD_DIM = 64
PATCHES = 196
TEXT = 512
F32 = jnp.float32
BF16 = jnp.bfloat16
VMEM_BYTES = 60 * 1024 * 1024


def dot(lhs, rhs, lhs_dim=1, rhs_dim=0):
    return lax.dot_general(
        lhs, rhs, (((lhs_dim,), (rhs_dim,)), ((), ())), preferred_element_type=F32
    )


def normalize(values):
    center = values - jnp.mean(values, axis=-1, keepdims=True)
    spread = jnp.mean(center * center, axis=-1, keepdims=True)
    scale = lax.rsqrt(spread + 1e-06)
    return center * scale, scale


def normalize_back(unit, scale, gain, cotangent):
    inner = cotangent * gain
    mean_inner = jnp.mean(inner, axis=-1, keepdims=True)
    mean_unit = jnp.mean(inner * unit, axis=-1, keepdims=True)
    return scale * (inner - mean_inner - unit * mean_unit)


def column_sum(values):
    return jnp.sum(values, axis=0, keepdims=True)


def call(kernel, grid, in_specs, out_shape, out_specs, scratch=(), flops=0, nbytes=0, trans=0):
    return pl.pallas_call(
        kernel,
        grid_spec=pltpu.PrefetchScalarGridSpec(
            num_scalar_prefetch=1,
            grid=grid,
            in_specs=in_specs,
            out_specs=out_specs,
            scratch_shapes=list(scratch),
        ),
        out_shape=out_shape,
        compiler_params=pltpu.CompilerParams(vmem_limit_bytes=VMEM_BYTES),
        cost_estimate=pl.CostEstimate(flops=flops, bytes_accessed=nbytes, transcendentals=trans),
    )


def fixed(shape):
    zeros = (0,) * len(shape)
    return pl.BlockSpec(shape, lambda *_: zeros)


def shape_of(shape, dtype):
    return jax.ShapeDtypeStruct(shape, dtype)


def place(number, order):
    out = 0
    for bit in order:
        out = out * 2 + ((number >> (bit - 1)) & 1)
    return out


def store_shards(tile_ref, send_ref, keep_ref, info_ref, slot, order, rows, pairs, at):
    core = info_ref[1]
    for pair in range(pairs):
        number = pair if at is None else at * pairs + pair
        index = place(number, order) ^ info_ref[slot]
        sent = tile_ref[pl.ds(pl.multiple_of(rows * (2 * pair + 1 - core), 8), rows), :]
        kept = tile_ref[pl.ds(pl.multiple_of(rows * (2 * pair + core), 8), rows), :]
        send_ref[index] = sent.astype(send_ref.dtype).reshape(send_ref.shape[1:])
        keep_ref[index] = kept.reshape(keep_ref.shape[1:])


def qkv_kernel(info_ref, own_ref, other_ref, gain_ref, shift_ref, w_ref, bias_ref, n1_ref, kv_ref):
    @pl.when(pl.program_id(0) == 0)
    def _():
        rows = jnp.concatenate([own_ref[0], other_ref[...]], axis=0).astype(F32)
        unit, _ = normalize(rows)
        n1_ref[...] = (unit * gain_ref[...] + shift_ref[...]).astype(BF16)

    kv_ref[0] = (dot(n1_ref[...], w_ref[...]) + bias_ref[0]).astype(BF16)


def query_kernel(info_ref, n1_ref, w_ref, bias_ref, q_ref):
    q_ref[...] = ((dot(n1_ref[...], w_ref[...]) + bias_ref[...]) * 0.125).astype(BF16)


def halves(value):
    lane = lax.broadcasted_iota(jnp.int32, value.shape, 1)
    zero = jnp.zeros_like(value)
    return jnp.where(lane < HEAD_DIM, value, zero), jnp.where(lane < HEAD_DIM, zero, value)


def join(first, second):
    lane = lax.broadcasted_iota(jnp.int32, first.shape, 1)
    return jnp.where(lane < HEAD_DIM, first, second)


def attention_kernel(info_ref, q_ref, own_ref, other_ref, mask_ref, ctx_ref, att_ref):
    keys = jnp.concatenate([own_ref[0], other_ref[0]], axis=0)
    values = jnp.concatenate([own_ref[1], other_ref[1]], axis=0)
    parts = []
    for head, query in enumerate(halves(q_ref[...])):
        scores = dot(query, keys, 1, 1) + mask_ref[...]
        exponent = jnp.exp(scores - jnp.max(scores, axis=-1, keepdims=True))
        total = jnp.sum(exponent, axis=-1, keepdims=True)
        att = (exponent * (1.0 / total)).astype(BF16)
        att_ref[head] = att
        parts.append(dot(att, values))
    ctx_ref[...] = join(*parts).astype(BF16)


def attention_back_kernel(
    info_ref, att_ref, q_ref, own_ref, other_ref, gctx_ref, dq_ref, dbq_ref, down_ref, dother_ref
):
    keys = jnp.concatenate([own_ref[0], other_ref[0]], axis=0)
    values = jnp.concatenate([own_ref[1], other_ref[1]], axis=0)
    queries = q_ref[...]
    gctx = gctx_ref[...]
    dq, dk, dv = [], [], []
    for head, grad in enumerate(halves(gctx)):
        att = att_ref[head]
        wide = att.astype(F32)
        datt = dot(grad, values, 1, 1)
        inner = jnp.sum(wide * datt, axis=-1, keepdims=True)
        dscore = (wide * (datt - inner)).astype(BF16)
        dq.append(dot(dscore, keys))
        dk.append(dot(dscore, queries, 0, 0))
        dv.append(dot(att, gctx, 0, 0))
    dquery = join(*dq) * 0.125
    dq_ref[...] = dquery.astype(BF16)
    dbq_ref[...] = column_sum(dquery)
    rows = queries.shape[0]
    for i, grad in enumerate((join(*dk), join(*dv))):
        down_ref[i] = grad[:rows]
        dother_ref[i] = grad[rows:].astype(BF16)


def mlp_kernel(
    orders,
    rows_up,
    rows_down,
    steps,
    info_ref,
    x_ref,
    xo_ref,
    g_ref,
    go_ref,
    ctx_ref,
    wo_ref,
    bo_ref,
    gain_ref,
    shift_ref,
    wu_ref,
    bu_ref,
    wd_ref,
    bd_ref,
    out_ref,
    outo_ref,
    gmid_ref,
    gctx_ref,
    vec_ref,
    su_ref,
    ku_ref,
    sd_ref,
    kd_ref,
    so_ref,
    ko_ref,
    mid_ref,
    n2_ref,
    acc_ref,
    dn_ref,
    tile_ref,
):
    step = pl.program_id(0)
    half = xo_ref.shape[0]
    grad_low = jnp.concatenate([g_ref[0], go_ref[...]], axis=0)

    @pl.when(step == 0)
    def _():
        rows = jnp.concatenate([x_ref[0], xo_ref[...]], axis=0).astype(F32)
        middle = rows + dot(ctx_ref[...], wo_ref[...]) + bo_ref[...]
        mid_ref[...] = middle
        unit, _ = normalize(middle)
        n2_ref[...] = (unit * gain_ref[...] + shift_ref[...]).astype(BF16)
        acc_ref[...] = middle + bd_ref[...]
        dn_ref[...] = jnp.zeros_like(dn_ref)

    normed = n2_ref[...]
    pre = dot(normed, wu_ref[...]) + bu_ref[0]
    phi = 0.5 * (1.0 + lax.erf(pre * math.sqrt(0.5)))
    hidden = (pre * phi).astype(BF16)
    slope = phi + pre * (jnp.exp(-0.5 * pre * pre) * (1.0 / math.sqrt(2 * math.pi)))
    acc_ref[...] += dot(hidden, wd_ref[...])
    grad_pre = dot(grad_low, wd_ref[...], 1, 1) * slope
    vec_ref[pl.ds(4 + step, 1), :] = column_sum(grad_pre)
    gpre_low = grad_pre.astype(BF16)
    dn_ref[...] += dot(gpre_low, wu_ref[...], 1, 1)
    tile_ref[...] = dot(normed, gpre_low, 0, 0)
    n_up = tile_ref.shape[0] // (2 * rows_up)
    store_shards(tile_ref, su_ref, ku_ref, info_ref, 2, orders[0], rows_up, n_up, None)
    tile_ref[...] = dot(hidden, grad_low, 0, 0)
    n_down = tile_ref.shape[0] // (2 * rows_down)
    for at in range(steps):

        @pl.when(step == at)
        def _(at=at):
            store_shards(tile_ref, sd_ref, kd_ref, info_ref, 3, orders[1], rows_down, n_down, at)

    @pl.when(step == steps - 1)
    def _():
        result = acc_ref[...].astype(BF16)
        out_ref[...] = result[:half]
        outo_ref[...] = result[half:]
        unit, scale = normalize(mid_ref[...])
        dn = dn_ref[...]
        grad = grad_low.astype(F32)
        gmid = grad + normalize_back(unit, scale, gain_ref[...], dn)
        gmid_ref[...] = gmid
        vec_ref[0:1, :] = column_sum(gmid)
        vec_ref[1:2, :] = column_sum(dn * unit)
        vec_ref[2:3, :] = column_sum(dn)
        vec_ref[3:4, :] = column_sum(grad)
        low = gmid.astype(BF16)
        gctx_ref[...] = dot(low, wo_ref[...], 1, 1).astype(BF16)
        tile_ref[...] = dot(ctx_ref[...], low, 0, 0)
        store_shards(tile_ref, so_ref, ko_ref, info_ref, 4, orders[2], rows_up, n_up, None)


def query_back_kernel(order, rows, info_ref, n1_ref, dq_ref, w_ref, dn_ref, s_ref, k_ref, tile_ref):
    tile_ref[...] = dot(n1_ref[...], dq_ref[...], 0, 0)
    pairs = tile_ref.shape[0] // (2 * rows)
    store_shards(tile_ref, s_ref, k_ref, info_ref, 2, order, rows, pairs, None)
    dn_ref[...] = dot(dq_ref[...], w_ref[...], 1, 1)


def key_value_back_kernel(
    orders, rows, info_ref, n1_ref, own_ref, other_ref, dkv_ref, dbv_ref, sk_ref, kk_ref, sv_ref, kv_ref, tile_ref
):
    pairs = tile_ref.shape[0] // (2 * rows)
    for i, (s_ref, k_ref, slot) in enumerate(((sk_ref, kk_ref, 2), (sv_ref, kv_ref, 3))):
        grad = own_ref[i] + other_ref[i].astype(F32)
        low = grad.astype(BF16)
        dkv_ref[i] = low
        if i == 1:
            dbv_ref[...] = column_sum(grad)
        tile_ref[...] = dot(n1_ref[...], low, 0, 0)
        store_shards(tile_ref, s_ref, k_ref, info_ref, slot, orders[i], rows, pairs, None)


def input_back_kernel(
    info_ref, x_ref, xo_ref, gain_ref, dkv_ref, w_ref, dnq_ref, gmid_ref, dbq_ref, dbv_ref, own_ref, other_ref, vec_ref
):
    half = xo_ref.shape[0]
    dn = dnq_ref[...]
    for i in range(2):
        width = dn.shape[1]
        dn = dn + dot(dkv_ref[i], w_ref[:, (i + 1) * width : (i + 2) * width], 1, 1)
    rows = jnp.concatenate([x_ref[0], xo_ref[...]], axis=0).astype(F32)
    unit, scale = normalize(rows)
    result = (gmid_ref[...] + normalize_back(unit, scale, gain_ref[...], dn)).astype(BF16)
    own_ref[...] = result[:half]
    other_ref[...] = result[half:]
    vec_ref[0:1, :] = column_sum(dn * unit)
    vec_ref[1:2, :] = column_sum(dn)
    vec_ref[2:3, :] = dbq_ref[...]
    vec_ref[3:4, :] = dbv_ref[...]
    vec_ref[4:8, :] = jnp.zeros_like(vec_ref[4:8, :])


def finish_kernel(factor, info_ref, *refs):
    count = len(refs) // 3
    for i in range(count):
        keep, recv, out = refs[2 * i], refs[2 * i + 1], refs[2 * count + i]
        total = (keep[0] + recv[0].astype(F32)) * factor
        if total.ndim == 3:
            width = total.shape[-1]
            for block in range(total.shape[0]):
                out[:, block * width : (block + 1) * width] = total[block]
        else:
            out[...] = total


def vector_kernel(factor, per, per_up, info_ref, early_ref, late_ref, out_ref, up_ref):
    me = info_ref[5]
    width = early_ref.shape[1]
    both = jnp.concatenate([early_ref[...], late_ref[...]], axis=0) * factor
    turned = pltpu.roll(both, lax.rem(width - me * per, width), 1)
    out_ref[...] = turned[:, : out_ref.shape[1]]
    row = (me * per_up) // width
    up = early_ref[pl.ds(4 + row, 1), :] * factor
    up = jnp.broadcast_to(up, (8, width))
    shift = lax.rem(width - (me * per_up - row * width), width)
    up_ref[...] = pltpu.roll(up, shift, 1)[:, : up_ref.shape[1]]


def on_device(
    layer_in,
    out_grad,
    pre_gain,
    pre_bias,
    qkv_w,
    q_bias,
    v_bias,
    out_w,
    out_b,
    mid_gain,
    mid_bias,
    up_w,
    up_b,
    down_w,
    down_b,
    patch_keep,
    text_len,
):
    seq_here, half, width = layer_in.shape
    dp, seq = lax.axis_size("dp"), lax.axis_size("seq")
    assert seq_here == 2 and seq == 4
    full = half * seq
    rows = 2 * half
    ff = up_w.shape[1]
    steps = ff // width
    devices = dp * seq
    place_seq = lax.axis_index("seq")
    me = lax.axis_index("dp") * seq + place_seq
    mine, core = place_seq // 2, place_seq % 2

    bits = devices.bit_length() - 1
    halving = devices == 1 << bits and width % devices == 0 and (width // devices) % 8 == 0
    if halving:
        shards, at_me, at_core = devices, me, core
        dp_bits = list(range(2, bits))
        order_x = [1] + dp_bits
        order_y = dp_bits[:1] + [1] + dp_bits[1:]
        order_z = dp_bits[1:] + [1] + dp_bits[:1]
    else:
        shards, at_me, at_core = 32, 0, 0
        order_x = order_y = order_z = [4, 3, 2, 1]
    per = width // shards
    per_down = ff // shards
    pairs = shards // 2
    info = jnp.stack(
        [
            jnp.asarray(v, jnp.int32)
            for v in (
                mine,
                at_core,
                place(at_me >> 1, order_x),
                place(at_me >> 1, order_y),
                place(at_me >> 1, order_z),
                me,
            )
        ]
    )

    def swap(value, bit):
        if bit < 2:
            return lax.ppermute(value, "seq", [(i, i ^ (1 << bit)) for i in range(seq)])
        return lax.ppermute(value, "dp", [(i, i ^ (1 << (bit - 2))) for i in range(dp)])

    row = lambda v: v.reshape(-1, width)
    own_rows = pl.BlockSpec((1, half, width), lambda i, info: (info[0], 0, 0))
    vec = fixed((1, width))
    act = fixed((rows, width))

    x_other = swap(lax.dynamic_index_in_dim(layer_in, 1 - mine, 0, False), 1)
    g_other = swap(lax.dynamic_index_in_dim(out_grad, 1 - mine, 0, False), 1)

    patches = lax.dynamic_index_in_dim(patch_keep, mine, 0, False)
    length = lax.dynamic_index_in_dim(text_len, mine, 0, False)
    valid = jnp.concatenate(
        [
            jnp.ones((2,), jnp.int32),
            patches,
            jnp.ones((1,), jnp.int32),
            (jnp.arange(TEXT, dtype=jnp.int32) < length).astype(jnp.int32),
            jnp.zeros((full - 3 - PATCHES - TEXT,), jnp.int32),
        ]
    )
    valid = valid.reshape(seq, half)
    valid = jnp.concatenate(
        [lax.dynamic_index_in_dim(valid, place_seq ^ turn, 0, True) for turn in (0, 2, 1, 3)], axis=1
    )
    mask = jnp.where(valid > 0, 0.0, -1e30).astype(F32)

    square = 2 * rows * width * width
    kv_bias = jnp.concatenate([jnp.zeros((1, 1, width), F32), v_bias.reshape(1, 1, width)], axis=0)
    n1, kv = call(
        qkv_kernel,
        (2,),
        [
            own_rows,
            fixed((half, width)),
            vec,
            vec,
            pl.BlockSpec((width, width), lambda i, _: (0, i + 1)),
            pl.BlockSpec((1, 1, width), lambda i, _: (i, 0, 0)),
        ],
        [shape_of((rows, width), BF16), shape_of((2, rows, width), BF16)],
        [act, pl.BlockSpec((1, rows, width), lambda i, _: (i, 0, 0))],
        flops=2 * square,
        nbytes=5 * 10**6,
    )(info, layer_in, x_other, row(pre_gain), row(pre_bias), qkv_w, kv_bias)
    kv_other = swap(kv, 0)
    q = call(
        query_kernel,
        (1,),
        [act, pl.BlockSpec((width, width), lambda i, _: (0, 0)), vec],
        shape_of((rows, width), BF16),
        act,
        flops=square,
        nbytes=3 * 10**6,
    )(info, n1, qkv_w, row(q_bias))

    pair_width = 2 * HEAD_DIM
    blocks = width // pair_width
    col = pl.BlockSpec((rows, pair_width), lambda i, _: (0, i))
    col2 = pl.BlockSpec((2, rows, pair_width), lambda i, _: (0, 0, i))
    att_spec = pl.BlockSpec((2, rows, full), lambda i, _: (i, 0, 0))
    head_flops = 2 * rows * full * pair_width * HEADS
    ctx, att = call(
        attention_kernel,
        (blocks,),
        [col, col2, col2, fixed((1, full))],
        [shape_of((rows, width), BF16), shape_of((HEADS, rows, full), BF16)],
        [col, att_spec],
        flops=4 * head_flops,
        nbytes=12 * 10**6,
        trans=HEADS * rows * full,
    )(info, q, kv, kv_other, mask)

    orders = (order_x, order_y, order_z)
    mlp_out = call(
        functools.partial(mlp_kernel, orders, per, per_down, steps),
        (steps,),
        [
            own_rows,
            fixed((half, width)),
            own_rows,
            fixed((half, width)),
            act,
            fixed((width, width)),
            vec,
            vec,
            vec,
            pl.BlockSpec((width, width), lambda i, _: (0, i)),
            pl.BlockSpec((1, 1, width), lambda i, _: (i, 0, 0)),
            pl.BlockSpec((width, width), lambda i, _: (i, 0)),
            vec,
        ],
        [
            shape_of((half, width), BF16),
            shape_of((half, width), BF16),
            shape_of((rows, width), F32),
            shape_of((rows, width), BF16),
            shape_of((4 + steps, width), F32),
            shape_of((pairs, steps, per, width), BF16),
            shape_of((pairs, steps, per, width), F32),
            shape_of((pairs, per_down, width), BF16),
            shape_of((pairs, per_down, width), F32),
            shape_of((pairs, per, width), BF16),
            shape_of((pairs, per, width), F32),
        ],
        [
            fixed((half, width)),
            fixed((half, width)),
            act,
            act,
            fixed((4 + steps, width)),
            pl.BlockSpec((pairs, 1, per, width), lambda i, _: (0, i, 0, 0)),
            pl.BlockSpec((pairs, 1, per, width), lambda i, _: (0, i, 0, 0)),
            fixed((pairs, per_down, width)),
            fixed((pairs, per_down, width)),
            fixed((pairs, per, width)),
            fixed((pairs, per, width)),
        ],
        scratch=[
            pltpu.VMEM((rows, width), F32),
            pltpu.VMEM((rows, width), BF16),
            pltpu.VMEM((rows, width), F32),
            pltpu.VMEM((rows, width), F32),
            pltpu.VMEM((width, width), F32),
        ],
        flops=(6 * steps + 3) * square,
        nbytes=40 * 10**6,
        trans=2 * rows * ff,
    )(
        info,
        layer_in,
        x_other,
        out_grad,
        g_other,
        ctx,
        out_w,
        row(out_b),
        row(mid_gain),
        row(mid_bias),
        up_w,
        up_b.reshape(steps, 1, width),
        down_w,
        row(down_b),
    )
    out_own, out_other, gmid, gctx, early, s_up, k_up, s_down, k_down, s_out, k_out = mlp_out
    out_back = swap(out_other, 1)

    def reduce(sent, kept, order):
        got = swap(sent, 0)
        for bit in order:
            total = kept + got.astype(F32)
            cut = total.shape[0] // 2
            kept = total[:cut]
            got = swap(total[cut:].astype(BF16), bit)
        return kept, got

    def natural(sent, kept):
        return jnp.stack([kept, sent.astype(F32)], axis=1)

    if halving:
        up_pair = reduce(s_up, k_up, order_x)
        down_pair = reduce(s_down, k_down, order_y)
        out_pair = reduce(s_out, k_out, order_z)

    dq, dbq, dkv_own, dkv_send = call(
        attention_back_kernel,
        (blocks,),
        [att_spec, col, col2, col2, col],
        [
            shape_of((rows, width), BF16),
            shape_of((1, width), F32),
            shape_of((2, rows, width), F32),
            shape_of((2, rows, width), BF16),
        ],
        [col, pl.BlockSpec((1, pair_width), lambda i, _: (0, i)), col2, col2],
        flops=8 * head_flops,
        nbytes=16 * 10**6,
    )(info, att, q, kv, kv_other, gctx)
    dkv_other = swap(dkv_send, 0)
    shard = fixed((pairs, per, width))
    tile = pltpu.VMEM((width, width), F32)
    dn_q, s_q, k_q = call(
        functools.partial(query_back_kernel, order_x, per),
        (1,),
        [act, act, pl.BlockSpec((width, width), lambda i, _: (0, 0))],
        [shape_of((rows, width), F32), shape_of((pairs, per, width), BF16), shape_of((pairs, per, width), F32)],
        [act, shard, shard],
        scratch=[tile],
        flops=2 * square,
        nbytes=6 * 10**6,
    )(info, n1, dq, qkv_w)
    dkv, dbv, s_k, k_k, s_v, k_v = call(
        functools.partial(key_value_back_kernel, (order_x, order_y), per),
        (1,),
        [act, fixed((2, rows, width)), fixed((2, rows, width))],
        [
            shape_of((2, rows, width), BF16),
            shape_of((1, width), F32),
            shape_of((pairs, per, width), BF16),
            shape_of((pairs, per, width), F32),
            shape_of((pairs, per, width), BF16),
            shape_of((pairs, per, width), F32),
        ],
        [fixed((2, rows, width)), vec, shard, shard, shard, shard],
        scratch=[tile],
        flops=2 * square,
        nbytes=10 * 10**6,
    )(info, n1, dkv_own, dkv_other)
    if halving:
        q_pair = reduce(s_q, k_q, order_x)
        k_pair = reduce(s_k, k_k, order_x)
        v_pair = reduce(s_v, k_v, order_y)
    in_own, in_other, late = call(
        input_back_kernel,
        (1,),
        [
            own_rows,
            fixed((half, width)),
            vec,
            fixed((2, rows, width)),
            fixed((width, 3 * width)),
            act,
            act,
            vec,
            vec,
        ],
        [shape_of((half, width), BF16), shape_of((half, width), BF16), shape_of((8, width), F32)],
        [fixed((half, width)), fixed((half, width)), fixed((8, width))],
        flops=2 * square,
        nbytes=10 * 10**6,
    )(info, layer_in, x_other, row(pre_gain), dkv, qkv_w, dn_q, gmid, dbq, dbv)
    in_back = swap(in_other, 1)

    def give_back(own, other):
        first = jnp.where(mine == 0, own, other)
        second = jnp.where(mine == 0, other, own)
        return jnp.stack([first, second])

    layer_out = give_back(out_own, out_back)
    in_grad = give_back(in_own, in_back)

    factor = 1.0 / math.sqrt(seq_here * full * dp)
    vectors = jnp.concatenate([early, late], axis=0)
    if halving:
        for bit in range(bits):
            vectors = vectors + swap(vectors, bit)
    else:
        vectors = lax.psum(vectors, ("dp", "seq"))
    per_vec, per_up = width // devices, ff // devices
    early_rows = 4 + steps
    small, up_bias = call(
        functools.partial(vector_kernel, factor, per_vec, per_up),
        (1,),
        [
            pl.BlockSpec((early_rows, width), lambda i, _: (0, 0)),
            pl.BlockSpec((8, width), lambda i, _: (early_rows // 8, 0)),
        ],
        [shape_of((early_rows + 8, 128), F32), shape_of((8, 128), F32)],
        [fixed((early_rows + 8, 128)), fixed((8, 128))],
    )(info, vectors, vectors)
    pick = lambda i: small[i, :per_vec]
    d_upbias = up_bias[0, :per_up]
    d_outbias, d_midgain, d_midbias, d_downbias = (pick(i) for i in range(4))
    d_pregain, d_prebias, d_qbias, d_vbias = (pick(early_rows + i) for i in range(4))

    if halving:

        def finish(named):
            operands = [v for pair, _ in named for v in pair]
            shapes = [s for _, s in named]
            return call(
                functools.partial(finish_kernel, factor),
                (1,),
                [fixed(v.shape) for v in operands],
                [shape_of(s, F32) for s in shapes],
                [fixed(s) for s in shapes],
            )(info, *operands)

        d_wup, d_wdown, d_wout = finish(
            [(up_pair, (per, ff)), (down_pair, (per_down, width)), (out_pair, (per, width))]
        )
        d_q, d_k, d_v = finish([(pair, (per, width)) for pair in (q_pair, k_pair, v_pair)])
        d_qkv = jnp.concatenate([d_q, d_k, d_v], axis=1)
    else:

        def scatter(value):
            return lax.psum_scatter(value, ("dp", "seq"), scatter_dimension=0, tiled=True) * factor

        d_wup = scatter(
            natural(s_up, k_up).transpose(0, 1, 3, 2, 4).reshape(width, ff)
        )
        d_wdown = scatter(natural(s_down, k_down).reshape(ff, width))
        d_wout = scatter(natural(s_out, k_out).reshape(width, width))
        d_qkv = scatter(
            jnp.concatenate(
                [natural(s, k).reshape(width, width) for s, k in ((s_q, k_q), (s_k, k_k), (s_v, k_v))],
                axis=1,
            )
        )
    return (
        layer_out,
        in_grad,
        d_pregain,
        d_prebias,
        d_qkv,
        d_qbias,
        d_vbias,
        d_wout,
        d_outbias,
        d_midgain,
        d_midbias,
        d_wup,
        d_upbias,
        d_wdown,
        d_downbias,
    )


def solution(mesh):
    both = ("dp", "seq")
    rows = P("dp", "seq", None)
    return jax.shard_map(
        on_device,
        mesh=mesh,
        in_specs=(rows, rows) + (P(),) * 13 + (P("dp", None), P("dp")),
        out_specs=(
            rows,
            rows,
            P(both),
            P(both),
            P(both, None),
            P(both),
            P(both),
            P(both, None),
            P(both),
            P(both),
            P(both),
            P(both, None),
            P(both),
            P(both, None),
            P(both),
        ),
        check_vma=False,
    )
```

```python
import functools
import math

import jax
import jax.numpy as jnp
from jax import lax
from jax.experimental import pallas as pl
from jax.experimental.pallas import tpu as pltpu
from jax.sharding import PartitionSpec as P

HEADS = 12
HEAD_DIM = 64
PATCHES = 196
TEXT = 512
F32 = jnp.float32
BF16 = jnp.bfloat16
VMEM_BYTES = 60 * 1024 * 1024


def dot(lhs, rhs, lhs_dim=1, rhs_dim=0):
    return lax.dot_general(
        lhs, rhs, (((lhs_dim,), (rhs_dim,)), ((), ())), preferred_element_type=F32
    )


def normalize(values):
    center = values - jnp.mean(values, axis=-1, keepdims=True)
    spread = jnp.mean(center * center, axis=-1, keepdims=True)
    scale = lax.rsqrt(spread + 1e-06)
    return center * scale, scale


def normalize_back(unit, scale, gain, cotangent):
    inner = cotangent * gain
    mean_inner = jnp.mean(inner, axis=-1, keepdims=True)
    mean_unit = jnp.mean(inner * unit, axis=-1, keepdims=True)
    return scale * (inner - mean_inner - unit * mean_unit)


def column_sum(values):
    return jnp.sum(values, axis=0, keepdims=True)


def call(kernel, grid, in_specs, out_shape, out_specs, scratch=(), flops=0, nbytes=0, trans=0):
    return pl.pallas_call(
        kernel,
        grid_spec=pltpu.PrefetchScalarGridSpec(
            num_scalar_prefetch=1,
            grid=grid,
            in_specs=in_specs,
            out_specs=out_specs,
            scratch_shapes=list(scratch),
        ),
        out_shape=out_shape,
        compiler_params=pltpu.CompilerParams(vmem_limit_bytes=VMEM_BYTES),
        cost_estimate=pl.CostEstimate(flops=flops, bytes_accessed=nbytes, transcendentals=trans),
    )


def fixed(shape):
    zeros = (0,) * len(shape)
    return pl.BlockSpec(shape, lambda *_: zeros)


def shape_of(shape, dtype):
    return jax.ShapeDtypeStruct(shape, dtype)


def place(number, order):
    out = 0
    for bit in order:
        out = out * 2 + ((number >> (bit - 1)) & 1)
    return out


def store_shards(tile_ref, send_ref, keep_ref, info_ref, slot, order, rows, pairs, at):
    core = info_ref[1]
    for pair in range(pairs):
        number = pair if at is None else at * pairs + pair
        index = place(number, order) ^ info_ref[slot]
        sent = tile_ref[pl.ds(pl.multiple_of(rows * (2 * pair + 1 - core), 8), rows), :]
        kept = tile_ref[pl.ds(pl.multiple_of(rows * (2 * pair + core), 8), rows), :]
        send_ref[index] = sent.astype(send_ref.dtype).reshape(send_ref.shape[1:])
        keep_ref[index] = kept.reshape(keep_ref.shape[1:])


def qkv_kernel(info_ref, own_ref, other_ref, gain_ref, shift_ref, w_ref, bias_ref, n1_ref, kv_ref):
    @pl.when(pl.program_id(0) == 0)
    def _():
        rows = jnp.concatenate([own_ref[0], other_ref[...]], axis=0).astype(F32)
        unit, _ = normalize(rows)
        n1_ref[...] = (unit * gain_ref[...] + shift_ref[...]).astype(BF16)

    kv_ref[0] = (dot(n1_ref[...], w_ref[...]) + bias_ref[0]).astype(BF16)


def query_kernel(info_ref, n1_ref, w_ref, bias_ref, q_ref):
    q_ref[...] = ((dot(n1_ref[...], w_ref[...]) + bias_ref[...]) * 0.125).astype(BF16)


def halves(value):
    lane = lax.broadcasted_iota(jnp.int32, value.shape, 1)
    zero = jnp.zeros_like(value)
    return jnp.where(lane < HEAD_DIM, value, zero), jnp.where(lane < HEAD_DIM, zero, value)


def join(first, second):
    lane = lax.broadcasted_iota(jnp.int32, first.shape, 1)
    return jnp.where(lane < HEAD_DIM, first, second)


def attention_kernel(info_ref, q_ref, own_ref, other_ref, mask_ref, ctx_ref, att_ref):
    keys = jnp.concatenate([own_ref[0], other_ref[0]], axis=0)
    values = jnp.concatenate([own_ref[1], other_ref[1]], axis=0)
    parts = []
    for head, query in enumerate(halves(q_ref[...])):
        scores = dot(query, keys, 1, 1) + mask_ref[...]
        exponent = jnp.exp(scores - jnp.max(scores, axis=-1, keepdims=True))
        total = jnp.sum(exponent, axis=-1, keepdims=True)
        att = (exponent * (1.0 / total)).astype(BF16)
        att_ref[head] = att
        parts.append(dot(att, values))
    ctx_ref[...] = join(*parts).astype(BF16)


def attention_back_kernel(
    info_ref, att_ref, q_ref, own_ref, other_ref, gctx_ref, dq_ref, dbq_ref, down_ref, dother_ref
):
    keys = jnp.concatenate([own_ref[0], other_ref[0]], axis=0)
    values = jnp.concatenate([own_ref[1], other_ref[1]], axis=0)
    queries = q_ref[...]
    gctx = gctx_ref[...]
    dq, dk, dv = [], [], []
    for head, grad in enumerate(halves(gctx)):
        att = att_ref[head]
        wide = att.astype(F32)
        datt = dot(grad, values, 1, 1)
        inner = jnp.sum(wide * datt, axis=-1, keepdims=True)
        dscore = (wide * (datt - inner)).astype(BF16)
        dq.append(dot(dscore, keys))
        dk.append(dot(dscore, queries, 0, 0))
        dv.append(dot(att, gctx, 0, 0))
    dquery = join(*dq) * 0.125
    dq_ref[...] = dquery.astype(BF16)
    dbq_ref[...] = column_sum(dquery)
    rows = queries.shape[0]
    for i, grad in enumerate((join(*dk), join(*dv))):
        down_ref[i] = grad[:rows]
        dother_ref[i] = grad[rows:].astype(BF16)


def mlp_kernel(
    orders,
    rows_up,
    rows_down,
    steps,
    info_ref,
    x_ref,
    xo_ref,
    g_ref,
    go_ref,
    ctx_ref,
    wo_ref,
    bo_ref,
    gain_ref,
    shift_ref,
    wu_ref,
    bu_ref,
    wd_ref,
    bd_ref,
    out_ref,
    outo_ref,
    gmid_ref,
    gctx_ref,
    vec_ref,
    su_ref,
    ku_ref,
    sd_ref,
    kd_ref,
    so_ref,
    ko_ref,
    mid_ref,
    n2_ref,
    acc_ref,
    dn_ref,
    tile_ref,
):
    step = pl.program_id(0)
    half = xo_ref.shape[0]
    grad_low = jnp.concatenate([g_ref[0], go_ref[...]], axis=0)

    @pl.when(step == 0)
    def _():
        rows = jnp.concatenate([x_ref[0], xo_ref[...]], axis=0).astype(F32)
        middle = rows + dot(ctx_ref[...], wo_ref[...]) + bo_ref[...]
        mid_ref[...] = middle
        unit, _ = normalize(middle)
        n2_ref[...] = (unit * gain_ref[...] + shift_ref[...]).astype(BF16)
        acc_ref[...] = middle + bd_ref[...]
        dn_ref[...] = jnp.zeros_like(dn_ref)

    normed = n2_ref[...]
    pre = dot(normed, wu_ref[...]) + bu_ref[0]
    phi = 0.5 * (1.0 + lax.erf(pre * math.sqrt(0.5)))
    hidden = (pre * phi).astype(BF16)
    slope = phi + pre * (jnp.exp(-0.5 * pre * pre) * (1.0 / math.sqrt(2 * math.pi)))
    acc_ref[...] += dot(hidden, wd_ref[...])
    grad_pre = dot(grad_low, wd_ref[...], 1, 1) * slope
    vec_ref[pl.ds(4 + step, 1), :] = column_sum(grad_pre)
    gpre_low = grad_pre.astype(BF16)
    dn_ref[...] += dot(gpre_low, wu_ref[...], 1, 1)
    tile_ref[...] = dot(normed, gpre_low, 0, 0)
    n_up = tile_ref.shape[0] // (2 * rows_up)
    store_shards(tile_ref, su_ref, ku_ref, info_ref, 2, orders[0], rows_up, n_up, None)
    tile_ref[...] = dot(hidden, grad_low, 0, 0)
    n_down = tile_ref.shape[0] // (2 * rows_down)
    for at in range(steps):

        @pl.when(step == at)
        def _(at=at):
            store_shards(tile_ref, sd_ref, kd_ref, info_ref, 3, orders[1], rows_down, n_down, at)

    @pl.when(step == steps - 1)
    def _():
        result = acc_ref[...].astype(BF16)
        out_ref[...] = result[:half]
        outo_ref[...] = result[half:]
        unit, scale = normalize(mid_ref[...])
        dn = dn_ref[...]
        grad = grad_low.astype(F32)
        gmid = grad + normalize_back(unit, scale, gain_ref[...], dn)
        gmid_ref[...] = gmid
        vec_ref[0:1, :] = column_sum(gmid)
        vec_ref[1:2, :] = column_sum(dn * unit)
        vec_ref[2:3, :] = column_sum(dn)
        vec_ref[3:4, :] = column_sum(grad)
        low = gmid.astype(BF16)
        gctx_ref[...] = dot(low, wo_ref[...], 1, 1).astype(BF16)
        tile_ref[...] = dot(ctx_ref[...], low, 0, 0)
        store_shards(tile_ref, so_ref, ko_ref, info_ref, 4, orders[2], rows_up, n_up, None)


def query_back_kernel(order, rows, info_ref, n1_ref, dq_ref, w_ref, dn_ref, s_ref, k_ref, tile_ref):
    tile_ref[...] = dot(n1_ref[...], dq_ref[...], 0, 0)
    pairs = tile_ref.shape[0] // (2 * rows)
    store_shards(tile_ref, s_ref, k_ref, info_ref, 2, order, rows, pairs, None)
    dn_ref[...] = dot(dq_ref[...], w_ref[...], 1, 1)


def key_value_back_kernel(
    orders, rows, info_ref, n1_ref, own_ref, other_ref, dkv_ref, dbv_ref, sk_ref, kk_ref, sv_ref, kv_ref, tile_ref
):
    pairs = tile_ref.shape[0] // (2 * rows)
    for i, (s_ref, k_ref, slot) in enumerate(((sk_ref, kk_ref, 2), (sv_ref, kv_ref, 3))):
        grad = own_ref[i] + other_ref[i].astype(F32)
        low = grad.astype(BF16)
        dkv_ref[i] = low
        if i == 1:
            dbv_ref[...] = column_sum(grad)
        tile_ref[...] = dot(n1_ref[...], low, 0, 0)
        store_shards(tile_ref, s_ref, k_ref, info_ref, slot, orders[i], rows, pairs, None)


def input_back_kernel(
    info_ref, x_ref, xo_ref, gain_ref, dkv_ref, w_ref, dnq_ref, gmid_ref, dbq_ref, dbv_ref, own_ref, other_ref, vec_ref
):
    half = xo_ref.shape[0]
    dn = dnq_ref[...]
    for i in range(2):
        width = dn.shape[1]
        dn = dn + dot(dkv_ref[i], w_ref[:, (i + 1) * width : (i + 2) * width], 1, 1)
    rows = jnp.concatenate([x_ref[0], xo_ref[...]], axis=0).astype(F32)
    unit, scale = normalize(rows)
    result = (gmid_ref[...] + normalize_back(unit, scale, gain_ref[...], dn)).astype(BF16)
    own_ref[...] = result[:half]
    other_ref[...] = result[half:]
    vec_ref[0:1, :] = column_sum(dn * unit)
    vec_ref[1:2, :] = column_sum(dn)
    vec_ref[2:3, :] = dbq_ref[...]
    vec_ref[3:4, :] = dbv_ref[...]
    vec_ref[4:8, :] = jnp.zeros_like(vec_ref[4:8, :])


def finish_kernel(factor, info_ref, *refs):
    count = len(refs) // 3
    for i in range(count):
        keep, recv, out = refs[2 * i], refs[2 * i + 1], refs[2 * count + i]
        total = (keep[0] + recv[0].astype(F32)) * factor
        if total.ndim == 3:
            width = total.shape[-1]
            for block in range(total.shape[0]):
                out[:, block * width : (block + 1) * width] = total[block]
        else:
            out[...] = total


def vector_kernel(factor, per, per_up, info_ref, early_ref, late_ref, out_ref, up_ref):
    me = info_ref[5]
    width = early_ref.shape[1]
    both = jnp.concatenate([early_ref[...], late_ref[...]], axis=0) * factor
    turned = pltpu.roll(both, lax.rem(width - me * per, width), 1)
    out_ref[...] = turned[:, : out_ref.shape[1]]
    row = (me * per_up) // width
    up = early_ref[pl.ds(4 + row, 1), :] * factor
    up = jnp.broadcast_to(up, (8, width))
    shift = lax.rem(width - (me * per_up - row * width), width)
    up_ref[...] = pltpu.roll(up, shift, 1)[:, : up_ref.shape[1]]


UNIT_STAGES = 5
STAGE_AT = (0, 0, 8, 12, 14)


def spots(order, number, device_bits):
    out = 0
    for bit in order:
        value = (number // (1 << bit)) % 2
        mine = device_bits[bit]
        out = out * 2 + (value + mine - 2 * value * mine)
    return out


def back_kernel(
    factor,
    plan,
    layer_in_ref,
    x_other_ref,
    out_grad_ref,
    g_other_ref,
    ctx_in_ref,
    n1_in_ref,
    q_in_ref,
    kv_in_ref,
    kvo_in_ref,
    att_in_ref,
    qkv_w_ref,
    out_w_ref,
    up_w_ref,
    down_w_ref,
    par_ref,
    layer_out_ref,
    in_grad_ref,
    dup_ref,
    ddown_ref,
    dout_ref,
    dqkv_ref,
    small_ref,
    upb_ref,
    x_ref,
    g_ref,
    ctx_ref,
    n1_ref,
    q_ref,
    kv_ref,
    kvo_ref,
    att_ref,
    wo_ref,
    w_ref,
    mid_ref,
    acc_ref,
    dn_ref,
    n2_ref,
    tile_ref,
    gctx_ref,
    dq_ref,
    down_ref,
    dsend_ref,
    drecv_ref,
    res_ref,
    vec_ref,
    vrecv_ref,
    s_ref,
    k_ref,
    r0_ref,
    r_ref,
    in_sem,
    w_sem,
    att_sem,
    send_sem,
    recv_sem,
    dk_send_sem,
    dk_recv_sem,
    v_send_sem,
    v_recv_sem,
    io_sem,
    io_send_sem,
    io_recv_sem,
):
    half, width = x_other_ref.shape
    rows = 2 * half
    steps = up_w_ref.shape[1] // width
    orders, after_pair, after_third, tail = plan
    dp, seq = lax.axis_index("dp"), lax.axis_index("seq")
    core, mine = seq % 2, seq // 2
    y, z0, z1 = dp % 2, (dp // 2) % 2, (dp // 4) % 2
    bits = (mine, y, z0, z1)
    partner_core = {"seq": seq + 1 - 2 * core}
    partner_x = {"seq": seq + 2 - 4 * mine}
    partners = (partner_x, {"dp": dp + 1 - 2 * y}, {"dp": dp + 2 - 4 * z0}, {"dp": dp + 4 - 8 * z1})
    mesh_ids = pl.DeviceIdType.MESH

    barrier = pltpu.get_barrier_semaphore()
    for other in (partner_core,) + partners:
        pl.semaphore_signal(barrier, inc=1, device_id=other, device_id_type=mesh_ids)

    loads = [
        (x_other_ref, x_ref.at[pl.ds(half, half)]),
        (layer_in_ref.at[mine], x_ref.at[pl.ds(0, half)]),
        (ctx_in_ref, ctx_ref),
        (out_w_ref, wo_ref),
        (g_other_ref, g_ref.at[pl.ds(half, half)]),
        (out_grad_ref.at[mine], g_ref.at[pl.ds(0, half)]),
        (q_in_ref, q_ref),
        (kv_in_ref, kv_ref),
        (kvo_in_ref, kvo_ref),
        (n1_in_ref, n1_ref),
    ]

    def load(i):
        return pltpu.make_async_copy(loads[i][0], loads[i][1], in_sem.at[i])

    def weights(j, slot):
        at = pl.multiple_of(j * width, width)
        return (
            pltpu.make_async_copy(up_w_ref.at[:, pl.ds(at, width)], w_ref.at[slot], w_sem.at[slot]),
            pltpu.make_async_copy(down_w_ref.at[pl.ds(at, width), :], w_ref.at[2 + slot], w_sem.at[2 + slot]),
        )

    def proj_weights(i):
        return pltpu.make_async_copy(qkv_w_ref.at[:, i * width : (i + 1) * width], w_ref.at[i], w_sem.at[4 + i])

    def attention_load(p, slot):
        return pltpu.make_async_copy(att_in_ref.at[pl.ds(2 * p, 2)], att_ref.at[slot], att_sem.at[slot])

    for i in range(4):
        load(i).start()
    for copy in weights(0, 0):
        copy.start()
    for i in range(4, len(loads)):
        load(i).start()
    for p in range(2):
        attention_load(p, p).start()

    def transfer(unit, stage, order):
        count = 16 >> stage
        if stage == 0:
            target, landing = partner_core, r0_ref.at[unit]
        else:
            target = partners[order[stage - 1]]
            landing = r_ref.at[unit, pl.ds(STAGE_AT[stage], count)]
        return pltpu.make_async_remote_copy(
            src_ref=s_ref.at[unit, pl.ds(STAGE_AT[stage], count)],
            dst_ref=landing,
            send_sem=send_sem.at[unit, stage],
            recv_sem=recv_sem.at[unit, stage],
            device_id=target,
            device_id_type=mesh_ids,
        )

    def advance(unit, stage, order):
        transfer(unit, stage, order).wait()
        count = 8 >> stage

        def arrived(i):
            if stage == 0:
                return r0_ref[unit, i].astype(F32)
            return r_ref[unit, STAGE_AT[stage] + i].astype(F32)

        @pl.loop(0, count)
        def _(i):
            k_ref[unit, i] = (k_ref[unit, i].astype(F32) + arrived(i)).astype(BF16)
            s_ref[unit, STAGE_AT[stage + 1] + i] = (
                k_ref[unit, count + i].astype(F32) + arrived(count + i)
            ).astype(BF16)

        transfer(unit, stage + 1, order).start()

    def total(unit, order):
        transfer(unit, UNIT_STAGES - 1, order).wait()
        return (k_ref[unit, 0].astype(F32) + r_ref[unit, STAGE_AT[-1]].astype(F32)) * factor

    def place_unit(unit, order, block, pairs, first, at):
        piece = s_ref.shape[2]

        @pl.loop(0, pairs)
        def _(pair):
            index = spots(order, first + pair, bits)
            sent = pl.multiple_of(block * (2 * pair + 1 - core) + at, 8)
            kept = pl.multiple_of(block * (2 * pair + core) + at, 8)
            s_ref[unit, index] = tile_ref[pl.ds(sent, piece), :].astype(BF16)
            k_ref[unit, index] = tile_ref[pl.ds(kept, piece), :].astype(BF16)

    per = s_ref.shape[2]
    up, down, out, qkv = 0, steps, 2 * steps, 2 * steps + 1

    def run(events):
        for unit, stage in events:
            advance(unit, stage, orders[unit])

    for i in range(4):
        load(i).wait()
    middle = x_ref[...].astype(F32) + dot(ctx_ref[...], wo_ref[...]) + par_ref[0:1, :]
    mid_ref[...] = middle
    unit_mid, _ = normalize(middle)
    n2_ref[...] = (unit_mid * par_ref[1:2, :] + par_ref[2:3, :]).astype(BF16)
    acc_ref[...] = middle + par_ref[3:4, :]
    dn_ref[...] = jnp.zeros_like(dn_ref)
    vec_ref[...] = jnp.zeros_like(vec_ref)
    for i in range(4, 6):
        load(i).wait()
    pl.semaphore_wait(barrier, 1 + len(partners))

    @pl.loop(0, steps)
    def _(j):
        slot = j % 2
        for copy in weights(j, slot):
            copy.wait()

        @pl.when(j + 1 < steps)
        def _():
            for copy in weights(j + 1, 1 - slot):
                copy.start()

        normed = n2_ref[...]
        grad_low = g_ref[...]
        wu, wd = w_ref.at[slot], w_ref.at[2 + slot]
        pre = dot(normed, wu[...]) + par_ref[pl.ds(8 + j, 1), :]
        phi = 0.5 * (1.0 + lax.erf(pre * math.sqrt(0.5)))
        hidden = (pre * phi).astype(BF16)
        slope = phi + pre * (jnp.exp(-0.5 * pre * pre) * (1.0 / math.sqrt(2 * math.pi)))
        acc_ref[...] += dot(hidden, wd[...])
        grad_pre = dot(grad_low, wd[...], 1, 1) * slope
        vec_ref[pl.ds(4 + j, 1), :] = column_sum(grad_pre)
        gpre_low = grad_pre.astype(BF16)
        dn_ref[...] += dot(gpre_low, wu[...], 1, 1)

        @pl.when(j >= 1)
        def _():
            advance(up + j - 1, 0, orders[up])

        tile_ref[...] = dot(normed, gpre_low, 0, 0)
        place_unit(up + j, orders[up], per, 16, 0, 0)
        transfer(up + j, 0, orders[up]).start()
        tile_ref[...] = dot(hidden, grad_low, 0, 0)
        for b in range(steps):
            place_unit(down + b, orders[down + b], steps * per, 16 // steps, j * (16 // steps), b * per)

        @pl.when(j >= 2)
        def _():
            advance(up + j - 2, 1, orders[up])

    for b in range(steps):
        transfer(down + b, 0, orders[down + b]).start()
    for i in range(3):
        proj_weights(i).start()
    result = acc_ref[...].astype(BF16)
    res_ref[0] = result

    def give(ref, n):
        mine_copy = pltpu.make_async_copy(res_ref.at[n, pl.ds(0, half)], ref.at[mine], io_sem.at[n])
        other_copy = pltpu.make_async_remote_copy(
            src_ref=res_ref.at[n, pl.ds(half, half)],
            dst_ref=ref.at[mine],
            send_sem=io_send_sem.at[n],
            recv_sem=io_recv_sem.at[n],
            device_id=partner_x,
            device_id_type=mesh_ids,
        )
        return mine_copy, other_copy

    for copy in give(layer_out_ref, 0):
        copy.start()
    unit_mid, scale = normalize(mid_ref[...])
    dn = dn_ref[...]
    grad = g_ref[...].astype(F32)
    gmid = grad + normalize_back(unit_mid, scale, par_ref[1:2, :], dn)
    vec_ref[0:1, :] = column_sum(gmid)
    vec_ref[1:2, :] = column_sum(dn * unit_mid)
    vec_ref[2:3, :] = column_sum(dn)
    vec_ref[3:4, :] = column_sum(grad)
    acc_ref[...] = gmid
    low = gmid.astype(BF16)
    gctx_ref[...] = dot(low, wo_ref[...], 1, 1).astype(BF16)
    tile_ref[...] = dot(ctx_ref[...], low, 0, 0)
    place_unit(out, orders[out], per, 16, 0, 0)
    transfer(out, 0, orders[out]).start()
    dn_ref[...] = jnp.zeros_like(dn_ref)
    for i in range(6, len(loads)):
        load(i).wait()
    run(((up + steps - 1, 0), (up + steps - 2, 1)))

    pair_width = 2 * HEAD_DIM
    third = 2 * pair_width

    def exchange(t):
        return pltpu.make_async_remote_copy(
            src_ref=dsend_ref.at[t],
            dst_ref=drecv_ref.at[t],
            send_sem=dk_send_sem.at[t],
            recv_sem=dk_recv_sem.at[t],
            device_id=partner_core,
            device_id_type=mesh_ids,
        )

    def finish_third(t):
        exchange(t).wait()
        cols = slice(t * third, (t + 1) * third)
        more = jnp.zeros((rows, width), F32)
        for i in range(2):
            grad = down_ref[t % 2, i] + drecv_ref[t, i].astype(F32)
            if i == 1:
                vec_ref[11:12, cols] = column_sum(grad)
            low = grad.astype(BF16)
            tile_ref[:, (i + 1) * third : (i + 2) * third] = dot(n1_ref[...], low, 0, 0)
            more = more + dot(low, w_ref[1 + i, :, cols], 1, 1)
        place_unit(qkv + t, orders[qkv + t], per, 16, 0, 0)
        transfer(qkv + t, 0, orders[qkv + t]).start()
        dn_ref[...] += more

    for t in range(3):

        @pl.loop(0, 2)
        def _(i, t=t):
            p = 2 * t + i
            attention_load(p, i).wait()
            lanes = pl.ds(pl.multiple_of(p * pair_width, pair_width), pair_width)
            here = pl.ds(pl.multiple_of(i * pair_width, pair_width), pair_width)
            keys = jnp.concatenate([kv_ref[0, :, lanes], kvo_ref[0, :, lanes]], axis=0)
            values = jnp.concatenate([kv_ref[1, :, lanes], kvo_ref[1, :, lanes]], axis=0)
            queries = q_ref[:, lanes]
            gctx = gctx_ref[:, lanes]
            dq, dk, dv = [], [], []
            for head, grad in enumerate(halves(gctx)):
                att = att_ref[i, head]
                wide = att.astype(F32)
                datt = dot(grad, values, 1, 1)
                inner = jnp.sum(wide * datt, axis=-1, keepdims=True)
                dscore = (wide * (datt - inner)).astype(BF16)
                dq.append(dot(dscore, keys))
                dk.append(dot(dscore, queries, 0, 0))
                dv.append(dot(att, gctx, 0, 0))
            dquery = join(*dq) * 0.125
            dq_ref[:, here] = dquery.astype(BF16)
            vec_ref[10:11, lanes] = column_sum(dquery)
            for n, grad in enumerate((join(*dk), join(*dv))):
                down_ref[t % 2, n, :, here] = grad[:rows]
                dsend_ref[t, n, :, here] = grad[rows:].astype(BF16)
            if t < 2:
                attention_load(p + 2, i).start()
            for n in range(2):
                if after_pair[2 * t + n]:

                    @pl.when(i == n)
                    def _(n=n):
                        run(after_pair[2 * t + n])

        exchange(t).start()
        if t == 0:
            for i in range(3):
                proj_weights(i).wait()
        else:
            finish_third(t - 1)
        tile_ref[:, 0:third] = dot(n1_ref[...], dq_ref[...], 0, 0)
        dn_ref[...] += dot(dq_ref[...], w_ref[0, :, t * third : (t + 1) * third], 1, 1)
        run(after_third[t])
    finish_third(2)

    unit_in, scale = normalize(x_ref[...].astype(F32))
    dn = dn_ref[...]
    res_ref[1] = (acc_ref[...] + normalize_back(unit_in, scale, par_ref[4:5, :], dn)).astype(BF16)
    for copy in give(in_grad_ref, 1):
        copy.start()
    vec_ref[8:9, :] = column_sum(dn * unit_in)
    vec_ref[9:10, :] = column_sum(dn)

    def vector_copy(stage):
        return pltpu.make_async_remote_copy(
            src_ref=vec_ref,
            dst_ref=vrecv_ref.at[stage],
            send_sem=v_send_sem.at[stage],
            recv_sem=v_recv_sem.at[stage],
            device_id=((partner_core,) + partners)[stage],
            device_id_type=mesh_ids,
        )

    for stage, events in enumerate(tail):
        if stage < UNIT_STAGES:
            vector_copy(stage).start()
        run(events)
        if stage < UNIT_STAGES:
            vector_copy(stage).wait()
            vec_ref[...] += vrecv_ref[stage]

    both = vec_ref[...] * factor
    me = dp * lax.axis_size("seq") + seq
    turned = pltpu.roll(both, (width - me * per) % width, 1)
    small_ref[...] = turned[:, : small_ref.shape[1]]
    per_up = steps * per
    row = (me * per_up) // width
    up_bias = jnp.broadcast_to(vec_ref[pl.ds(4 + row, 1), :] * factor, (8, width))
    shift = (width - (me * per_up - row * width)) % width
    upb_ref[...] = pltpu.roll(up_bias, shift, 1)[:, : upb_ref.shape[1]]

    for j in range(steps):
        dup_ref[:, j * width : (j + 1) * width] = total(up + j, orders[up + j])
    for b in range(steps):
        ddown_ref[b * per : (b + 1) * per, :] = total(down + b, orders[down + b])
    dout_ref[...] = total(out, orders[out])
    for t in range(3):
        value = total(qkv + t, orders[qkv + t])
        for n in range(3):
            at = n * width + t * third
            dqkv_ref[:, at : at + third] = value[:, n * third : (n + 1) * third]
    for n, ref in enumerate((layer_out_ref, in_grad_ref)):
        for copy in give(ref, n):
            copy.wait()


X, Y, ZX, ZY = (0, 1, 2, 3), (1, 0, 2, 3), (2, 0, 1, 3), (2, 1, 0, 3)
PLAN = (
    (X, X, X, X, X, ZY, ZY, X, X, Y, ZY, Y),
    (
        ((4, 0), (5, 0), (6, 0), (7, 0), (8, 0), (0, 2), (1, 2), (2, 2)),
        ((3, 1),),
        ((5, 1), (4, 1)),
        ((3, 2),),
        ((9, 0), (4, 2), (1, 3), (2, 3), (3, 3)),
        ((8, 1), (6, 2), (5, 3), (4, 3)),
    ),
    ((), ((6, 1), (7, 1), (5, 2), (0, 3)), ((7, 2), (6, 3))),
    (
        ((10, 0), (9, 1), (7, 3), (8, 2), (11, 0)),
        (),
        ((9, 2),),
        ((10, 1),),
        ((11, 1), (8, 3)),
        ((9, 3), (10, 2), (11, 2), (10, 3), (11, 3)),
    ),
)


def on_device(
    layer_in,
    out_grad,
    pre_gain,
    pre_bias,
    qkv_w,
    q_bias,
    v_bias,
    out_w,
    out_b,
    mid_gain,
    mid_bias,
    up_w,
    up_b,
    down_w,
    down_b,
    patch_keep,
    text_len,
):
    seq_here, half, width = layer_in.shape
    dp, seq = lax.axis_size("dp"), lax.axis_size("seq")
    assert seq_here == 2 and seq == 4
    full = half * seq
    rows = 2 * half
    ff = up_w.shape[1]
    steps = ff // width
    devices = dp * seq
    place_seq = lax.axis_index("seq")
    me = lax.axis_index("dp") * seq + place_seq
    mine, core = place_seq // 2, place_seq % 2

    bits = devices.bit_length() - 1
    halving = devices == 1 << bits and width % devices == 0 and (width // devices) % 8 == 0
    if halving:
        shards, at_me, at_core = devices, me, core
        dp_bits = list(range(2, bits))
        order_x = [1] + dp_bits
        order_y = dp_bits[:1] + [1] + dp_bits[1:]
        order_z = dp_bits[1:] + [1] + dp_bits[:1]
    else:
        shards, at_me, at_core = 32, 0, 0
        order_x = order_y = order_z = [4, 3, 2, 1]
    per = width // shards
    per_down = ff // shards
    pairs = shards // 2
    info = jnp.stack(
        [
            jnp.asarray(v, jnp.int32)
            for v in (
                mine,
                at_core,
                place(at_me >> 1, order_x),
                place(at_me >> 1, order_y),
                place(at_me >> 1, order_z),
                me,
            )
        ]
    )

    def swap(value, bit):
        if bit < 2:
            return lax.ppermute(value, "seq", [(i, i ^ (1 << bit)) for i in range(seq)])
        return lax.ppermute(value, "dp", [(i, i ^ (1 << (bit - 2))) for i in range(dp)])

    row = lambda v: v.reshape(-1, width)
    own_rows = pl.BlockSpec((1, half, width), lambda i, info: (info[0], 0, 0))
    vec = fixed((1, width))
    act = fixed((rows, width))

    x_other = swap(lax.dynamic_index_in_dim(layer_in, 1 - mine, 0, False), 1)
    g_other = swap(lax.dynamic_index_in_dim(out_grad, 1 - mine, 0, False), 1)

    patches = lax.dynamic_index_in_dim(patch_keep, mine, 0, False)
    length = lax.dynamic_index_in_dim(text_len, mine, 0, False)
    valid = jnp.concatenate(
        [
            jnp.ones((2,), jnp.int32),
            patches,
            jnp.ones((1,), jnp.int32),
            (jnp.arange(TEXT, dtype=jnp.int32) < length).astype(jnp.int32),
            jnp.zeros((full - 3 - PATCHES - TEXT,), jnp.int32),
        ]
    )
    valid = valid.reshape(seq, half)
    valid = jnp.concatenate(
        [lax.dynamic_index_in_dim(valid, place_seq ^ turn, 0, True) for turn in (0, 2, 1, 3)], axis=1
    )
    mask = jnp.where(valid > 0, 0.0, -1e30).astype(F32)

    square = 2 * rows * width * width
    kv_bias = jnp.concatenate([jnp.zeros((1, 1, width), F32), v_bias.reshape(1, 1, width)], axis=0)
    n1, kv = call(
        qkv_kernel,
        (2,),
        [
            own_rows,
            fixed((half, width)),
            vec,
            vec,
            pl.BlockSpec((width, width), lambda i, _: (0, i + 1)),
            pl.BlockSpec((1, 1, width), lambda i, _: (i, 0, 0)),
        ],
        [shape_of((rows, width), BF16), shape_of((2, rows, width), BF16)],
        [act, pl.BlockSpec((1, rows, width), lambda i, _: (i, 0, 0))],
        flops=2 * square,
        nbytes=5 * 10**6,
    )(info, layer_in, x_other, row(pre_gain), row(pre_bias), qkv_w, kv_bias)
    kv_other = swap(kv, 0)
    q = call(
        query_kernel,
        (1,),
        [act, pl.BlockSpec((width, width), lambda i, _: (0, 0)), vec],
        shape_of((rows, width), BF16),
        act,
        flops=square,
        nbytes=3 * 10**6,
    )(info, n1, qkv_w, row(q_bias))

    pair_width = 2 * HEAD_DIM
    blocks = width // pair_width
    col = pl.BlockSpec((rows, pair_width), lambda i, _: (0, i))
    col2 = pl.BlockSpec((2, rows, pair_width), lambda i, _: (0, 0, i))
    att_spec = pl.BlockSpec((2, rows, full), lambda i, _: (i, 0, 0))
    head_flops = 2 * rows * full * pair_width * HEADS
    ctx, att = call(
        attention_kernel,
        (blocks,),
        [col, col2, col2, fixed((1, full))],
        [shape_of((rows, width), BF16), shape_of((HEADS, rows, full), BF16)],
        [col, att_spec],
        flops=4 * head_flops,
        nbytes=12 * 10**6,
        trans=HEADS * rows * full,
    )(info, q, kv, kv_other, mask)

    factor = 1.0 / math.sqrt(seq_here * full * dp)
    per_vec, per_up = width // devices, ff // devices
    if halving:
        params = jnp.concatenate(
            [row(v) for v in (out_b, mid_gain, mid_bias, down_b, pre_gain, pre_gain, pre_gain, pre_gain, up_b)], axis=0
        )
        hbm = pl.BlockSpec(memory_space=pl.ANY)
        units = 2 * steps + 4
        third = 4 * HEAD_DIM
        big = lambda *shape: pltpu.VMEM(shape, F32)
        low = lambda *shape: pltpu.VMEM(shape, BF16)
        dma = lambda *shape: pltpu.SemaphoreType.DMA(shape)
        operands = (layer_in, x_other, out_grad, g_other, ctx, n1, q, kv, kv_other, att, qkv_w, out_w, up_w, down_w)
        results = [(per, ff), (per_down, width), (per, width), (per, 3 * width), (16, 128), (8, 128)]
        layer_out, in_grad, d_wup, d_wdown, d_wout, d_qkv, small, up_bias = pl.pallas_call(
            functools.partial(back_kernel, factor, PLAN),
            in_specs=[hbm] * len(operands) + [fixed(params.shape)],
            out_shape=[shape_of(layer_in.shape, BF16)] * 2 + [shape_of(s, F32) for s in results],
            out_specs=[hbm] * 2 + [fixed(s) for s in results],
            scratch_shapes=[
                low(rows, width),
                low(rows, width),
                low(rows, width),
                low(rows, width),
                low(rows, width),
                low(2, rows, width),
                low(2, rows, width),
                low(2, 2, rows, full),
                low(width, width),
                low(4, width, width),
                big(rows, width),
                big(rows, width),
                big(rows, width),
                low(rows, width),
                big(width, width),
                low(rows, width),
                low(rows, third),
                big(2, 2, rows, third),
                low(3, 2, rows, third),
                low(3, 2, rows, third),
                low(2, rows, width),
                big(16, width),
                big(5, 16, width),
                low(units, 16, per, width),
                low(units, 16, per, width),
                low(units, 16, per, width),
                low(units, 16, per, width),
                dma(10),
                dma(7),
                dma(2),
                dma(units, 5),
                dma(units, 5),
                dma(3),
                dma(3),
                dma(5),
                dma(5),
                dma(2),
                dma(2),
                dma(2),
            ],
            compiler_params=pltpu.CompilerParams(
                vmem_limit_bytes=64 * 1024 * 1024, collective_id=0, has_side_effects=True
            ),
        )(*operands, params)
        pick = lambda i: small[i, :per_vec]
        return (
            layer_out,
            in_grad,
            pick(8),
            pick(9),
            d_qkv,
            pick(10),
            pick(11),
            d_wout,
            pick(0),
            pick(1),
            pick(2),
            d_wup,
            up_bias[0, :per_up],
            d_wdown,
            pick(3),
        )

    orders = (order_x, order_y, order_z)
    mlp_out = call(
        functools.partial(mlp_kernel, orders, per, per_down, steps),
        (steps,),
        [
            own_rows,
            fixed((half, width)),
            own_rows,
            fixed((half, width)),
            act,
            fixed((width, width)),
            vec,
            vec,
            vec,
            pl.BlockSpec((width, width), lambda i, _: (0, i)),
            pl.BlockSpec((1, 1, width), lambda i, _: (i, 0, 0)),
            pl.BlockSpec((width, width), lambda i, _: (i, 0)),
            vec,
        ],
        [
            shape_of((half, width), BF16),
            shape_of((half, width), BF16),
            shape_of((rows, width), F32),
            shape_of((rows, width), BF16),
            shape_of((4 + steps, width), F32),
            shape_of((pairs, steps, per, width), BF16),
            shape_of((pairs, steps, per, width), F32),
            shape_of((pairs, per_down, width), BF16),
            shape_of((pairs, per_down, width), F32),
            shape_of((pairs, per, width), BF16),
            shape_of((pairs, per, width), F32),
        ],
        [
            fixed((half, width)),
            fixed((half, width)),
            act,
            act,
            fixed((4 + steps, width)),
            pl.BlockSpec((pairs, 1, per, width), lambda i, _: (0, i, 0, 0)),
            pl.BlockSpec((pairs, 1, per, width), lambda i, _: (0, i, 0, 0)),
            fixed((pairs, per_down, width)),
            fixed((pairs, per_down, width)),
            fixed((pairs, per, width)),
            fixed((pairs, per, width)),
        ],
        scratch=[
            pltpu.VMEM((rows, width), F32),
            pltpu.VMEM((rows, width), BF16),
            pltpu.VMEM((rows, width), F32),
            pltpu.VMEM((rows, width), F32),
            pltpu.VMEM((width, width), F32),
        ],
        flops=(6 * steps + 3) * square,
        nbytes=40 * 10**6,
        trans=2 * rows * ff,
    )(
        info,
        layer_in,
        x_other,
        out_grad,
        g_other,
        ctx,
        out_w,
        row(out_b),
        row(mid_gain),
        row(mid_bias),
        up_w,
        up_b.reshape(steps, 1, width),
        down_w,
        row(down_b),
    )
    out_own, out_other, gmid, gctx, early, s_up, k_up, s_down, k_down, s_out, k_out = mlp_out
    out_back = swap(out_other, 1)

    def reduce(sent, kept, order):
        got = swap(sent, 0)
        for bit in order:
            total = kept + got.astype(F32)
            cut = total.shape[0] // 2
            kept = total[:cut]
            got = swap(total[cut:].astype(BF16), bit)
        return kept, got

    def natural(sent, kept):
        return jnp.stack([kept, sent.astype(F32)], axis=1)

    if halving:
        up_pair = reduce(s_up, k_up, order_x)
        down_pair = reduce(s_down, k_down, order_y)
        out_pair = reduce(s_out, k_out, order_z)

    dq, dbq, dkv_own, dkv_send = call(
        attention_back_kernel,
        (blocks,),
        [att_spec, col, col2, col2, col],
        [
            shape_of((rows, width), BF16),
            shape_of((1, width), F32),
            shape_of((2, rows, width), F32),
            shape_of((2, rows, width), BF16),
        ],
        [col, pl.BlockSpec((1, pair_width), lambda i, _: (0, i)), col2, col2],
        flops=8 * head_flops,
        nbytes=16 * 10**6,
    )(info, att, q, kv, kv_other, gctx)
    dkv_other = swap(dkv_send, 0)
    shard = fixed((pairs, per, width))
    tile = pltpu.VMEM((width, width), F32)
    dn_q, s_q, k_q = call(
        functools.partial(query_back_kernel, order_x, per),
        (1,),
        [act, act, pl.BlockSpec((width, width), lambda i, _: (0, 0))],
        [shape_of((rows, width), F32), shape_of((pairs, per, width), BF16), shape_of((pairs, per, width), F32)],
        [act, shard, shard],
        scratch=[tile],
        flops=2 * square,
        nbytes=6 * 10**6,
    )(info, n1, dq, qkv_w)
    dkv, dbv, s_k, k_k, s_v, k_v = call(
        functools.partial(key_value_back_kernel, (order_x, order_y), per),
        (1,),
        [act, fixed((2, rows, width)), fixed((2, rows, width))],
        [
            shape_of((2, rows, width), BF16),
            shape_of((1, width), F32),
            shape_of((pairs, per, width), BF16),
            shape_of((pairs, per, width), F32),
            shape_of((pairs, per, width), BF16),
            shape_of((pairs, per, width), F32),
        ],
        [fixed((2, rows, width)), vec, shard, shard, shard, shard],
        scratch=[tile],
        flops=2 * square,
        nbytes=10 * 10**6,
    )(info, n1, dkv_own, dkv_other)
    if halving:
        q_pair = reduce(s_q, k_q, order_x)
        k_pair = reduce(s_k, k_k, order_x)
        v_pair = reduce(s_v, k_v, order_y)
    in_own, in_other, late = call(
        input_back_kernel,
        (1,),
        [
            own_rows,
            fixed((half, width)),
            vec,
            fixed((2, rows, width)),
            fixed((width, 3 * width)),
            act,
            act,
            vec,
            vec,
        ],
        [shape_of((half, width), BF16), shape_of((half, width), BF16), shape_of((8, width), F32)],
        [fixed((half, width)), fixed((half, width)), fixed((8, width))],
        flops=2 * square,
        nbytes=10 * 10**6,
    )(info, layer_in, x_other, row(pre_gain), dkv, qkv_w, dn_q, gmid, dbq, dbv)
    in_back = swap(in_other, 1)

    def give_back(own, other):
        first = jnp.where(mine == 0, own, other)
        second = jnp.where(mine == 0, other, own)
        return jnp.stack([first, second])

    layer_out = give_back(out_own, out_back)
    in_grad = give_back(in_own, in_back)

    factor = 1.0 / math.sqrt(seq_here * full * dp)
    vectors = jnp.concatenate([early, late], axis=0)
    if halving:
        for bit in range(bits):
            vectors = vectors + swap(vectors, bit)
    else:
        vectors = lax.psum(vectors, ("dp", "seq"))
    per_vec, per_up = width // devices, ff // devices
    early_rows = 4 + steps
    small, up_bias = call(
        functools.partial(vector_kernel, factor, per_vec, per_up),
        (1,),
        [
            pl.BlockSpec((early_rows, width), lambda i, _: (0, 0)),
            pl.BlockSpec((8, width), lambda i, _: (early_rows // 8, 0)),
        ],
        [shape_of((early_rows + 8, 128), F32), shape_of((8, 128), F32)],
        [fixed((early_rows + 8, 128)), fixed((8, 128))],
    )(info, vectors, vectors)
    pick = lambda i: small[i, :per_vec]
    d_upbias = up_bias[0, :per_up]
    d_outbias, d_midgain, d_midbias, d_downbias = (pick(i) for i in range(4))
    d_pregain, d_prebias, d_qbias, d_vbias = (pick(early_rows + i) for i in range(4))

    if halving:

        def finish(named):
            operands = [v for pair, _ in named for v in pair]
            shapes = [s for _, s in named]
            return call(
                functools.partial(finish_kernel, factor),
                (1,),
                [fixed(v.shape) for v in operands],
                [shape_of(s, F32) for s in shapes],
                [fixed(s) for s in shapes],
            )(info, *operands)

        d_wup, d_wdown, d_wout = finish(
            [(up_pair, (per, ff)), (down_pair, (per_down, width)), (out_pair, (per, width))]
        )
        d_q, d_k, d_v = finish([(pair, (per, width)) for pair in (q_pair, k_pair, v_pair)])
        d_qkv = jnp.concatenate([d_q, d_k, d_v], axis=1)
    else:

        def scatter(value):
            return lax.psum_scatter(value, ("dp", "seq"), scatter_dimension=0, tiled=True) * factor

        d_wup = scatter(
            natural(s_up, k_up).transpose(0, 1, 3, 2, 4).reshape(width, ff)
        )
        d_wdown = scatter(natural(s_down, k_down).reshape(ff, width))
        d_wout = scatter(natural(s_out, k_out).reshape(width, width))
        d_qkv = scatter(
            jnp.concatenate(
                [natural(s, k).reshape(width, width) for s, k in ((s_q, k_q), (s_k, k_k), (s_v, k_v))],
                axis=1,
            )
        )
    return (
        layer_out,
        in_grad,
        d_pregain,
        d_prebias,
        d_qkv,
        d_qbias,
        d_vbias,
        d_wout,
        d_outbias,
        d_midgain,
        d_midbias,
        d_wup,
        d_upbias,
        d_wdown,
        d_downbias,
    )


def solution(mesh):
    both = ("dp", "seq")
    rows = P("dp", "seq", None)
    return jax.shard_map(
        on_device,
        mesh=mesh,
        in_specs=(rows, rows) + (P(),) * 13 + (P("dp", None), P("dp")),
        out_specs=(
            rows,
            rows,
            P(both),
            P(both),
            P(both, None),
            P(both),
            P(both),
            P(both, None),
            P(both),
            P(both),
            P(both),
            P(both, None),
            P(both),
            P(both, None),
            P(both),
        ),
        check_vma=False,
    )
```

```python
import functools
import math

import jax
import jax.numpy as jnp
from jax import lax
from jax.experimental import pallas as pl
from jax.experimental.pallas import tpu as pltpu
from jax.sharding import PartitionSpec as P

HEADS = 12
HEAD_DIM = 64
PATCHES = 196
TEXT = 512
F32 = jnp.float32
BF16 = jnp.bfloat16
VMEM_BYTES = 60 * 1024 * 1024


def dot(lhs, rhs, lhs_dim=1, rhs_dim=0):
    return lax.dot_general(
        lhs, rhs, (((lhs_dim,), (rhs_dim,)), ((), ())), preferred_element_type=F32
    )


def normalize(values):
    center = values - jnp.mean(values, axis=-1, keepdims=True)
    spread = jnp.mean(center * center, axis=-1, keepdims=True)
    scale = lax.rsqrt(spread + 1e-06)
    return center * scale, scale


def normalize_back(unit, scale, gain, cotangent):
    inner = cotangent * gain
    mean_inner = jnp.mean(inner, axis=-1, keepdims=True)
    mean_unit = jnp.mean(inner * unit, axis=-1, keepdims=True)
    return scale * (inner - mean_inner - unit * mean_unit)


def column_sum(values):
    return jnp.sum(values, axis=0, keepdims=True)


def call(kernel, grid, in_specs, out_shape, out_specs, scratch=(), flops=0, nbytes=0, trans=0):
    return pl.pallas_call(
        kernel,
        grid_spec=pltpu.PrefetchScalarGridSpec(
            num_scalar_prefetch=1,
            grid=grid,
            in_specs=in_specs,
            out_specs=out_specs,
            scratch_shapes=list(scratch),
        ),
        out_shape=out_shape,
        compiler_params=pltpu.CompilerParams(vmem_limit_bytes=VMEM_BYTES),
        cost_estimate=pl.CostEstimate(flops=flops, bytes_accessed=nbytes, transcendentals=trans),
    )


def fixed(shape):
    zeros = (0,) * len(shape)
    return pl.BlockSpec(shape, lambda *_: zeros)


def shape_of(shape, dtype):
    return jax.ShapeDtypeStruct(shape, dtype)


def place(number, order):
    out = 0
    for bit in order:
        out = out * 2 + ((number >> (bit - 1)) & 1)
    return out


def store_shards(tile_ref, send_ref, keep_ref, info_ref, slot, order, rows, pairs, at):
    core = info_ref[1]
    for pair in range(pairs):
        number = pair if at is None else at * pairs + pair
        index = place(number, order) ^ info_ref[slot]
        sent = tile_ref[pl.ds(pl.multiple_of(rows * (2 * pair + 1 - core), 8), rows), :]
        kept = tile_ref[pl.ds(pl.multiple_of(rows * (2 * pair + core), 8), rows), :]
        send_ref[index] = sent.astype(send_ref.dtype).reshape(send_ref.shape[1:])
        keep_ref[index] = kept.reshape(keep_ref.shape[1:])


def qkv_kernel(info_ref, own_ref, other_ref, gain_ref, shift_ref, w_ref, bias_ref, n1_ref, kv_ref):
    @pl.when(pl.program_id(0) == 0)
    def _():
        rows = jnp.concatenate([own_ref[0], other_ref[...]], axis=0).astype(F32)
        unit, _ = normalize(rows)
        n1_ref[...] = (unit * gain_ref[...] + shift_ref[...]).astype(BF16)

    kv_ref[0] = (dot(n1_ref[...], w_ref[...]) + bias_ref[0]).astype(BF16)


def query_kernel(info_ref, n1_ref, w_ref, bias_ref, q_ref):
    q_ref[...] = ((dot(n1_ref[...], w_ref[...]) + bias_ref[...]) * 0.125).astype(BF16)


def halves(value):
    lane = lax.broadcasted_iota(jnp.int32, value.shape, 1)
    zero = jnp.zeros_like(value)
    return jnp.where(lane < HEAD_DIM, value, zero), jnp.where(lane < HEAD_DIM, zero, value)


def join(first, second):
    lane = lax.broadcasted_iota(jnp.int32, first.shape, 1)
    return jnp.where(lane < HEAD_DIM, first, second)


def attention_kernel(info_ref, q_ref, own_ref, other_ref, mask_ref, ctx_ref, att_ref):
    keys = jnp.concatenate([own_ref[0], other_ref[0]], axis=0)
    values = jnp.concatenate([own_ref[1], other_ref[1]], axis=0)
    parts = []
    for head, query in enumerate(halves(q_ref[...])):
        scores = dot(query, keys, 1, 1) + mask_ref[...]
        exponent = jnp.exp(scores - jnp.max(scores, axis=-1, keepdims=True))
        total = jnp.sum(exponent, axis=-1, keepdims=True)
        att = (exponent * (1.0 / total)).astype(BF16)
        att_ref[head] = att
        parts.append(dot(att, values))
    ctx_ref[...] = join(*parts).astype(BF16)


def attention_back_kernel(
    info_ref, att_ref, q_ref, own_ref, other_ref, gctx_ref, dq_ref, dbq_ref, down_ref, dother_ref
):
    keys = jnp.concatenate([own_ref[0], other_ref[0]], axis=0)
    values = jnp.concatenate([own_ref[1], other_ref[1]], axis=0)
    queries = q_ref[...]
    gctx = gctx_ref[...]
    dq, dk, dv = [], [], []
    for head, grad in enumerate(halves(gctx)):
        att = att_ref[head]
        wide = att.astype(F32)
        datt = dot(grad, values, 1, 1)
        inner = jnp.sum(wide * datt, axis=-1, keepdims=True)
        dscore = (wide * (datt - inner)).astype(BF16)
        dq.append(dot(dscore, keys))
        dk.append(dot(dscore, queries, 0, 0))
        dv.append(dot(att, gctx, 0, 0))
    dquery = join(*dq) * 0.125
    dq_ref[...] = dquery.astype(BF16)
    dbq_ref[...] = column_sum(dquery)
    rows = queries.shape[0]
    for i, grad in enumerate((join(*dk), join(*dv))):
        down_ref[i] = grad[:rows]
        dother_ref[i] = grad[rows:].astype(BF16)


def mlp_kernel(
    orders,
    rows_up,
    rows_down,
    steps,
    info_ref,
    x_ref,
    xo_ref,
    g_ref,
    go_ref,
    ctx_ref,
    wo_ref,
    bo_ref,
    gain_ref,
    shift_ref,
    wu_ref,
    bu_ref,
    wd_ref,
    bd_ref,
    out_ref,
    outo_ref,
    gmid_ref,
    gctx_ref,
    vec_ref,
    su_ref,
    ku_ref,
    sd_ref,
    kd_ref,
    so_ref,
    ko_ref,
    mid_ref,
    n2_ref,
    acc_ref,
    dn_ref,
    tile_ref,
):
    step = pl.program_id(0)
    half = xo_ref.shape[0]
    grad_low = jnp.concatenate([g_ref[0], go_ref[...]], axis=0)

    @pl.when(step == 0)
    def _():
        rows = jnp.concatenate([x_ref[0], xo_ref[...]], axis=0).astype(F32)
        middle = rows + dot(ctx_ref[...], wo_ref[...]) + bo_ref[...]
        mid_ref[...] = middle
        unit, _ = normalize(middle)
        n2_ref[...] = (unit * gain_ref[...] + shift_ref[...]).astype(BF16)
        acc_ref[...] = middle + bd_ref[...]
        dn_ref[...] = jnp.zeros_like(dn_ref)

    normed = n2_ref[...]
    pre = dot(normed, wu_ref[...]) + bu_ref[0]
    phi = 0.5 * (1.0 + lax.erf(pre * math.sqrt(0.5)))
    hidden = (pre * phi).astype(BF16)
    slope = phi + pre * (jnp.exp(-0.5 * pre * pre) * (1.0 / math.sqrt(2 * math.pi)))
    acc_ref[...] += dot(hidden, wd_ref[...])
    grad_pre = dot(grad_low, wd_ref[...], 1, 1) * slope
    vec_ref[pl.ds(4 + step, 1), :] = column_sum(grad_pre)
    gpre_low = grad_pre.astype(BF16)
    dn_ref[...] += dot(gpre_low, wu_ref[...], 1, 1)
    tile_ref[...] = dot(normed, gpre_low, 0, 0)
    n_up = tile_ref.shape[0] // (2 * rows_up)
    store_shards(tile_ref, su_ref, ku_ref, info_ref, 2, orders[0], rows_up, n_up, None)
    tile_ref[...] = dot(hidden, grad_low, 0, 0)
    n_down = tile_ref.shape[0] // (2 * rows_down)
    for at in range(steps):

        @pl.when(step == at)
        def _(at=at):
            store_shards(tile_ref, sd_ref, kd_ref, info_ref, 3, orders[1], rows_down, n_down, at)

    @pl.when(step == steps - 1)
    def _():
        result = acc_ref[...].astype(BF16)
        out_ref[...] = result[:half]
        outo_ref[...] = result[half:]
        unit, scale = normalize(mid_ref[...])
        dn = dn_ref[...]
        grad = grad_low.astype(F32)
        gmid = grad + normalize_back(unit, scale, gain_ref[...], dn)
        gmid_ref[...] = gmid
        vec_ref[0:1, :] = column_sum(gmid)
        vec_ref[1:2, :] = column_sum(dn * unit)
        vec_ref[2:3, :] = column_sum(dn)
        vec_ref[3:4, :] = column_sum(grad)
        low = gmid.astype(BF16)
        gctx_ref[...] = dot(low, wo_ref[...], 1, 1).astype(BF16)
        tile_ref[...] = dot(ctx_ref[...], low, 0, 0)
        store_shards(tile_ref, so_ref, ko_ref, info_ref, 4, orders[2], rows_up, n_up, None)


def query_back_kernel(order, rows, info_ref, n1_ref, dq_ref, w_ref, dn_ref, s_ref, k_ref, tile_ref):
    tile_ref[...] = dot(n1_ref[...], dq_ref[...], 0, 0)
    pairs = tile_ref.shape[0] // (2 * rows)
    store_shards(tile_ref, s_ref, k_ref, info_ref, 2, order, rows, pairs, None)
    dn_ref[...] = dot(dq_ref[...], w_ref[...], 1, 1)


def key_value_back_kernel(
    orders, rows, info_ref, n1_ref, own_ref, other_ref, dkv_ref, dbv_ref, sk_ref, kk_ref, sv_ref, kv_ref, tile_ref
):
    pairs = tile_ref.shape[0] // (2 * rows)
    for i, (s_ref, k_ref, slot) in enumerate(((sk_ref, kk_ref, 2), (sv_ref, kv_ref, 3))):
        grad = own_ref[i] + other_ref[i].astype(F32)
        low = grad.astype(BF16)
        dkv_ref[i] = low
        if i == 1:
            dbv_ref[...] = column_sum(grad)
        tile_ref[...] = dot(n1_ref[...], low, 0, 0)
        store_shards(tile_ref, s_ref, k_ref, info_ref, slot, orders[i], rows, pairs, None)


def input_back_kernel(
    info_ref, x_ref, xo_ref, gain_ref, dkv_ref, w_ref, dnq_ref, gmid_ref, dbq_ref, dbv_ref, own_ref, other_ref, vec_ref
):
    half = xo_ref.shape[0]
    dn = dnq_ref[...]
    for i in range(2):
        width = dn.shape[1]
        dn = dn + dot(dkv_ref[i], w_ref[:, (i + 1) * width : (i + 2) * width], 1, 1)
    rows = jnp.concatenate([x_ref[0], xo_ref[...]], axis=0).astype(F32)
    unit, scale = normalize(rows)
    result = (gmid_ref[...] + normalize_back(unit, scale, gain_ref[...], dn)).astype(BF16)
    own_ref[...] = result[:half]
    other_ref[...] = result[half:]
    vec_ref[0:1, :] = column_sum(dn * unit)
    vec_ref[1:2, :] = column_sum(dn)
    vec_ref[2:3, :] = dbq_ref[...]
    vec_ref[3:4, :] = dbv_ref[...]
    vec_ref[4:8, :] = jnp.zeros_like(vec_ref[4:8, :])


def finish_kernel(factor, info_ref, *refs):
    count = len(refs) // 3
    for i in range(count):
        keep, recv, out = refs[2 * i], refs[2 * i + 1], refs[2 * count + i]
        total = (keep[0] + recv[0].astype(F32)) * factor
        if total.ndim == 3:
            width = total.shape[-1]
            for block in range(total.shape[0]):
                out[:, block * width : (block + 1) * width] = total[block]
        else:
            out[...] = total


def vector_kernel(factor, per, per_up, info_ref, early_ref, late_ref, out_ref, up_ref):
    me = info_ref[5]
    width = early_ref.shape[1]
    both = jnp.concatenate([early_ref[...], late_ref[...]], axis=0) * factor
    turned = pltpu.roll(both, lax.rem(width - me * per, width), 1)
    out_ref[...] = turned[:, : out_ref.shape[1]]
    row = (me * per_up) // width
    up = early_ref[pl.ds(4 + row, 1), :] * factor
    up = jnp.broadcast_to(up, (8, width))
    shift = lax.rem(width - (me * per_up - row * width), width)
    up_ref[...] = pltpu.roll(up, shift, 1)[:, : up_ref.shape[1]]


SEND_AT = (0, 0, 8, 12)
LAND_AT = (None, 0, 8, 12)


def differs(bit, mine):
    return bit + mine - 2 * bit * mine


def back_kernel(
    factor,
    plan,
    layer_in_ref,
    x_other_ref,
    out_grad_ref,
    g_other_ref,
    ctx_in_ref,
    n1_in_ref,
    q_in_ref,
    kv_in_ref,
    kvo_in_ref,
    att_in_ref,
    qkv_w_ref,
    out_w_ref,
    up_w_ref,
    down_w_ref,
    par_ref,
    layer_out_ref,
    in_grad_ref,
    dup_ref,
    ddown_ref,
    dout_ref,
    dqkv_ref,
    small_ref,
    upb_ref,
    x_ref,
    g_ref,
    ctx_ref,
    n1_ref,
    q_ref,
    kv_ref,
    kvo_ref,
    att_ref,
    wo_ref,
    w_ref,
    mid_ref,
    acc_ref,
    dn_ref,
    n2_ref,
    tile_ref,
    gctx_ref,
    dg_ref,
    down_ref,
    dsend_ref,
    drecv_ref,
    res_ref,
    ve_ref,
    vl_ref,
    verecv_ref,
    vlrecv_ref,
    s_ref,
    k_ref,
    r0_ref,
    r_ref,
    rz_ref,
    in_sem,
    w_sem,
    att_sem,
    send_sem,
    recv_sem,
    dk_send_sem,
    dk_recv_sem,
    v_send_sem,
    v_recv_sem,
    io_sem,
    io_send_sem,
    io_recv_sem,
):
    half, width = x_other_ref.shape
    rows = 2 * half
    steps = up_w_ref.shape[1] // width
    dp, seq = lax.axis_index("dp"), lax.axis_index("seq")
    core, mine = seq % 2, seq // 2
    y, z = dp % 2, dp // 2
    bits = (mine, y)
    partner_core = {"seq": seq + 1 - 2 * core}
    partner_x = {"seq": seq + 2 - 4 * mine}
    partner_y = {"dp": dp + 1 - 2 * y}
    partner_xy = {"dp": dp + 1 - 2 * y, "seq": seq + 2 - 4 * mine}
    along_z = [{"dp": (dp + 2 * turn) % 8} for turn in (1, 2, 3)]
    plane = (partner_x, partner_y)
    mesh_ids = pl.DeviceIdType.MESH

    barrier = pltpu.get_barrier_semaphore()
    friends = [partner_core, partner_x, partner_y, partner_xy] + along_z
    for other in friends:
        pl.semaphore_signal(barrier, inc=1, device_id=other, device_id_type=mesh_ids)

    loads = [
        (x_other_ref, x_ref.at[pl.ds(half, half)]),
        (layer_in_ref.at[mine], x_ref.at[pl.ds(0, half)]),
        (ctx_in_ref, ctx_ref),
        (out_w_ref, wo_ref),
        (g_other_ref, g_ref.at[pl.ds(half, half)]),
        (out_grad_ref.at[mine], g_ref.at[pl.ds(0, half)]),
        (q_in_ref, q_ref),
        (kv_in_ref, kv_ref),
        (kvo_in_ref, kvo_ref),
        (n1_in_ref, n1_ref),
    ]

    def load(i):
        return pltpu.make_async_copy(loads[i][0], loads[i][1], in_sem.at[i])

    def weights(j, slot):
        at = pl.multiple_of(j * width, width)
        return (
            pltpu.make_async_copy(up_w_ref.at[:, pl.ds(at, width)], w_ref.at[slot], w_sem.at[slot]),
            pltpu.make_async_copy(down_w_ref.at[pl.ds(at, width), :], w_ref.at[2 + slot], w_sem.at[2 + slot]),
        )

    def proj_weights(i):
        return pltpu.make_async_copy(qkv_w_ref.at[:, i * width : (i + 1) * width], w_ref.at[i], w_sem.at[4 + i])

    def attention_load(p, slot):
        return pltpu.make_async_copy(att_in_ref.at[pl.ds(2 * p, 2)], att_ref.at[slot], att_sem.at[slot])

    for i in range(4):
        load(i).start()
    for copy in weights(0, 0):
        copy.start()
    for i in range(4, len(loads)):
        load(i).start()
    for p in range(2):
        attention_load(p, p).start()

    per = s_ref.shape[2]
    up, down, out, qkv = 0, steps, 2 * steps, 2 * steps + 1
    last = qkv + 3
    pair_width = 2 * HEAD_DIM
    piece_lanes = 3 * pair_width

    def buffer(unit):
        if isinstance(unit, int) and unit >= last - 1:
            return last - 1, (unit - last + 1) * piece_lanes, piece_lanes
        return unit, 0, width

    def is_last(unit):
        return isinstance(unit, int) and unit == last

    def remote(unit, sem, sent, landing, target):
        return pltpu.make_async_remote_copy(
            src_ref=sent,
            dst_ref=landing,
            send_sem=send_sem.at[unit, sem],
            recv_sem=recv_sem.at[unit, sem],
            device_id=target,
            device_id_type=mesh_ids,
        )

    def remaining(axes, stage):
        count = 16
        for axis in axes[: stage - 1]:
            count //= 4 if axis == 2 else 2
        return count

    def land_at(axes, stage):
        return 14 if stage == 3 and axes[2] != 2 else LAND_AT[stage]

    def arrived(unit, stage, axes):
        at, first, lanes = buffer(unit)
        cols = slice(first, first + lanes)
        if stage == 0:
            return 16, lambda i: k_ref[at, i, :, cols].astype(F32) + r0_ref[at, i, :, cols].astype(F32)
        if is_last(unit):
            axis, count, held, landing = (None, 4, 0, 0) if stage == 1 else (2, 1, z, LAND_AT[3])
        else:
            axis, landing = axes[stage - 1], land_at(axes, stage)
            count = remaining(axes, stage + 1)
            held = z * count if axis == 2 else 0

        def piece(i):
            value = k_ref[at, held + i, :, cols].astype(F32)
            for n in range(3 if axis in (None, 2) else 1):
                value = value + r_ref[at, landing + n * count + i, :, cols].astype(F32)
            return value

        return count, piece

    def transfers(unit, stage, axes):
        at, first, lanes = buffer(unit)
        cols = slice(first, first + lanes)
        if stage == 0:
            return [remote(unit, 0, s_ref.at[at, :, :, cols], r0_ref.at[at, :, :, cols], partner_core)]
        if stage < 3 and is_last(unit):
            targets = (partner_y, partner_x, partner_xy)
            return [
                remote(
                    unit,
                    1 + i,
                    s_ref.at[at, pl.ds(4 + 4 * i, 4), :, cols],
                    r_ref.at[at, pl.ds(4 * i, 4), :, cols],
                    targets[i],
                )
                for i in range(3)
            ]
        if is_last(unit):
            sent, landing, count = 0, LAND_AT[3], 1
        else:
            sent, landing, count = SEND_AT[stage], land_at(axes, stage), remaining(axes, stage)
            if axes[stage - 1] != 2:
                half_count = count // 2
                return [
                    remote(
                        unit,
                        stage,
                        s_ref.at[at, pl.ds(sent, half_count), :, cols],
                        r_ref.at[at, pl.ds(landing, half_count), :, cols],
                        plane[axes[stage - 1]],
                    )
                ]
            count //= 4
        return [
            remote(
                unit,
                4 + i,
                s_ref.at[at, pl.ds(sent + (z + 1 + i) % 4 * count, count), :, cols],
                r_ref.at[at, pl.ds(landing + i * count, count), :, cols],
                along_z[i],
            )
            for i in range(3)
        ]

    def start(unit, stage, axes):
        for copy in transfers(unit, stage, axes):
            copy.start()

    def finish(unit, stage, axes):
        for copy in transfers(unit, stage, axes):
            copy.wait()

    def down_send(j, unit):
        place = (j - z + 3) % 4
        return [
            remote(
                unit,
                4 + place,
                s_ref.at[unit, pl.ds(SEND_AT[3], 4)],
                rz_ref.at[place],
                {"dp": 2 * j + y},
            )
        ]

    def advance(unit, stage, axes):
        finish(unit, stage, axes)
        at, first, lanes = buffer(unit)
        cols = slice(first, first + lanes)
        count, piece = arrived(unit, stage, axes)
        following = 3 if is_last(unit) and stage == 1 else stage + 1
        sent = 0 if is_last(unit) else SEND_AT[following]
        if is_last(unit) or axes[following - 1] == 2:

            @pl.loop(0, count)
            def _(i):
                value = piece(i).astype(BF16)
                k_ref[at, i, :, cols] = value
                s_ref[at, sent + i, :, cols] = value

        else:

            @pl.loop(0, count // 2)
            def _(i):
                stays, goes = piece(i), piece(count // 2 + i)
                k_ref[at, i, :, cols] = stays.astype(BF16)
                s_ref[at, sent + i, :, cols] = goes.astype(BF16)

        if following == 3 and isinstance(unit, int) and down <= unit < out:
            chunk = unit - down

            @pl.when(z != chunk)
            def _():
                for copy in down_send(chunk, unit):
                    copy.start()

        else:
            start(unit, following, axes)

    def total(unit, axes):
        finish(unit, 3, axes)
        _, piece = arrived(unit, 3, axes)
        return piece(0) * factor

    def place_unit(at, axes, first, lanes):
        count, weight = 16, {}
        for axis in axes:
            count //= 4 if axis == 2 else 2
            weight[axis] = count
        for far in range(4):

            @pl.loop(0, 4)
            def _(near, far=far):
                index = weight[2] * far
                for axis, value in enumerate((near % 2, near // 2)):
                    index = index + weight[axis] * differs(value, bits[axis])
                top = per * (2 * (4 * far + near))
                sent = pl.multiple_of(top + per * (1 - core), 8)
                kept = pl.multiple_of(top + per * core, 8)
                cols = pl.ds(first, lanes)
                s_ref[at, index, :, cols] = tile_ref[pl.ds(sent, per), cols].astype(BF16)
                k_ref[at, index, :, cols] = tile_ref[pl.ds(kept, per), cols].astype(BF16)

    def place_down(at, axes):
        a, b, _ = axes
        block = steps * per

        @pl.loop(0, 4)
        def _(near):
            value = (near % 2, near // 2)
            index = 8 * differs(value[a], bits[a]) + 4 * differs(value[b], bits[b])
            for part in range(steps):
                sent = pl.multiple_of(block * (2 * near + 1 - core) + part * per, 8)
                kept = pl.multiple_of(block * (2 * near + core) + part * per, 8)
                s_ref[at, index + part] = tile_ref[pl.ds(sent, per), :].astype(BF16)
                k_ref[at, index + part] = tile_ref[pl.ds(kept, per), :].astype(BF16)

    def vector_copy(late, n):
        ref, recv = (vl_ref, vlrecv_ref) if late else (ve_ref, verecv_ref)
        if late:
            target = ([partner_core, partner_x, partner_y, partner_xy] + along_z)[n]
        else:
            target = ([partner_core, partner_x, partner_y] + along_z)[n]
        return pltpu.make_async_remote_copy(
            src_ref=ref,
            dst_ref=recv.at[n],
            send_sem=v_send_sem.at[late, n],
            recv_sem=v_recv_sem.at[late, n],
            device_id=target,
            device_id_type=mesh_ids,
        )

    STEPS = (((0,), (1,), (2,), (3, 4, 5)), ((0,), (1, 2, 3), (4, 5, 6)))

    def vector_step(late, n):
        ref, recv = (vl_ref, vlrecv_ref) if late else (ve_ref, verecv_ref)
        if n:
            for i in STEPS[late][n - 1]:
                vector_copy(late, i).wait()
            for i in STEPS[late][n - 1]:
                ref[...] += recv[i]
        if n < len(STEPS[late]):
            for i in STEPS[late][n]:
                vector_copy(late, i).start()

    orders, in_chunk, after_mlp, in_pair, after_proj, tail = plan

    def run(events):
        for unit, stage in events:
            if unit == "give":
                for copy in give(*((layer_out_ref, 0), (in_grad_ref, 1))[stage]):
                    copy.start()
            elif unit == "early":
                vector_step(0, stage)
            elif unit == "late":
                vector_step(1, stage)
            else:
                advance(unit, stage, orders[unit])

    for i in range(4):
        load(i).wait()
    middle = x_ref[...].astype(F32) + dot(ctx_ref[...], wo_ref[...]) + par_ref[0:1, :]
    mid_ref[...] = middle
    unit_mid, _ = normalize(middle)
    n2_ref[...] = (unit_mid * par_ref[1:2, :] + par_ref[2:3, :]).astype(BF16)
    acc_ref[...] = middle + par_ref[3:4, :]
    dn_ref[...] = jnp.zeros_like(dn_ref)
    vl_ref[...] = jnp.zeros_like(vl_ref)
    for i in range(4, 6):
        load(i).wait()
    pl.semaphore_wait(barrier, len(friends))

    def chunk_events(j, where):
        for n in range(steps):
            if in_chunk[n][where]:

                @pl.when(j == n)
                def _(n=n):
                    run(in_chunk[n][where])

    @pl.loop(0, steps)
    def _(j):
        slot = j % 2
        for copy in weights(j, slot):
            copy.wait()

        @pl.when(j + 1 < steps)
        def _():
            for copy in weights(j + 1, 1 - slot):
                copy.start()

        normed = n2_ref[...]
        grad_low = g_ref[...]
        wu, wd = w_ref.at[slot], w_ref.at[2 + slot]
        pre = dot(normed, wu[...]) + par_ref[pl.ds(8 + j, 1), :]
        phi = 0.5 * (1.0 + lax.erf(pre * math.sqrt(0.5)))
        hidden = (pre * phi).astype(BF16)
        slope = phi + pre * (jnp.exp(-0.5 * pre * pre) * (1.0 / math.sqrt(2 * math.pi)))
        chunk_events(j, 0)
        acc_ref[...] += dot(hidden, wd[...])
        tile_ref[...] = dot(hidden, grad_low, 0, 0)
        place_down(down + j, orders[down])
        start(down + j, 0, orders[down])
        grad_pre = dot(grad_low, wd[...], 1, 1) * slope
        ve_ref[pl.ds(4 + j, 1), :] = column_sum(grad_pre)
        gpre_low = grad_pre.astype(BF16)
        chunk_events(j, 1)
        tile_ref[...] = dot(normed, gpre_low, 0, 0)
        place_unit(up + j, orders[up], 0, width)
        start(up + j, 0, orders[up])
        dn_ref[...] += dot(gpre_low, wu[...], 1, 1)
        chunk_events(j, 2)

    for i in range(3):
        proj_weights(i).start()
    res_ref[0] = acc_ref[...].astype(BF16)

    def give(ref, n):
        mine_copy = pltpu.make_async_copy(res_ref.at[n, pl.ds(0, half)], ref.at[mine], io_sem.at[n])
        other_copy = pltpu.make_async_remote_copy(
            src_ref=res_ref.at[n, pl.ds(half, half)],
            dst_ref=ref.at[mine],
            send_sem=io_send_sem.at[n],
            recv_sem=io_recv_sem.at[n],
            device_id=partner_x,
            device_id_type=mesh_ids,
        )
        return mine_copy, other_copy

    unit_mid, scale = normalize(mid_ref[...])
    dn = dn_ref[...]
    grad = g_ref[...].astype(F32)
    gmid = grad + normalize_back(unit_mid, scale, par_ref[1:2, :], dn)
    ve_ref[0:1, :] = column_sum(gmid)
    ve_ref[1:2, :] = column_sum(dn * unit_mid)
    ve_ref[2:3, :] = column_sum(dn)
    ve_ref[3:4, :] = column_sum(grad)
    acc_ref[...] = gmid
    low = gmid.astype(BF16)
    tile_ref[...] = dot(ctx_ref[...], low, 0, 0)
    place_unit(out, orders[out], 0, width)
    start(out, 0, orders[out])
    gctx_ref[...] = dot(low, wo_ref[...], 1, 1).astype(BF16)
    dn_ref[...] = jnp.zeros_like(dn_ref)
    for i in range(6, len(loads)):
        load(i).wait()
    run(after_mlp)

    third = 2 * pair_width

    def exchange(p):
        return pltpu.make_async_remote_copy(
            src_ref=dsend_ref.at[p % 3],
            dst_ref=drecv_ref.at[p],
            send_sem=dk_send_sem.at[p],
            recv_sem=dk_recv_sem.at[p],
            device_id=partner_core,
            device_id_type=mesh_ids,
        )

    def project(pairs, unit):
        at, first, lanes = buffer(unit)
        span = len(pairs) * pair_width
        for i, p in enumerate(pairs):
            exchange(p).wait()
            lane = slice(p * pair_width, (p + 1) * pair_width)
            here = slice(i * pair_width, (i + 1) * pair_width)
            for n in range(2):
                grad = down_ref[p % 3, n] + drecv_ref[p, n].astype(F32)
                if n == 1:
                    vl_ref[3:4, lane] = column_sum(grad)
                dg_ref[1 + n, :, here] = grad.astype(BF16)
            dg_ref[0, :, here] = dq_of(p)
        cols = slice(pairs[0] * pair_width, pairs[0] * pair_width + span)
        for n in range(3):
            tile_ref[:, first + n * span : first + (n + 1) * span] = dot(n1_ref[...], dg_ref[n, :, :span], 0, 0)
        place_unit(at, orders[unit], first, lanes)
        start(unit, 0, orders[unit])
        more = dot(dg_ref[0, :, :span], w_ref[0, :, cols], 1, 1)
        for n in range(1, 3):
            more = more + dot(dg_ref[n, :, :span], w_ref[n, :, cols], 1, 1)
        dn_ref[...] += more

    def dq_of(p):
        return dg_ref[3, :, (p % 3) * pair_width : (p % 3 + 1) * pair_width]

    def attention_pair(p, slot, third_slot, between):
        attention_load(p, slot).wait()
        lanes = pl.ds(pl.multiple_of(p * pair_width, pair_width), pair_width)
        keys = jnp.concatenate([kv_ref[0, :, lanes], kvo_ref[0, :, lanes]], axis=0)
        values = jnp.concatenate([kv_ref[1, :, lanes], kvo_ref[1, :, lanes]], axis=0)
        queries = q_ref[:, lanes]
        gctx = gctx_ref[:, lanes]
        dq, dk, dv = [], [], []
        for head, grad in enumerate(halves(gctx)):
            att = att_ref[slot, head]
            wide = att.astype(F32)
            datt = dot(grad, values, 1, 1)
            inner = jnp.sum(wide * datt, axis=-1, keepdims=True)
            dscore = (wide * (datt - inner)).astype(BF16)
            dq.append(dot(dscore, keys))
            dk.append(dot(dscore, queries, 0, 0))
            dv.append(dot(att, gctx, 0, 0))
            if head == 0:
                between()
        dquery = join(*dq) * 0.125
        dg_ref[3, :, pl.ds(pl.multiple_of(third_slot * pair_width, pair_width), pair_width)] = dquery.astype(BF16)
        vl_ref[2:3, lanes] = column_sum(dquery)
        for n, grad in enumerate((join(*dk), join(*dv))):
            down_ref[third_slot, n] = grad[:rows]
            dsend_ref[third_slot, n] = grad[rows:].astype(BF16)
        exchange(p).start()

    def pairs_loop(first, count):
        def pair_events(i, where):
            for n in range(count):
                if in_pair[first + n][where]:

                    @pl.when(i == n)
                    def _(n=n):
                        run(in_pair[first + n][where])

        @pl.loop(0, count)
        def _(i):
            p = first + i
            attention_pair(p, p % 2, p % 3, lambda: pair_events(i, 0))

            @pl.when(p + 2 < HEADS // 2)
            def _():
                attention_load(p + 2, p % 2).start()

            pair_events(i, 1)

    pairs_loop(0, 3)
    for i in range(3):
        proj_weights(i).wait()
    project((0, 1), qkv)
    run(after_proj[0])
    pairs_loop(3, 2)
    project((2, 3), qkv + 1)
    run(after_proj[1])
    pairs_loop(5, 1)
    project((4,), last - 1)
    run(after_proj[2])
    project((5,), last)
    run(after_proj[3])

    unit_in, scale = normalize(x_ref[...].astype(F32))
    dn = dn_ref[...]
    res_ref[1] = (acc_ref[...] + normalize_back(unit_in, scale, par_ref[4:5, :], dn)).astype(BF16)
    vl_ref[0:1, :] = column_sum(dn * unit_in)
    vl_ref[1:2, :] = column_sum(dn)
    vector_step(1, 0)
    run(tail)

    me = dp * lax.axis_size("seq") + seq
    both = jnp.concatenate([ve_ref[...], vl_ref[...]], axis=0) * factor
    turned = pltpu.roll(both, (width - me * per) % width, 1)
    small_ref[...] = turned[:, : small_ref.shape[1]]
    per_up = steps * per
    row = (me * per_up) // width
    up_bias = jnp.broadcast_to(ve_ref[pl.ds(4 + row, 1), :] * factor, (8, width))
    shift = (width - (me * per_up - row * width)) % width
    upb_ref[...] = pltpu.roll(up_bias, shift, 1)[:, : upb_ref.shape[1]]

    for j in range(steps):
        dup_ref[:, j * width : (j + 1) * width] = total(up + j, orders[up])
    for j in range(steps):

        @pl.when(z == j)
        def _(j=j):
            for i in range(3):
                remote(down + j, 4 + i, rz_ref.at[i], rz_ref.at[i], along_z[i]).wait_recv()
            for part in range(steps):
                value = k_ref[down + j, part].astype(F32)
                for i in range(3):
                    value = value + rz_ref[i, part].astype(F32)
                ddown_ref[part * per : (part + 1) * per, :] = value * factor

        @pl.when(z != j)
        def _(j=j):
            for copy in down_send(j, down + j):
                copy.wait_send()

    dout_ref[...] = total(out, orders[out])
    for pairs, unit in (((0, 1), qkv), ((2, 3), qkv + 1), ((4,), last - 1), ((5,), last)):
        value = total(unit, orders[unit])
        span = len(pairs) * pair_width
        for n in range(3):
            at = n * width + pairs[0] * pair_width
            dqkv_ref[:, at : at + span] = value[:, n * span : (n + 1) * span]
    for n, ref in enumerate((layer_out_ref, in_grad_ref)):
        for copy in give(ref, n):
            copy.wait()

def results_kernel(info_ref, small_ref, upb_ref, *refs):
    count = (len(refs) - 9) // 2
    big_in, outs = refs[:count], refs[count:]
    for i in range(count):
        outs[i][...] = big_in[i][...]
    vectors = outs[count:]
    for i, row in enumerate((8, 9, 10, 11, 0, 1, 2, 3)):
        vectors[i][...] = small_ref[row : row + 1, : vectors[i].shape[1]]
    vectors[8][...] = upb_ref[0:1, : vectors[8].shape[1]]


PLAN = (((1, 2, 0), (1, 2, 0), (1, 2, 0), (1, 2, 0), (0, 1, 2), (0, 1, 2), (0, 1, 2), (0, 1, 2), (0, 1, 2), (0, 2, 1), (0, 2, 1), (0, 1, 2), (0, 1, 2)), (((), (), ((4, 0),)), (((0, 0),), (), ((5, 0),)), (((1, 0), (4, 1)), ((0, 1),), ((6, 0),)), (((5, 1), (2, 0), (1, 1)), (), ((0, 2), (4, 2), (7, 0), (6, 1), (3, 0)))), (('early', 0), (5, 2), (1, 2)), ((((8, 0), ('early', 1)), ((7, 1), (2, 1))), ((), ((6, 2), ('give', 0))), ((), ((8, 1), ('early', 2))), (((9, 0), (7, 2)), ()), (((8, 2), ('early', 3)), ()), (((10, 0),), ())), (((2, 2), (3, 1)), ((3, 2), (9, 1)), (('early', 4),), ((11, 0),)), ((12, 0), (10, 1), (9, 2), ('late', 1), ('give', 1), (11, 1), (12, 1), ('late', 2), (11, 2), (10, 2), ('late', 3)))


def on_device(
    layer_in,
    out_grad,
    pre_gain,
    pre_bias,
    qkv_w,
    q_bias,
    v_bias,
    out_w,
    out_b,
    mid_gain,
    mid_bias,
    up_w,
    up_b,
    down_w,
    down_b,
    patch_keep,
    text_len,
):
    seq_here, half, width = layer_in.shape
    dp, seq = lax.axis_size("dp"), lax.axis_size("seq")
    assert seq_here == 2 and seq == 4
    full = half * seq
    rows = 2 * half
    ff = up_w.shape[1]
    steps = ff // width
    devices = dp * seq
    place_seq = lax.axis_index("seq")
    me = lax.axis_index("dp") * seq + place_seq
    mine, core = place_seq // 2, place_seq % 2

    bits = devices.bit_length() - 1
    halving = (dp, seq) == (8, 4) and width % (8 * devices) == 0
    if halving:
        shards, at_me, at_core = devices, me, core
        dp_bits = list(range(2, bits))
        order_x = [1] + dp_bits
        order_y = dp_bits[:1] + [1] + dp_bits[1:]
        order_z = dp_bits[1:] + [1] + dp_bits[:1]
    else:
        shards, at_me, at_core = 32, 0, 0
        order_x = order_y = order_z = [4, 3, 2, 1]
    per = width // shards
    per_down = ff // shards
    pairs = shards // 2
    info = jnp.stack(
        [
            jnp.asarray(v, jnp.int32)
            for v in (
                mine,
                at_core,
                place(at_me >> 1, order_x),
                place(at_me >> 1, order_y),
                place(at_me >> 1, order_z),
                me,
            )
        ]
    )

    def swap(value, bit):
        if bit < 2:
            return lax.ppermute(value, "seq", [(i, i ^ (1 << bit)) for i in range(seq)])
        return lax.ppermute(value, "dp", [(i, i ^ (1 << (bit - 2))) for i in range(dp)])

    row = lambda v: v.reshape(-1, width)
    own_rows = pl.BlockSpec((1, half, width), lambda i, info: (info[0], 0, 0))
    vec = fixed((1, width))
    act = fixed((rows, width))

    x_other = swap(lax.dynamic_index_in_dim(layer_in, 1 - mine, 0, False), 1)
    g_other = swap(lax.dynamic_index_in_dim(out_grad, 1 - mine, 0, False), 1)

    patches = lax.dynamic_index_in_dim(patch_keep, mine, 0, False)
    length = lax.dynamic_index_in_dim(text_len, mine, 0, False)
    valid = jnp.concatenate(
        [
            jnp.ones((2,), jnp.int32),
            patches,
            jnp.ones((1,), jnp.int32),
            (jnp.arange(TEXT, dtype=jnp.int32) < length).astype(jnp.int32),
            jnp.zeros((full - 3 - PATCHES - TEXT,), jnp.int32),
        ]
    )
    valid = valid.reshape(seq, half)
    valid = jnp.concatenate(
        [lax.dynamic_index_in_dim(valid, place_seq ^ turn, 0, True) for turn in (0, 2, 1, 3)], axis=1
    )
    mask = jnp.where(valid > 0, 0.0, -1e30).astype(F32)

    square = 2 * rows * width * width
    kv_bias = jnp.concatenate([jnp.zeros((1, 1, width), F32), v_bias.reshape(1, 1, width)], axis=0)
    n1, kv = call(
        qkv_kernel,
        (2,),
        [
            own_rows,
            fixed((half, width)),
            vec,
            vec,
            pl.BlockSpec((width, width), lambda i, _: (0, i + 1)),
            pl.BlockSpec((1, 1, width), lambda i, _: (i, 0, 0)),
        ],
        [shape_of((rows, width), BF16), shape_of((2, rows, width), BF16)],
        [act, pl.BlockSpec((1, rows, width), lambda i, _: (i, 0, 0))],
        flops=2 * square,
        nbytes=5 * 10**6,
    )(info, layer_in, x_other, row(pre_gain), row(pre_bias), qkv_w, kv_bias)
    kv_other = swap(kv, 0)
    q = call(
        query_kernel,
        (1,),
        [act, pl.BlockSpec((width, width), lambda i, _: (0, 0)), vec],
        shape_of((rows, width), BF16),
        act,
        flops=square,
        nbytes=3 * 10**6,
    )(info, n1, qkv_w, row(q_bias))

    pair_width = 2 * HEAD_DIM
    blocks = width // pair_width
    col = pl.BlockSpec((rows, pair_width), lambda i, _: (0, i))
    col2 = pl.BlockSpec((2, rows, pair_width), lambda i, _: (0, 0, i))
    att_spec = pl.BlockSpec((2, rows, full), lambda i, _: (i, 0, 0))
    head_flops = 2 * rows * full * pair_width * HEADS
    ctx, att = call(
        attention_kernel,
        (blocks,),
        [col, col2, col2, fixed((1, full))],
        [shape_of((rows, width), BF16), shape_of((HEADS, rows, full), BF16)],
        [col, att_spec],
        flops=4 * head_flops,
        nbytes=12 * 10**6,
        trans=HEADS * rows * full,
    )(info, q, kv, kv_other, mask)

    factor = 1.0 / math.sqrt(seq_here * full * dp)
    per_vec, per_up = width // devices, ff // devices
    if halving:
        params = jnp.concatenate(
            [row(v) for v in (out_b, mid_gain, mid_bias, down_b, pre_gain, pre_gain, pre_gain, pre_gain, up_b)], axis=0
        )
        hbm = pl.BlockSpec(memory_space=pl.ANY)
        units = 2 * steps + 4
        big = lambda *shape: pltpu.VMEM(shape, F32)
        low = lambda *shape: pltpu.VMEM(shape, BF16)
        dma = lambda *shape: pltpu.SemaphoreType.DMA(shape)
        operands = (layer_in, x_other, out_grad, g_other, ctx, n1, q, kv, kv_other, att, qkv_w, out_w, up_w, down_w)
        results = [(per, ff), (per_down, width), (per, width), (per, 3 * width), (16, 128), (8, 128)]
        *large, small, up_bias = pl.pallas_call(
            functools.partial(back_kernel, factor, PLAN),
            in_specs=[hbm] * len(operands) + [fixed(params.shape)],
            out_shape=[shape_of(layer_in.shape, BF16)] * 2 + [shape_of(s, F32) for s in results],
            out_specs=[hbm] * 2 + [fixed(s) for s in results],
            scratch_shapes=[
                low(rows, width),
                low(rows, width),
                low(rows, width),
                low(rows, width),
                low(rows, width),
                low(2, rows, width),
                low(2, rows, width),
                low(2, 2, rows, full),
                low(width, width),
                low(4, width, width),
                big(rows, width),
                big(rows, width),
                big(rows, width),
                low(rows, width),
                big(width, width),
                low(rows, width),
                low(4, rows, 6 * HEAD_DIM),
                big(3, 2, rows, 2 * HEAD_DIM),
                low(3, 2, rows, 2 * HEAD_DIM),
                low(6, 2, rows, 2 * HEAD_DIM),
                low(2, rows, width),
                big(8, width),
                big(8, width),
                big(6, 8, width),
                big(7, 8, width),
                low(units, 16, per, width),
                low(units, 16, per, width),
                low(units, 16, per, width),
                low(units, 16, per, width),
                low(3, steps, per, width),
                dma(10),
                dma(7),
                dma(2),
                dma(units + 1, 7),
                dma(units + 1, 7),
                dma(6),
                dma(6),
                dma(2, 7),
                dma(2, 7),
                dma(2),
                dma(2),
                dma(2),
            ],
            compiler_params=pltpu.CompilerParams(
                vmem_limit_bytes=64 * 1024 * 1024, collective_id=0, has_side_effects=True
            ),
        )(*operands, params)
        vec_shapes = [(1, per_vec)] * 8 + [(1, per_up)]
        whole = call(
            results_kernel,
            (1,),
            [fixed((16, 128)), fixed((8, 128))] + [fixed(v.shape) for v in large],
            [shape_of(v.shape, v.dtype) for v in large] + [shape_of(s, F32) for s in vec_shapes],
            [fixed(v.shape) for v in large] + [fixed(s) for s in vec_shapes],
        )(info, small, up_bias, *large)
        layer_out, in_grad, d_wup, d_wdown, d_wout, d_qkv = whole[:6]
        d_pregain, d_prebias, d_qbias, d_vbias, d_outbias, d_midgain, d_midbias, d_downbias, d_upbias = (
            v.reshape(-1) for v in whole[6:]
        )
        return (
            layer_out,
            in_grad,
            d_pregain,
            d_prebias,
            d_qkv,
            d_qbias,
            d_vbias,
            d_wout,
            d_outbias,
            d_midgain,
            d_midbias,
            d_wup,
            d_upbias,
            d_wdown,
            d_downbias,
        )

    orders = (order_x, order_y, order_z)
    mlp_out = call(
        functools.partial(mlp_kernel, orders, per, per_down, steps),
        (steps,),
        [
            own_rows,
            fixed((half, width)),
            own_rows,
            fixed((half, width)),
            act,
            fixed((width, width)),
            vec,
            vec,
            vec,
            pl.BlockSpec((width, width), lambda i, _: (0, i)),
            pl.BlockSpec((1, 1, width), lambda i, _: (i, 0, 0)),
            pl.BlockSpec((width, width), lambda i, _: (i, 0)),
            vec,
        ],
        [
            shape_of((half, width), BF16),
            shape_of((half, width), BF16),
            shape_of((rows, width), F32),
            shape_of((rows, width), BF16),
            shape_of((4 + steps, width), F32),
            shape_of((pairs, steps, per, width), BF16),
            shape_of((pairs, steps, per, width), F32),
            shape_of((pairs, per_down, width), BF16),
            shape_of((pairs, per_down, width), F32),
            shape_of((pairs, per, width), BF16),
            shape_of((pairs, per, width), F32),
        ],
        [
            fixed((half, width)),
            fixed((half, width)),
            act,
            act,
            fixed((4 + steps, width)),
            pl.BlockSpec((pairs, 1, per, width), lambda i, _: (0, i, 0, 0)),
            pl.BlockSpec((pairs, 1, per, width), lambda i, _: (0, i, 0, 0)),
            fixed((pairs, per_down, width)),
            fixed((pairs, per_down, width)),
            fixed((pairs, per, width)),
            fixed((pairs, per, width)),
        ],
        scratch=[
            pltpu.VMEM((rows, width), F32),
            pltpu.VMEM((rows, width), BF16),
            pltpu.VMEM((rows, width), F32),
            pltpu.VMEM((rows, width), F32),
            pltpu.VMEM((width, width), F32),
        ],
        flops=(6 * steps + 3) * square,
        nbytes=40 * 10**6,
        trans=2 * rows * ff,
    )(
        info,
        layer_in,
        x_other,
        out_grad,
        g_other,
        ctx,
        out_w,
        row(out_b),
        row(mid_gain),
        row(mid_bias),
        up_w,
        up_b.reshape(steps, 1, width),
        down_w,
        row(down_b),
    )
    out_own, out_other, gmid, gctx, early, s_up, k_up, s_down, k_down, s_out, k_out = mlp_out
    out_back = swap(out_other, 1)

    def reduce(sent, kept, order):
        got = swap(sent, 0)
        for bit in order:
            total = kept + got.astype(F32)
            cut = total.shape[0] // 2
            kept = total[:cut]
            got = swap(total[cut:].astype(BF16), bit)
        return kept, got

    def natural(sent, kept):
        return jnp.stack([kept, sent.astype(F32)], axis=1)

    if halving:
        up_pair = reduce(s_up, k_up, order_x)
        down_pair = reduce(s_down, k_down, order_y)
        out_pair = reduce(s_out, k_out, order_z)

    dq, dbq, dkv_own, dkv_send = call(
        attention_back_kernel,
        (blocks,),
        [att_spec, col, col2, col2, col],
        [
            shape_of((rows, width), BF16),
            shape_of((1, width), F32),
            shape_of((2, rows, width), F32),
            shape_of((2, rows, width), BF16),
        ],
        [col, pl.BlockSpec((1, pair_width), lambda i, _: (0, i)), col2, col2],
        flops=8 * head_flops,
        nbytes=16 * 10**6,
    )(info, att, q, kv, kv_other, gctx)
    dkv_other = swap(dkv_send, 0)
    shard = fixed((pairs, per, width))
    tile = pltpu.VMEM((width, width), F32)
    dn_q, s_q, k_q = call(
        functools.partial(query_back_kernel, order_x, per),
        (1,),
        [act, act, pl.BlockSpec((width, width), lambda i, _: (0, 0))],
        [shape_of((rows, width), F32), shape_of((pairs, per, width), BF16), shape_of((pairs, per, width), F32)],
        [act, shard, shard],
        scratch=[tile],
        flops=2 * square,
        nbytes=6 * 10**6,
    )(info, n1, dq, qkv_w)
    dkv, dbv, s_k, k_k, s_v, k_v = call(
        functools.partial(key_value_back_kernel, (order_x, order_y), per),
        (1,),
        [act, fixed((2, rows, width)), fixed((2, rows, width))],
        [
            shape_of((2, rows, width), BF16),
            shape_of((1, width), F32),
            shape_of((pairs, per, width), BF16),
            shape_of((pairs, per, width), F32),
            shape_of((pairs, per, width), BF16),
            shape_of((pairs, per, width), F32),
        ],
        [fixed((2, rows, width)), vec, shard, shard, shard, shard],
        scratch=[tile],
        flops=2 * square,
        nbytes=10 * 10**6,
    )(info, n1, dkv_own, dkv_other)
    if halving:
        q_pair = reduce(s_q, k_q, order_x)
        k_pair = reduce(s_k, k_k, order_x)
        v_pair = reduce(s_v, k_v, order_y)
    in_own, in_other, late = call(
        input_back_kernel,
        (1,),
        [
            own_rows,
            fixed((half, width)),
            vec,
            fixed((2, rows, width)),
            fixed((width, 3 * width)),
            act,
            act,
            vec,
            vec,
        ],
        [shape_of((half, width), BF16), shape_of((half, width), BF16), shape_of((8, width), F32)],
        [fixed((half, width)), fixed((half, width)), fixed((8, width))],
        flops=2 * square,
        nbytes=10 * 10**6,
    )(info, layer_in, x_other, row(pre_gain), dkv, qkv_w, dn_q, gmid, dbq, dbv)
    in_back = swap(in_other, 1)

    def give_back(own, other):
        first = jnp.where(mine == 0, own, other)
        second = jnp.where(mine == 0, other, own)
        return jnp.stack([first, second])

    layer_out = give_back(out_own, out_back)
    in_grad = give_back(in_own, in_back)

    factor = 1.0 / math.sqrt(seq_here * full * dp)
    vectors = jnp.concatenate([early, late], axis=0)
    if halving:
        for bit in range(bits):
            vectors = vectors + swap(vectors, bit)
    else:
        vectors = lax.psum(vectors, ("dp", "seq"))
    per_vec, per_up = width // devices, ff // devices
    early_rows = 4 + steps
    small, up_bias = call(
        functools.partial(vector_kernel, factor, per_vec, per_up),
        (1,),
        [
            pl.BlockSpec((early_rows, width), lambda i, _: (0, 0)),
            pl.BlockSpec((8, width), lambda i, _: (early_rows // 8, 0)),
        ],
        [shape_of((early_rows + 8, 128), F32), shape_of((8, 128), F32)],
        [fixed((early_rows + 8, 128)), fixed((8, 128))],
    )(info, vectors, vectors)
    pick = lambda i: small[i, :per_vec]
    d_upbias = up_bias[0, :per_up]
    d_outbias, d_midgain, d_midbias, d_downbias = (pick(i) for i in range(4))
    d_pregain, d_prebias, d_qbias, d_vbias = (pick(early_rows + i) for i in range(4))

    if halving:

        def finish(named):
            operands = [v for pair, _ in named for v in pair]
            shapes = [s for _, s in named]
            return call(
                functools.partial(finish_kernel, factor),
                (1,),
                [fixed(v.shape) for v in operands],
                [shape_of(s, F32) for s in shapes],
                [fixed(s) for s in shapes],
            )(info, *operands)

        d_wup, d_wdown, d_wout = finish(
            [(up_pair, (per, ff)), (down_pair, (per_down, width)), (out_pair, (per, width))]
        )
        d_q, d_k, d_v = finish([(pair, (per, width)) for pair in (q_pair, k_pair, v_pair)])
        d_qkv = jnp.concatenate([d_q, d_k, d_v], axis=1)
    else:

        def scatter(value):
            return lax.psum_scatter(value, ("dp", "seq"), scatter_dimension=0, tiled=True) * factor

        d_wup = scatter(
            natural(s_up, k_up).transpose(0, 1, 3, 2, 4).reshape(width, ff)
        )
        d_wdown = scatter(natural(s_down, k_down).reshape(ff, width))
        d_wout = scatter(natural(s_out, k_out).reshape(width, width))
        d_qkv = scatter(
            jnp.concatenate(
                [natural(s, k).reshape(width, width) for s, k in ((s_q, k_q), (s_k, k_k), (s_v, k_v))],
                axis=1,
            )
        )
    return (
        layer_out,
        in_grad,
        d_pregain,
        d_prebias,
        d_qkv,
        d_qbias,
        d_vbias,
        d_wout,
        d_outbias,
        d_midgain,
        d_midbias,
        d_wup,
        d_upbias,
        d_wdown,
        d_downbias,
    )


def solution(mesh):
    both = ("dp", "seq")
    rows = P("dp", "seq", None)
    return jax.shard_map(
        on_device,
        mesh=mesh,
        in_specs=(rows, rows) + (P(),) * 13 + (P("dp", None), P("dp")),
        out_specs=(
            rows,
            rows,
            P(both),
            P(both),
            P(both, None),
            P(both),
            P(both),
            P(both, None),
            P(both),
            P(both),
            P(both),
            P(both, None),
            P(both),
            P(both, None),
            P(both),
        ),
        check_vma=False,
    )
```

```python
import functools
import math

import jax
import jax.numpy as jnp
from jax import lax
from jax.experimental import pallas as pl
from jax.experimental.pallas import tpu as pltpu
from jax.sharding import PartitionSpec as P

HEADS = 12
HEAD_DIM = 64
PATCHES = 196
TEXT = 512
F32 = jnp.float32
BF16 = jnp.bfloat16
VMEM_BYTES = 60 * 1024 * 1024


def dot(lhs, rhs, lhs_dim=1, rhs_dim=0):
    return lax.dot_general(
        lhs, rhs, (((lhs_dim,), (rhs_dim,)), ((), ())), preferred_element_type=F32
    )


def normalize(values):
    center = values - jnp.mean(values, axis=-1, keepdims=True)
    spread = jnp.mean(center * center, axis=-1, keepdims=True)
    scale = lax.rsqrt(spread + 1e-06)
    return center * scale, scale


def normalize_back(unit, scale, gain, cotangent):
    inner = cotangent * gain
    mean_inner = jnp.mean(inner, axis=-1, keepdims=True)
    mean_unit = jnp.mean(inner * unit, axis=-1, keepdims=True)
    return scale * (inner - mean_inner - unit * mean_unit)


def column_sum(values):
    return jnp.sum(values, axis=0, keepdims=True)


def call(kernel, grid, in_specs, out_shape, out_specs, scratch=(), flops=0, nbytes=0, trans=0):
    return pl.pallas_call(
        kernel,
        grid_spec=pltpu.PrefetchScalarGridSpec(
            num_scalar_prefetch=1,
            grid=grid,
            in_specs=in_specs,
            out_specs=out_specs,
            scratch_shapes=list(scratch),
        ),
        out_shape=out_shape,
        compiler_params=pltpu.CompilerParams(vmem_limit_bytes=VMEM_BYTES),
        cost_estimate=pl.CostEstimate(flops=flops, bytes_accessed=nbytes, transcendentals=trans),
    )


def fixed(shape):
    zeros = (0,) * len(shape)
    return pl.BlockSpec(shape, lambda *_: zeros)


def shape_of(shape, dtype):
    return jax.ShapeDtypeStruct(shape, dtype)


def place(number, order):
    out = 0
    for bit in order:
        out = out * 2 + ((number >> (bit - 1)) & 1)
    return out


def store_shards(tile_ref, send_ref, keep_ref, info_ref, slot, order, rows, pairs, at):
    core = info_ref[1]
    for pair in range(pairs):
        number = pair if at is None else at * pairs + pair
        index = place(number, order) ^ info_ref[slot]
        sent = tile_ref[pl.ds(pl.multiple_of(rows * (2 * pair + 1 - core), 8), rows), :]
        kept = tile_ref[pl.ds(pl.multiple_of(rows * (2 * pair + core), 8), rows), :]
        send_ref[index] = sent.astype(send_ref.dtype).reshape(send_ref.shape[1:])
        keep_ref[index] = kept.reshape(keep_ref.shape[1:])


def qkv_kernel(info_ref, own_ref, other_ref, gain_ref, shift_ref, w_ref, bias_ref, n1_ref, kv_ref):
    @pl.when(pl.program_id(0) == 0)
    def _():
        rows = jnp.concatenate([own_ref[0], other_ref[...]], axis=0).astype(F32)
        unit, _ = normalize(rows)
        n1_ref[...] = (unit * gain_ref[...] + shift_ref[...]).astype(BF16)

    kv_ref[0] = (dot(n1_ref[...], w_ref[...]) + bias_ref[0]).astype(BF16)


def query_kernel(info_ref, n1_ref, w_ref, bias_ref, q_ref):
    q_ref[...] = ((dot(n1_ref[...], w_ref[...]) + bias_ref[...]) * 0.125).astype(BF16)


def halves(value):
    lane = lax.broadcasted_iota(jnp.int32, value.shape, 1)
    zero = jnp.zeros_like(value)
    return jnp.where(lane < HEAD_DIM, value, zero), jnp.where(lane < HEAD_DIM, zero, value)


def join(first, second):
    lane = lax.broadcasted_iota(jnp.int32, first.shape, 1)
    return jnp.where(lane < HEAD_DIM, first, second)


def attention_kernel(info_ref, q_ref, own_ref, other_ref, mask_ref, ctx_ref, att_ref):
    keys = jnp.concatenate([own_ref[0], other_ref[0]], axis=0)
    values = jnp.concatenate([own_ref[1], other_ref[1]], axis=0)
    parts = []
    for head, query in enumerate(halves(q_ref[...])):
        scores = dot(query, keys, 1, 1) + mask_ref[...]
        exponent = jnp.exp(scores - jnp.max(scores, axis=-1, keepdims=True))
        total = jnp.sum(exponent, axis=-1, keepdims=True)
        att = (exponent * (1.0 / total)).astype(BF16)
        att_ref[head] = att
        parts.append(dot(att, values))
    ctx_ref[...] = join(*parts).astype(BF16)


def attention_back_kernel(
    info_ref, att_ref, q_ref, own_ref, other_ref, gctx_ref, dq_ref, dbq_ref, down_ref, dother_ref
):
    keys = jnp.concatenate([own_ref[0], other_ref[0]], axis=0)
    values = jnp.concatenate([own_ref[1], other_ref[1]], axis=0)
    queries = q_ref[...]
    gctx = gctx_ref[...]
    dq, dk, dv = [], [], []
    for head, grad in enumerate(halves(gctx)):
        att = att_ref[head]
        wide = att.astype(F32)
        datt = dot(grad, values, 1, 1)
        inner = jnp.sum(wide * datt, axis=-1, keepdims=True)
        dscore = (wide * (datt - inner)).astype(BF16)
        dq.append(dot(dscore, keys))
        dk.append(dot(dscore, queries, 0, 0))
        dv.append(dot(att, gctx, 0, 0))
    dquery = join(*dq) * 0.125
    dq_ref[...] = dquery.astype(BF16)
    dbq_ref[...] = column_sum(dquery)
    rows = queries.shape[0]
    for i, grad in enumerate((join(*dk), join(*dv))):
        down_ref[i] = grad[:rows]
        dother_ref[i] = grad[rows:].astype(BF16)


def mlp_kernel(
    orders,
    rows_up,
    rows_down,
    steps,
    info_ref,
    x_ref,
    xo_ref,
    g_ref,
    go_ref,
    ctx_ref,
    wo_ref,
    bo_ref,
    gain_ref,
    shift_ref,
    wu_ref,
    bu_ref,
    wd_ref,
    bd_ref,
    out_ref,
    outo_ref,
    gmid_ref,
    gctx_ref,
    vec_ref,
    su_ref,
    ku_ref,
    sd_ref,
    kd_ref,
    so_ref,
    ko_ref,
    mid_ref,
    n2_ref,
    acc_ref,
    dn_ref,
    tile_ref,
):
    step = pl.program_id(0)
    half = xo_ref.shape[0]
    grad_low = jnp.concatenate([g_ref[0], go_ref[...]], axis=0)

    @pl.when(step == 0)
    def _():
        rows = jnp.concatenate([x_ref[0], xo_ref[...]], axis=0).astype(F32)
        middle = rows + dot(ctx_ref[...], wo_ref[...]) + bo_ref[...]
        mid_ref[...] = middle
        unit, _ = normalize(middle)
        n2_ref[...] = (unit * gain_ref[...] + shift_ref[...]).astype(BF16)
        acc_ref[...] = middle + bd_ref[...]
        dn_ref[...] = jnp.zeros_like(dn_ref)

    normed = n2_ref[...]
    pre = dot(normed, wu_ref[...]) + bu_ref[0]
    phi = 0.5 * (1.0 + lax.erf(pre * math.sqrt(0.5)))
    hidden = (pre * phi).astype(BF16)
    slope = phi + pre * (jnp.exp(-0.5 * pre * pre) * (1.0 / math.sqrt(2 * math.pi)))
    acc_ref[...] += dot(hidden, wd_ref[...])
    grad_pre = dot(grad_low, wd_ref[...], 1, 1) * slope
    vec_ref[pl.ds(4 + step, 1), :] = column_sum(grad_pre)
    gpre_low = grad_pre.astype(BF16)
    dn_ref[...] += dot(gpre_low, wu_ref[...], 1, 1)
    tile_ref[...] = dot(normed, gpre_low, 0, 0)
    n_up = tile_ref.shape[0] // (2 * rows_up)
    store_shards(tile_ref, su_ref, ku_ref, info_ref, 2, orders[0], rows_up, n_up, None)
    tile_ref[...] = dot(hidden, grad_low, 0, 0)
    n_down = tile_ref.shape[0] // (2 * rows_down)
    for at in range(steps):

        @pl.when(step == at)
        def _(at=at):
            store_shards(tile_ref, sd_ref, kd_ref, info_ref, 3, orders[1], rows_down, n_down, at)

    @pl.when(step == steps - 1)
    def _():
        result = acc_ref[...].astype(BF16)
        out_ref[...] = result[:half]
        outo_ref[...] = result[half:]
        unit, scale = normalize(mid_ref[...])
        dn = dn_ref[...]
        grad = grad_low.astype(F32)
        gmid = grad + normalize_back(unit, scale, gain_ref[...], dn)
        gmid_ref[...] = gmid
        vec_ref[0:1, :] = column_sum(gmid)
        vec_ref[1:2, :] = column_sum(dn * unit)
        vec_ref[2:3, :] = column_sum(dn)
        vec_ref[3:4, :] = column_sum(grad)
        low = gmid.astype(BF16)
        gctx_ref[...] = dot(low, wo_ref[...], 1, 1).astype(BF16)
        tile_ref[...] = dot(ctx_ref[...], low, 0, 0)
        store_shards(tile_ref, so_ref, ko_ref, info_ref, 4, orders[2], rows_up, n_up, None)


def query_back_kernel(order, rows, info_ref, n1_ref, dq_ref, w_ref, dn_ref, s_ref, k_ref, tile_ref):
    tile_ref[...] = dot(n1_ref[...], dq_ref[...], 0, 0)
    pairs = tile_ref.shape[0] // (2 * rows)
    store_shards(tile_ref, s_ref, k_ref, info_ref, 2, order, rows, pairs, None)
    dn_ref[...] = dot(dq_ref[...], w_ref[...], 1, 1)


def key_value_back_kernel(
    orders, rows, info_ref, n1_ref, own_ref, other_ref, dkv_ref, dbv_ref, sk_ref, kk_ref, sv_ref, kv_ref, tile_ref
):
    pairs = tile_ref.shape[0] // (2 * rows)
    for i, (s_ref, k_ref, slot) in enumerate(((sk_ref, kk_ref, 2), (sv_ref, kv_ref, 3))):
        grad = own_ref[i] + other_ref[i].astype(F32)
        low = grad.astype(BF16)
        dkv_ref[i] = low
        if i == 1:
            dbv_ref[...] = column_sum(grad)
        tile_ref[...] = dot(n1_ref[...], low, 0, 0)
        store_shards(tile_ref, s_ref, k_ref, info_ref, slot, orders[i], rows, pairs, None)


def input_back_kernel(
    info_ref, x_ref, xo_ref, gain_ref, dkv_ref, w_ref, dnq_ref, gmid_ref, dbq_ref, dbv_ref, own_ref, other_ref, vec_ref
):
    half = xo_ref.shape[0]
    dn = dnq_ref[...]
    for i in range(2):
        width = dn.shape[1]
        dn = dn + dot(dkv_ref[i], w_ref[:, (i + 1) * width : (i + 2) * width], 1, 1)
    rows = jnp.concatenate([x_ref[0], xo_ref[...]], axis=0).astype(F32)
    unit, scale = normalize(rows)
    result = (gmid_ref[...] + normalize_back(unit, scale, gain_ref[...], dn)).astype(BF16)
    own_ref[...] = result[:half]
    other_ref[...] = result[half:]
    vec_ref[0:1, :] = column_sum(dn * unit)
    vec_ref[1:2, :] = column_sum(dn)
    vec_ref[2:3, :] = dbq_ref[...]
    vec_ref[3:4, :] = dbv_ref[...]
    vec_ref[4:8, :] = jnp.zeros_like(vec_ref[4:8, :])


def finish_kernel(factor, info_ref, *refs):
    count = len(refs) // 3
    for i in range(count):
        keep, recv, out = refs[2 * i], refs[2 * i + 1], refs[2 * count + i]
        total = (keep[0] + recv[0].astype(F32)) * factor
        if total.ndim == 3:
            width = total.shape[-1]
            for block in range(total.shape[0]):
                out[:, block * width : (block + 1) * width] = total[block]
        else:
            out[...] = total


def vector_kernel(factor, per, per_up, info_ref, early_ref, late_ref, out_ref, up_ref):
    me = info_ref[5]
    width = early_ref.shape[1]
    both = jnp.concatenate([early_ref[...], late_ref[...]], axis=0) * factor
    turned = pltpu.roll(both, lax.rem(width - me * per, width), 1)
    out_ref[...] = turned[:, : out_ref.shape[1]]
    row = (me * per_up) // width
    up = early_ref[pl.ds(4 + row, 1), :] * factor
    up = jnp.broadcast_to(up, (8, width))
    shift = lax.rem(width - (me * per_up - row * width), width)
    up_ref[...] = pltpu.roll(up, shift, 1)[:, : up_ref.shape[1]]


SEND_AT = (0, 0, 8, 12)
LAND_AT = (None, 0, 8, 12)


def differs(bit, mine):
    return bit + mine - 2 * bit * mine


def back_kernel(
    factor,
    plan,
    layer_in_ref,
    out_grad_ref,
    qkv_w_ref,
    out_w_ref,
    up_w_ref,
    down_w_ref,
    out_b_ref,
    mid_gain_ref,
    mid_bias_ref,
    down_b_ref,
    pre_gain_ref,
    pre_bias_ref,
    q_bias_ref,
    v_bias_ref,
    up_b_ref,
    patch_ref,
    length_ref,
    layer_out_ref,
    in_grad_ref,
    dup_ref,
    ddown_ref,
    dout_ref,
    dqkv_ref,
    small_ref,
    upb_ref,
    att_hbm_ref,
    par_ref,
    mask_ref,
    x_ref,
    g_ref,
    ctx_ref,
    n1_ref,
    q_ref,
    kv_ref,
    kvo_ref,
    att_ref,
    wo_ref,
    w_ref,
    mid_ref,
    acc_ref,
    dn_ref,
    n2_ref,
    tile_ref,
    gctx_ref,
    dg_ref,
    down_ref,
    dsend_ref,
    drecv_ref,
    res_ref,
    ve_ref,
    vl_ref,
    verecv_ref,
    vlrecv_ref,
    s_ref,
    k_ref,
    r0_ref,
    r_ref,
    rz_ref,
    in_sem,
    w_sem,
    att_sem,
    send_sem,
    recv_sem,
    dk_send_sem,
    dk_recv_sem,
    v_send_sem,
    v_recv_sem,
    io_sem,
    io_send_sem,
    io_recv_sem,
    x_send_sem,
    x_recv_sem,
    kv_send_sem,
    kv_recv_sem,
):
    _, half, width = layer_in_ref.shape
    rows = 2 * half
    steps = up_w_ref.shape[1] // width
    dp, seq = lax.axis_index("dp"), lax.axis_index("seq")
    core, mine = seq % 2, seq // 2
    y, z = dp % 2, dp // 2
    bits = (mine, y)
    partner_core = {"seq": seq + 1 - 2 * core}
    partner_x = {"seq": seq + 2 - 4 * mine}
    partner_y = {"dp": dp + 1 - 2 * y}
    partner_xy = {"dp": dp + 1 - 2 * y, "seq": seq + 2 - 4 * mine}
    along_z = [{"dp": (dp + 2 * turn) % 8} for turn in (1, 2, 3)]
    plane = (partner_x, partner_y)
    mesh_ids = pl.DeviceIdType.MESH

    barrier = pltpu.get_barrier_semaphore()
    friends = [partner_core, partner_x, partner_y, partner_xy] + along_z
    for other in friends:
        pl.semaphore_signal(barrier, inc=1, device_id=other, device_id_type=mesh_ids)

    loads = [
        (layer_in_ref.at[mine], x_ref.at[pl.ds(0, half)]),
        (out_w_ref, wo_ref),
        (out_grad_ref.at[mine], g_ref.at[pl.ds(0, half)]),
    ]

    def load(i):
        return pltpu.make_async_copy(loads[i][0], loads[i][1], in_sem.at[i])

    def weights(j, slot):
        at = pl.multiple_of(j * width, width)
        return (
            pltpu.make_async_copy(up_w_ref.at[:, pl.ds(at, width)], w_ref.at[slot], w_sem.at[slot]),
            pltpu.make_async_copy(down_w_ref.at[pl.ds(at, width), :], w_ref.at[2 + slot], w_sem.at[2 + slot]),
        )

    def proj_weights(i):
        return pltpu.make_async_copy(qkv_w_ref.at[:, i * width : (i + 1) * width], w_ref.at[i], w_sem.at[4 + i])

    def attention_load(p, slot):
        return pltpu.make_async_copy(att_hbm_ref.at[pl.ds(2 * p, 2)], att_ref.at[slot], att_sem.at[slot])

    def attention_store(p, slot):
        return pltpu.make_async_copy(att_ref.at[slot], att_hbm_ref.at[pl.ds(2 * p, 2)], att_sem.at[2 + slot])

    load(0).start()
    for i in (1, 2, 0):
        proj_weights(i).start()
    for i in (1, 2):
        load(i).start()

    def rows_copy(n):
        source, landing = ((layer_in_ref, x_ref), (out_grad_ref, g_ref))[n]
        return pltpu.make_async_remote_copy(
            src_ref=source.at[1 - mine],
            dst_ref=landing.at[pl.ds(half, half)],
            send_sem=x_send_sem.at[n],
            recv_sem=x_recv_sem.at[n],
            device_id=partner_x,
            device_id_type=mesh_ids,
        )

    def keys_copy(b):
        at = pl.ds(pl.multiple_of(b * half, 16), half)
        return pltpu.make_async_remote_copy(
            src_ref=kv_ref.at[:, at],
            dst_ref=kvo_ref.at[:, at],
            send_sem=kv_send_sem.at[b],
            recv_sem=kv_recv_sem.at[b],
            device_id=partner_core,
            device_id_type=mesh_ids,
        )

    pl.semaphore_wait(barrier, len(friends))
    for n in range(2):
        rows_copy(n).start()
    for i, ref in enumerate(
        (out_b_ref, mid_gain_ref, mid_bias_ref, down_b_ref, pre_gain_ref, pre_bias_ref, q_bias_ref, v_bias_ref)
    ):
        par_ref[i : i + 1, :] = ref[...].reshape(1, width)
    for j in range(steps):
        par_ref[8 + j : 9 + j, :] = up_b_ref[j * width : (j + 1) * width].reshape(1, width)

    full = 4 * half
    chunks = (seq, seq + 2 - 4 * mine, seq + 1 - 2 * core, 3 - seq)
    mask_ref[...] = jnp.zeros_like(mask_ref)
    mask_ref[0:1, 2 : 2 + PATCHES] = patch_ref[pl.ds(mine, 1), :].astype(F32)
    first_chunk = core * 2 + mine
    kept = pltpu.roll(mask_ref[...], first_chunk * half, 1)[:, :full]
    lane = lax.broadcasted_iota(jnp.int32, kept.shape, 1)
    chunk = lane // half
    start_row = jnp.where(chunk < 2, jnp.where(chunk < 1, chunks[0], chunks[1]), jnp.where(chunk < 3, chunks[2], chunks[3]))
    number = start_row * half + lane - chunk * half
    token = number - (3 + PATCHES)
    valid = (
        (kept > 0.5)
        | (number < 2)
        | (number == 2 + PATCHES)
        | ((token >= 0) & (token < TEXT) & (token < length_ref[mine]))
    )
    mask_ref[:, :full] = jnp.where(valid, 0.0, -1e30)

    @pl.loop(0, 2)
    def _(b):
        @pl.when(b == 0)
        def _():
            load(0).wait()
            for i in (1, 2, 0):
                proj_weights(i).wait()

        @pl.when(b == 1)
        def _():
            rows_copy(0).wait()

        at = pl.ds(pl.multiple_of(b * half, 16), half)
        unit_in, _ = normalize(x_ref[at, :].astype(F32))
        n1_ref[at, :] = (unit_in * par_ref[4:5, :] + par_ref[5:6, :]).astype(BF16)
        kv_ref[0, at, :] = dot(n1_ref[at, :], w_ref[1]).astype(BF16)
        kv_ref[1, at, :] = (dot(n1_ref[at, :], w_ref[2]) + par_ref[7:8, :]).astype(BF16)
        keys_copy(b).start()
        q_ref[at, :] = ((dot(n1_ref[at, :], w_ref[0]) + par_ref[6:7, :]) * 0.125).astype(BF16)

    for copy in weights(0, 0):
        copy.start()
    for b in range(2):
        keys_copy(b).wait()

    @pl.loop(0, HEADS // 2)
    def _(p):
        slot = p % 2
        lanes = pl.ds(pl.multiple_of(p * 2 * HEAD_DIM, 2 * HEAD_DIM), 2 * HEAD_DIM)
        keys = jnp.concatenate([kv_ref[0, :, lanes], kvo_ref[0, :, lanes]], axis=0)
        values = jnp.concatenate([kv_ref[1, :, lanes], kvo_ref[1, :, lanes]], axis=0)

        @pl.when(p >= 2)
        def _():
            attention_store(p - 2, slot).wait()

        parts = []
        for head, query in enumerate(halves(q_ref[:, lanes])):
            scores = dot(query, keys, 1, 1) + mask_ref[0:1, :full]
            exponent = jnp.exp(scores - jnp.max(scores, axis=-1, keepdims=True))
            norm = jnp.sum(exponent, axis=-1, keepdims=True)
            att = (exponent * (1.0 / norm)).astype(BF16)
            att_ref[slot, head] = att
            parts.append(dot(att, values))
        ctx_ref[:, lanes] = join(*parts).astype(BF16)
        attention_store(p, slot).start()

    for p in (HEADS // 2 - 2, HEADS // 2 - 1):
        attention_store(p, p % 2).wait()
    for p in range(2):
        attention_load(p, p).start()

    per = s_ref.shape[2]
    up, down, out, qkv = 0, steps, 2 * steps, 2 * steps + 1
    last = qkv + 3
    pair_width = 2 * HEAD_DIM
    piece_lanes = 3 * pair_width

    def buffer(unit):
        if isinstance(unit, int) and unit >= last - 1:
            return last - 1, (unit - last + 1) * piece_lanes, piece_lanes
        return unit, 0, width

    def is_last(unit):
        return isinstance(unit, int) and unit == last

    def remote(unit, sem, sent, landing, target):
        return pltpu.make_async_remote_copy(
            src_ref=sent,
            dst_ref=landing,
            send_sem=send_sem.at[unit, sem],
            recv_sem=recv_sem.at[unit, sem],
            device_id=target,
            device_id_type=mesh_ids,
        )

    def remaining(axes, stage):
        count = 16
        for axis in axes[: stage - 1]:
            count //= 4 if axis == 2 else 2
        return count

    def land_at(axes, stage):
        return 14 if stage == 3 and axes[2] != 2 else LAND_AT[stage]

    def arrived(unit, stage, axes):
        at, first, lanes = buffer(unit)
        cols = slice(first, first + lanes)
        if stage == 0:
            return 16, lambda i: k_ref[at, i, :, cols].astype(F32) + r0_ref[at, i, :, cols].astype(F32)
        if is_last(unit):
            axis, count, held, landing = (None, 4, 0, 0) if stage == 1 else (2, 1, z, LAND_AT[3])
        else:
            axis, landing = axes[stage - 1], land_at(axes, stage)
            count = remaining(axes, stage + 1)
            held = z * count if axis == 2 else 0

        def piece(i):
            value = k_ref[at, held + i, :, cols].astype(F32)
            for n in range(3 if axis in (None, 2) else 1):
                value = value + r_ref[at, landing + n * count + i, :, cols].astype(F32)
            return value

        return count, piece

    def transfers(unit, stage, axes):
        at, first, lanes = buffer(unit)
        cols = slice(first, first + lanes)
        if stage == 0:
            return [remote(unit, 0, s_ref.at[at, :, :, cols], r0_ref.at[at, :, :, cols], partner_core)]
        if stage < 3 and is_last(unit):
            targets = (partner_y, partner_x, partner_xy)
            return [
                remote(
                    unit,
                    1 + i,
                    s_ref.at[at, pl.ds(4 + 4 * i, 4), :, cols],
                    r_ref.at[at, pl.ds(4 * i, 4), :, cols],
                    targets[i],
                )
                for i in range(3)
            ]
        if is_last(unit):
            sent, landing, count = 0, LAND_AT[3], 1
        else:
            sent, landing, count = SEND_AT[stage], land_at(axes, stage), remaining(axes, stage)
            if axes[stage - 1] != 2:
                half_count = count // 2
                return [
                    remote(
                        unit,
                        stage,
                        s_ref.at[at, pl.ds(sent, half_count), :, cols],
                        r_ref.at[at, pl.ds(landing, half_count), :, cols],
                        plane[axes[stage - 1]],
                    )
                ]
            count //= 4
        return [
            remote(
                unit,
                4 + i,
                s_ref.at[at, pl.ds(sent + (z + 1 + i) % 4 * count, count), :, cols],
                r_ref.at[at, pl.ds(landing + i * count, count), :, cols],
                along_z[i],
            )
            for i in range(3)
        ]

    def start(unit, stage, axes):
        for copy in transfers(unit, stage, axes):
            copy.start()

    def finish(unit, stage, axes):
        for copy in transfers(unit, stage, axes):
            copy.wait()

    def down_send(j, unit):
        place = (j - z + 3) % 4
        return [
            remote(
                unit,
                4 + place,
                s_ref.at[unit, pl.ds(SEND_AT[3], 4)],
                rz_ref.at[place],
                {"dp": 2 * j + y},
            )
        ]

    def advance(unit, stage, axes):
        finish(unit, stage, axes)
        at, first, lanes = buffer(unit)
        cols = slice(first, first + lanes)
        count, piece = arrived(unit, stage, axes)
        following = 3 if is_last(unit) and stage == 1 else stage + 1
        sent = 0 if is_last(unit) else SEND_AT[following]
        if is_last(unit) or axes[following - 1] == 2:

            @pl.loop(0, count)
            def _(i):
                value = piece(i).astype(BF16)
                k_ref[at, i, :, cols] = value
                s_ref[at, sent + i, :, cols] = value

        else:

            @pl.loop(0, count // 2)
            def _(i):
                stays, goes = piece(i), piece(count // 2 + i)
                k_ref[at, i, :, cols] = stays.astype(BF16)
                s_ref[at, sent + i, :, cols] = goes.astype(BF16)

        if following == 3 and isinstance(unit, int) and down <= unit < out:
            chunk = unit - down

            @pl.when(z != chunk)
            def _():
                for copy in down_send(chunk, unit):
                    copy.start()

        else:
            start(unit, following, axes)

    def total(unit, axes):
        finish(unit, 3, axes)
        _, piece = arrived(unit, 3, axes)
        return piece(0) * factor

    def place_unit(at, axes, first, lanes):
        count, weight = 16, {}
        for axis in axes:
            count //= 4 if axis == 2 else 2
            weight[axis] = count
        for far in range(4):

            @pl.loop(0, 4)
            def _(near, far=far):
                index = weight[2] * far
                for axis, value in enumerate((near % 2, near // 2)):
                    index = index + weight[axis] * differs(value, bits[axis])
                top = per * (2 * (4 * far + near))
                sent = pl.multiple_of(top + per * (1 - core), 8)
                kept = pl.multiple_of(top + per * core, 8)
                cols = pl.ds(first, lanes)
                s_ref[at, index, :, cols] = tile_ref[pl.ds(sent, per), cols].astype(BF16)
                k_ref[at, index, :, cols] = tile_ref[pl.ds(kept, per), cols].astype(BF16)

    def place_down(at, axes):
        a, b, _ = axes
        block = steps * per

        @pl.loop(0, 4)
        def _(near):
            value = (near % 2, near // 2)
            index = 8 * differs(value[a], bits[a]) + 4 * differs(value[b], bits[b])
            for part in range(steps):
                sent = pl.multiple_of(block * (2 * near + 1 - core) + part * per, 8)
                kept = pl.multiple_of(block * (2 * near + core) + part * per, 8)
                s_ref[at, index + part] = tile_ref[pl.ds(sent, per), :].astype(BF16)
                k_ref[at, index + part] = tile_ref[pl.ds(kept, per), :].astype(BF16)

    def vector_copy(late, n):
        ref, recv = (vl_ref, vlrecv_ref) if late else (ve_ref, verecv_ref)
        if late:
            target = ([partner_core, partner_x, partner_y, partner_xy] + along_z)[n]
        else:
            target = ([partner_core, partner_x, partner_y] + along_z)[n]
        return pltpu.make_async_remote_copy(
            src_ref=ref,
            dst_ref=recv.at[n],
            send_sem=v_send_sem.at[late, n],
            recv_sem=v_recv_sem.at[late, n],
            device_id=target,
            device_id_type=mesh_ids,
        )

    STEPS = (((0,), (1,), (2,), (3, 4, 5)), ((0,), (1, 2, 3), (4, 5, 6)))

    def vector_step(late, n):
        ref, recv = (vl_ref, vlrecv_ref) if late else (ve_ref, verecv_ref)
        if n:
            for i in STEPS[late][n - 1]:
                vector_copy(late, i).wait()
            for i in STEPS[late][n - 1]:
                ref[...] += recv[i]
        if n < len(STEPS[late]):
            for i in STEPS[late][n]:
                vector_copy(late, i).start()

    orders, in_chunk, after_mlp, in_pair, after_proj, tail = plan

    def run(events):
        for unit, stage in events:
            if unit == "give":
                for copy in give(*((layer_out_ref, 0), (in_grad_ref, 1))[stage]):
                    copy.start()
            elif unit == "early":
                vector_step(0, stage)
            elif unit == "late":
                vector_step(1, stage)
            else:
                advance(unit, stage, orders[unit])

    load(1).wait()
    middle = x_ref[...].astype(F32) + dot(ctx_ref[...], wo_ref[...]) + par_ref[0:1, :]
    mid_ref[...] = middle
    unit_mid, _ = normalize(middle)
    n2_ref[...] = (unit_mid * par_ref[1:2, :] + par_ref[2:3, :]).astype(BF16)
    acc_ref[...] = middle + par_ref[3:4, :]
    dn_ref[...] = jnp.zeros_like(dn_ref)
    vl_ref[...] = jnp.zeros_like(vl_ref)
    load(2).wait()
    rows_copy(1).wait()

    def chunk_events(j, where):
        for n in range(steps):
            if in_chunk[n][where]:

                @pl.when(j == n)
                def _(n=n):
                    run(in_chunk[n][where])

    @pl.loop(0, steps)
    def _(j):
        slot = j % 2
        for copy in weights(j, slot):
            copy.wait()

        @pl.when(j + 1 < steps)
        def _():
            for copy in weights(j + 1, 1 - slot):
                copy.start()

        normed = n2_ref[...]
        grad_low = g_ref[...]
        wu, wd = w_ref.at[slot], w_ref.at[2 + slot]
        pre = dot(normed, wu[...]) + par_ref[pl.ds(8 + j, 1), :]
        phi = 0.5 * (1.0 + lax.erf(pre * math.sqrt(0.5)))
        hidden = (pre * phi).astype(BF16)
        slope = phi + pre * (jnp.exp(-0.5 * pre * pre) * (1.0 / math.sqrt(2 * math.pi)))
        chunk_events(j, 0)
        acc_ref[...] += dot(hidden, wd[...])
        tile_ref[...] = dot(hidden, grad_low, 0, 0)
        place_down(down + j, orders[down])
        start(down + j, 0, orders[down])
        grad_pre = dot(grad_low, wd[...], 1, 1) * slope
        ve_ref[pl.ds(4 + j, 1), :] = column_sum(grad_pre)
        gpre_low = grad_pre.astype(BF16)
        chunk_events(j, 1)
        tile_ref[...] = dot(normed, gpre_low, 0, 0)
        place_unit(up + j, orders[up], 0, width)
        start(up + j, 0, orders[up])
        dn_ref[...] += dot(gpre_low, wu[...], 1, 1)
        chunk_events(j, 2)

    for i in range(3):
        proj_weights(i).start()
    res_ref[0] = acc_ref[...].astype(BF16)

    def give(ref, n):
        mine_copy = pltpu.make_async_copy(res_ref.at[n, pl.ds(0, half)], ref.at[mine], io_sem.at[n])
        other_copy = pltpu.make_async_remote_copy(
            src_ref=res_ref.at[n, pl.ds(half, half)],
            dst_ref=ref.at[mine],
            send_sem=io_send_sem.at[n],
            recv_sem=io_recv_sem.at[n],
            device_id=partner_x,
            device_id_type=mesh_ids,
        )
        return mine_copy, other_copy

    unit_mid, scale = normalize(mid_ref[...])
    dn = dn_ref[...]
    grad = g_ref[...].astype(F32)
    gmid = grad + normalize_back(unit_mid, scale, par_ref[1:2, :], dn)
    ve_ref[0:1, :] = column_sum(gmid)
    ve_ref[1:2, :] = column_sum(dn * unit_mid)
    ve_ref[2:3, :] = column_sum(dn)
    ve_ref[3:4, :] = column_sum(grad)
    acc_ref[...] = gmid
    low = gmid.astype(BF16)
    tile_ref[...] = dot(ctx_ref[...], low, 0, 0)
    place_unit(out, orders[out], 0, width)
    start(out, 0, orders[out])
    gctx_ref[...] = dot(low, wo_ref[...], 1, 1).astype(BF16)
    dn_ref[...] = jnp.zeros_like(dn_ref)
    run(after_mlp)

    third = 2 * pair_width

    def exchange(p):
        return pltpu.make_async_remote_copy(
            src_ref=dsend_ref.at[p % 3],
            dst_ref=drecv_ref.at[p],
            send_sem=dk_send_sem.at[p],
            recv_sem=dk_recv_sem.at[p],
            device_id=partner_core,
            device_id_type=mesh_ids,
        )

    def project(pairs, unit):
        at, first, lanes = buffer(unit)
        span = len(pairs) * pair_width
        for i, p in enumerate(pairs):
            exchange(p).wait()
            lane = slice(p * pair_width, (p + 1) * pair_width)
            here = slice(i * pair_width, (i + 1) * pair_width)
            for n in range(2):
                grad = down_ref[p % 3, n] + drecv_ref[p, n].astype(F32)
                if n == 1:
                    vl_ref[3:4, lane] = column_sum(grad)
                dg_ref[1 + n, :, here] = grad.astype(BF16)
            dg_ref[0, :, here] = dq_of(p)
        cols = slice(pairs[0] * pair_width, pairs[0] * pair_width + span)
        for n in range(3):
            tile_ref[:, first + n * span : first + (n + 1) * span] = dot(n1_ref[...], dg_ref[n, :, :span], 0, 0)
        place_unit(at, orders[unit], first, lanes)
        start(unit, 0, orders[unit])
        more = dot(dg_ref[0, :, :span], w_ref[0, :, cols], 1, 1)
        for n in range(1, 3):
            more = more + dot(dg_ref[n, :, :span], w_ref[n, :, cols], 1, 1)
        dn_ref[...] += more

    def dq_of(p):
        return dg_ref[3, :, (p % 3) * pair_width : (p % 3 + 1) * pair_width]

    def attention_pair(p, slot, third_slot, between):
        attention_load(p, slot).wait()
        lanes = pl.ds(pl.multiple_of(p * pair_width, pair_width), pair_width)
        keys = jnp.concatenate([kv_ref[0, :, lanes], kvo_ref[0, :, lanes]], axis=0)
        values = jnp.concatenate([kv_ref[1, :, lanes], kvo_ref[1, :, lanes]], axis=0)
        queries = q_ref[:, lanes]
        gctx = gctx_ref[:, lanes]
        dq, dk, dv = [], [], []
        for head, grad in enumerate(halves(gctx)):
            att = att_ref[slot, head]
            wide = att.astype(F32)
            datt = dot(grad, values, 1, 1)
            inner = jnp.sum(wide * datt, axis=-1, keepdims=True)
            dscore = (wide * (datt - inner)).astype(BF16)
            dq.append(dot(dscore, keys))
            dk.append(dot(dscore, queries, 0, 0))
            dv.append(dot(att, gctx, 0, 0))
            if head == 0:
                between()
        dquery = join(*dq) * 0.125
        dg_ref[3, :, pl.ds(pl.multiple_of(third_slot * pair_width, pair_width), pair_width)] = dquery.astype(BF16)
        vl_ref[2:3, lanes] = column_sum(dquery)
        for n, grad in enumerate((join(*dk), join(*dv))):
            down_ref[third_slot, n] = grad[:rows]
            dsend_ref[third_slot, n] = grad[rows:].astype(BF16)
        exchange(p).start()

    def pairs_loop(first, count):
        def pair_events(i, where):
            for n in range(count):
                if in_pair[first + n][where]:

                    @pl.when(i == n)
                    def _(n=n):
                        run(in_pair[first + n][where])

        @pl.loop(0, count)
        def _(i):
            p = first + i
            attention_pair(p, p % 2, p % 3, lambda: pair_events(i, 0))

            @pl.when(p + 2 < HEADS // 2)
            def _():
                attention_load(p + 2, p % 2).start()

            pair_events(i, 1)

    pairs_loop(0, 3)
    for i in range(3):
        proj_weights(i).wait()
    project((0, 1), qkv)
    run(after_proj[0])
    pairs_loop(3, 2)
    project((2, 3), qkv + 1)
    run(after_proj[1])
    pairs_loop(5, 1)
    project((4,), last - 1)
    run(after_proj[2])
    project((5,), last)
    run(after_proj[3])

    unit_in, scale = normalize(x_ref[...].astype(F32))
    dn = dn_ref[...]
    res_ref[1] = (acc_ref[...] + normalize_back(unit_in, scale, par_ref[4:5, :], dn)).astype(BF16)
    vl_ref[0:1, :] = column_sum(dn * unit_in)
    vl_ref[1:2, :] = column_sum(dn)
    vector_step(1, 0)
    run(tail)

    me = dp * lax.axis_size("seq") + seq
    both = jnp.concatenate([ve_ref[...], vl_ref[...]], axis=0) * factor
    turned = pltpu.roll(both, (width - me * per) % width, 1)
    small_ref[...] = turned[:, : small_ref.shape[1]]
    per_up = steps * per
    row = (me * per_up) // width
    up_bias = jnp.broadcast_to(ve_ref[pl.ds(4 + row, 1), :] * factor, (8, width))
    shift = (width - (me * per_up - row * width)) % width
    upb_ref[...] = pltpu.roll(up_bias, shift, 1)[:, : upb_ref.shape[1]]

    for j in range(steps):
        dup_ref[:, j * width : (j + 1) * width] = total(up + j, orders[up])
    for j in range(steps):

        @pl.when(z == j)
        def _(j=j):
            for i in range(3):
                remote(down + j, 4 + i, rz_ref.at[i], rz_ref.at[i], along_z[i]).wait_recv()
            for part in range(steps):
                value = k_ref[down + j, part].astype(F32)
                for i in range(3):
                    value = value + rz_ref[i, part].astype(F32)
                ddown_ref[part * per : (part + 1) * per, :] = value * factor

        @pl.when(z != j)
        def _(j=j):
            for copy in down_send(j, down + j):
                copy.wait_send()

    dout_ref[...] = total(out, orders[out])
    for pairs, unit in (((0, 1), qkv), ((2, 3), qkv + 1), ((4,), last - 1), ((5,), last)):
        value = total(unit, orders[unit])
        span = len(pairs) * pair_width
        for n in range(3):
            at = n * width + pairs[0] * pair_width
            dqkv_ref[:, at : at + span] = value[:, n * span : (n + 1) * span]
    for n, ref in enumerate((layer_out_ref, in_grad_ref)):
        for copy in give(ref, n):
            copy.wait()

def results_kernel(info_ref, small_ref, upb_ref, *refs):
    count = (len(refs) - 9) // 2
    big_in, outs = refs[:count], refs[count:]
    for i in range(count):
        outs[i][...] = big_in[i][...]
    vectors = outs[count:]
    for i, row in enumerate((8, 9, 10, 11, 0, 1, 2, 3)):
        vectors[i][...] = small_ref[row : row + 1, : vectors[i].shape[1]]
    vectors[8][...] = upb_ref[0:1, : vectors[8].shape[1]]


PLAN = (((0, 2, 1), (0, 2, 1), (0, 2, 1), (0, 2, 1), (1, 0, 2), (1, 0, 2), (1, 0, 2), (1, 0, 2), (1, 0, 2), (1, 0, 2), (1, 0, 2), (0, 1, 2), (0, 1, 2)), (((), (), ()), (((4, 0), (0, 0)), (), ()), (((5, 0), (1, 0)), ((4, 1), (0, 1)), ((6, 0),)), (((2, 0),), ((5, 1), (1, 1)), ((0, 2), (7, 0)))), (('early', 0), (4, 2), (3, 0), (6, 1), (8, 0)), (((('early', 1), (1, 2)), ((2, 1),)), ((), ((5, 2), ('give', 0))), (((7, 1),), ()), (((8, 1), (9, 0)), ((2, 2), (6, 2), ('early', 2))), ((), ()), ((('early', 3), (10, 0)), ())), (((3, 1),), ((9, 1),), ((7, 2), (3, 2)), ((11, 0), ('early', 4), (8, 2))), ((12, 0), (10, 1), (9, 2), ('late', 1), ('give', 1), (11, 1), (12, 1), (11, 2), (10, 2), ('late', 2), ('late', 3)))


def on_device(
    layer_in,
    out_grad,
    pre_gain,
    pre_bias,
    qkv_w,
    q_bias,
    v_bias,
    out_w,
    out_b,
    mid_gain,
    mid_bias,
    up_w,
    up_b,
    down_w,
    down_b,
    patch_keep,
    text_len,
):
    seq_here, half, width = layer_in.shape
    dp, seq = lax.axis_size("dp"), lax.axis_size("seq")
    assert seq_here == 2 and seq == 4
    full = half * seq
    rows = 2 * half
    ff = up_w.shape[1]
    steps = ff // width
    devices = dp * seq
    place_seq = lax.axis_index("seq")
    me = lax.axis_index("dp") * seq + place_seq
    mine, core = place_seq // 2, place_seq % 2

    bits = devices.bit_length() - 1
    halving = (dp, seq) == (8, 4) and width % (8 * devices) == 0
    if halving:
        shards, at_me, at_core = devices, me, core
        dp_bits = list(range(2, bits))
        order_x = [1] + dp_bits
        order_y = dp_bits[:1] + [1] + dp_bits[1:]
        order_z = dp_bits[1:] + [1] + dp_bits[:1]
    else:
        shards, at_me, at_core = 32, 0, 0
        order_x = order_y = order_z = [4, 3, 2, 1]
    per = width // shards
    per_down = ff // shards
    pairs = shards // 2
    info = jnp.stack(
        [
            jnp.asarray(v, jnp.int32)
            for v in (
                mine,
                at_core,
                place(at_me >> 1, order_x),
                place(at_me >> 1, order_y),
                place(at_me >> 1, order_z),
                me,
            )
        ]
    )

    def swap(value, bit):
        if bit < 2:
            return lax.ppermute(value, "seq", [(i, i ^ (1 << bit)) for i in range(seq)])
        return lax.ppermute(value, "dp", [(i, i ^ (1 << (bit - 2))) for i in range(dp)])

    row = lambda v: v.reshape(-1, width)
    own_rows = pl.BlockSpec((1, half, width), lambda i, info: (info[0], 0, 0))
    vec = fixed((1, width))
    act = fixed((rows, width))

    factor = 1.0 / math.sqrt(seq_here * full * dp)
    per_vec, per_up = width // devices, ff // devices
    if halving:
        hbm = pl.BlockSpec(memory_space=pl.ANY)
        units = 2 * steps + 4
        big = lambda *shape: pltpu.VMEM(shape, F32)
        low = lambda *shape: pltpu.VMEM(shape, BF16)
        dma = lambda *shape: pltpu.SemaphoreType.DMA(shape)
        operands = (layer_in, out_grad, qkv_w, out_w, up_w, down_w)
        vectors = (out_b, mid_gain, mid_bias, down_b, pre_gain, pre_bias, q_bias, v_bias, up_b, patch_keep)
        results = [(per, ff), (per_down, width), (per, width), (per, 3 * width), (16, 128), (8, 128)]
        *large, small, up_bias, _ = pl.pallas_call(
            functools.partial(back_kernel, factor, PLAN),
            in_specs=[hbm] * len(operands)
            + [fixed(v.shape) for v in vectors]
            + [pl.BlockSpec(memory_space=pltpu.SMEM)],
            out_shape=[shape_of(layer_in.shape, BF16)] * 2 + [shape_of(s, F32) for s in results]
            + [shape_of((HEADS, rows, full), BF16)],
            out_specs=[hbm] * 2 + [fixed(s) for s in results] + [hbm],
            scratch_shapes=[
                big(16, width),
                big(8, pl.cdiv(full, 128) * 128),
                low(rows, width),
                low(rows, width),
                low(rows, width),
                low(rows, width),
                low(rows, width),
                low(2, rows, width),
                low(2, rows, width),
                low(2, 2, rows, full),
                low(width, width),
                low(4, width, width),
                big(rows, width),
                big(rows, width),
                big(rows, width),
                low(rows, width),
                big(width, width),
                low(rows, width),
                low(4, rows, 6 * HEAD_DIM),
                big(3, 2, rows, 2 * HEAD_DIM),
                low(3, 2, rows, 2 * HEAD_DIM),
                low(6, 2, rows, 2 * HEAD_DIM),
                low(2, rows, width),
                big(8, width),
                big(8, width),
                big(6, 8, width),
                big(7, 8, width),
                low(units, 16, per, width),
                low(units, 16, per, width),
                low(units, 16, per, width),
                low(units, 16, per, width),
                low(3, steps, per, width),
                dma(3),
                dma(7),
                dma(4),
                dma(units + 1, 7),
                dma(units + 1, 7),
                dma(6),
                dma(6),
                dma(2, 7),
                dma(2, 7),
                dma(2),
                dma(2),
                dma(2),
                dma(2),
                dma(2),
                dma(2),
                dma(2),
            ],
            compiler_params=pltpu.CompilerParams(
                vmem_limit_bytes=64 * 1024 * 1024, collective_id=0, has_side_effects=True
            ),
        )(*operands, *vectors, text_len)
        vec_shapes = [(1, per_vec)] * 8 + [(1, per_up)]
        whole = call(
            results_kernel,
            (1,),
            [fixed((16, 128)), fixed((8, 128))] + [fixed(v.shape) for v in large],
            [shape_of(v.shape, v.dtype) for v in large] + [shape_of(s, F32) for s in vec_shapes],
            [fixed(v.shape) for v in large] + [fixed(s) for s in vec_shapes],
        )(info, small, up_bias, *large)
        layer_out, in_grad, d_wup, d_wdown, d_wout, d_qkv = whole[:6]
        d_pregain, d_prebias, d_qbias, d_vbias, d_outbias, d_midgain, d_midbias, d_downbias, d_upbias = (
            v.reshape(-1) for v in whole[6:]
        )
        return (
            layer_out,
            in_grad,
            d_pregain,
            d_prebias,
            d_qkv,
            d_qbias,
            d_vbias,
            d_wout,
            d_outbias,
            d_midgain,
            d_midbias,
            d_wup,
            d_upbias,
            d_wdown,
            d_downbias,
        )

    x_other = swap(lax.dynamic_index_in_dim(layer_in, 1 - mine, 0, False), 1)
    g_other = swap(lax.dynamic_index_in_dim(out_grad, 1 - mine, 0, False), 1)

    patches = lax.dynamic_index_in_dim(patch_keep, mine, 0, False)
    length = lax.dynamic_index_in_dim(text_len, mine, 0, False)
    valid = jnp.concatenate(
        [
            jnp.ones((2,), jnp.int32),
            patches,
            jnp.ones((1,), jnp.int32),
            (jnp.arange(TEXT, dtype=jnp.int32) < length).astype(jnp.int32),
            jnp.zeros((full - 3 - PATCHES - TEXT,), jnp.int32),
        ]
    )
    valid = valid.reshape(seq, half)
    valid = jnp.concatenate(
        [lax.dynamic_index_in_dim(valid, place_seq ^ turn, 0, True) for turn in (0, 2, 1, 3)], axis=1
    )
    mask = jnp.where(valid > 0, 0.0, -1e30).astype(F32)

    square = 2 * rows * width * width
    kv_bias = jnp.concatenate([jnp.zeros((1, 1, width), F32), v_bias.reshape(1, 1, width)], axis=0)
    n1, kv = call(
        qkv_kernel,
        (2,),
        [
            own_rows,
            fixed((half, width)),
            vec,
            vec,
            pl.BlockSpec((width, width), lambda i, _: (0, i + 1)),
            pl.BlockSpec((1, 1, width), lambda i, _: (i, 0, 0)),
        ],
        [shape_of((rows, width), BF16), shape_of((2, rows, width), BF16)],
        [act, pl.BlockSpec((1, rows, width), lambda i, _: (i, 0, 0))],
        flops=2 * square,
        nbytes=5 * 10**6,
    )(info, layer_in, x_other, row(pre_gain), row(pre_bias), qkv_w, kv_bias)
    kv_other = swap(kv, 0)
    q = call(
        query_kernel,
        (1,),
        [act, pl.BlockSpec((width, width), lambda i, _: (0, 0)), vec],
        shape_of((rows, width), BF16),
        act,
        flops=square,
        nbytes=3 * 10**6,
    )(info, n1, qkv_w, row(q_bias))

    pair_width = 2 * HEAD_DIM
    blocks = width // pair_width
    col = pl.BlockSpec((rows, pair_width), lambda i, _: (0, i))
    col2 = pl.BlockSpec((2, rows, pair_width), lambda i, _: (0, 0, i))
    att_spec = pl.BlockSpec((2, rows, full), lambda i, _: (i, 0, 0))
    head_flops = 2 * rows * full * pair_width * HEADS
    ctx, att = call(
        attention_kernel,
        (blocks,),
        [col, col2, col2, fixed((1, full))],
        [shape_of((rows, width), BF16), shape_of((HEADS, rows, full), BF16)],
        [col, att_spec],
        flops=4 * head_flops,
        nbytes=12 * 10**6,
        trans=HEADS * rows * full,
    )(info, q, kv, kv_other, mask)

    orders = (order_x, order_y, order_z)
    mlp_out = call(
        functools.partial(mlp_kernel, orders, per, per_down, steps),
        (steps,),
        [
            own_rows,
            fixed((half, width)),
            own_rows,
            fixed((half, width)),
            act,
            fixed((width, width)),
            vec,
            vec,
            vec,
            pl.BlockSpec((width, width), lambda i, _: (0, i)),
            pl.BlockSpec((1, 1, width), lambda i, _: (i, 0, 0)),
            pl.BlockSpec((width, width), lambda i, _: (i, 0)),
            vec,
        ],
        [
            shape_of((half, width), BF16),
            shape_of((half, width), BF16),
            shape_of((rows, width), F32),
            shape_of((rows, width), BF16),
            shape_of((4 + steps, width), F32),
            shape_of((pairs, steps, per, width), BF16),
            shape_of((pairs, steps, per, width), F32),
            shape_of((pairs, per_down, width), BF16),
            shape_of((pairs, per_down, width), F32),
            shape_of((pairs, per, width), BF16),
            shape_of((pairs, per, width), F32),
        ],
        [
            fixed((half, width)),
            fixed((half, width)),
            act,
            act,
            fixed((4 + steps, width)),
            pl.BlockSpec((pairs, 1, per, width), lambda i, _: (0, i, 0, 0)),
            pl.BlockSpec((pairs, 1, per, width), lambda i, _: (0, i, 0, 0)),
            fixed((pairs, per_down, width)),
            fixed((pairs, per_down, width)),
            fixed((pairs, per, width)),
            fixed((pairs, per, width)),
        ],
        scratch=[
            pltpu.VMEM((rows, width), F32),
            pltpu.VMEM((rows, width), BF16),
            pltpu.VMEM((rows, width), F32),
            pltpu.VMEM((rows, width), F32),
            pltpu.VMEM((width, width), F32),
        ],
        flops=(6 * steps + 3) * square,
        nbytes=40 * 10**6,
        trans=2 * rows * ff,
    )(
        info,
        layer_in,
        x_other,
        out_grad,
        g_other,
        ctx,
        out_w,
        row(out_b),
        row(mid_gain),
        row(mid_bias),
        up_w,
        up_b.reshape(steps, 1, width),
        down_w,
        row(down_b),
    )
    out_own, out_other, gmid, gctx, early, s_up, k_up, s_down, k_down, s_out, k_out = mlp_out
    out_back = swap(out_other, 1)

    def reduce(sent, kept, order):
        got = swap(sent, 0)
        for bit in order:
            total = kept + got.astype(F32)
            cut = total.shape[0] // 2
            kept = total[:cut]
            got = swap(total[cut:].astype(BF16), bit)
        return kept, got

    def natural(sent, kept):
        return jnp.stack([kept, sent.astype(F32)], axis=1)

    if halving:
        up_pair = reduce(s_up, k_up, order_x)
        down_pair = reduce(s_down, k_down, order_y)
        out_pair = reduce(s_out, k_out, order_z)

    dq, dbq, dkv_own, dkv_send = call(
        attention_back_kernel,
        (blocks,),
        [att_spec, col, col2, col2, col],
        [
            shape_of((rows, width), BF16),
            shape_of((1, width), F32),
            shape_of((2, rows, width), F32),
            shape_of((2, rows, width), BF16),
        ],
        [col, pl.BlockSpec((1, pair_width), lambda i, _: (0, i)), col2, col2],
        flops=8 * head_flops,
        nbytes=16 * 10**6,
    )(info, att, q, kv, kv_other, gctx)
    dkv_other = swap(dkv_send, 0)
    shard = fixed((pairs, per, width))
    tile = pltpu.VMEM((width, width), F32)
    dn_q, s_q, k_q = call(
        functools.partial(query_back_kernel, order_x, per),
        (1,),
        [act, act, pl.BlockSpec((width, width), lambda i, _: (0, 0))],
        [shape_of((rows, width), F32), shape_of((pairs, per, width), BF16), shape_of((pairs, per, width), F32)],
        [act, shard, shard],
        scratch=[tile],
        flops=2 * square,
        nbytes=6 * 10**6,
    )(info, n1, dq, qkv_w)
    dkv, dbv, s_k, k_k, s_v, k_v = call(
        functools.partial(key_value_back_kernel, (order_x, order_y), per),
        (1,),
        [act, fixed((2, rows, width)), fixed((2, rows, width))],
        [
            shape_of((2, rows, width), BF16),
            shape_of((1, width), F32),
            shape_of((pairs, per, width), BF16),
            shape_of((pairs, per, width), F32),
            shape_of((pairs, per, width), BF16),
            shape_of((pairs, per, width), F32),
        ],
        [fixed((2, rows, width)), vec, shard, shard, shard, shard],
        scratch=[tile],
        flops=2 * square,
        nbytes=10 * 10**6,
    )(info, n1, dkv_own, dkv_other)
    if halving:
        q_pair = reduce(s_q, k_q, order_x)
        k_pair = reduce(s_k, k_k, order_x)
        v_pair = reduce(s_v, k_v, order_y)
    in_own, in_other, late = call(
        input_back_kernel,
        (1,),
        [
            own_rows,
            fixed((half, width)),
            vec,
            fixed((2, rows, width)),
            fixed((width, 3 * width)),
            act,
            act,
            vec,
            vec,
        ],
        [shape_of((half, width), BF16), shape_of((half, width), BF16), shape_of((8, width), F32)],
        [fixed((half, width)), fixed((half, width)), fixed((8, width))],
        flops=2 * square,
        nbytes=10 * 10**6,
    )(info, layer_in, x_other, row(pre_gain), dkv, qkv_w, dn_q, gmid, dbq, dbv)
    in_back = swap(in_other, 1)

    def give_back(own, other):
        first = jnp.where(mine == 0, own, other)
        second = jnp.where(mine == 0, other, own)
        return jnp.stack([first, second])

    layer_out = give_back(out_own, out_back)
    in_grad = give_back(in_own, in_back)

    factor = 1.0 / math.sqrt(seq_here * full * dp)
    vectors = jnp.concatenate([early, late], axis=0)
    if halving:
        for bit in range(bits):
            vectors = vectors + swap(vectors, bit)
    else:
        vectors = lax.psum(vectors, ("dp", "seq"))
    per_vec, per_up = width // devices, ff // devices
    early_rows = 4 + steps
    small, up_bias = call(
        functools.partial(vector_kernel, factor, per_vec, per_up),
        (1,),
        [
            pl.BlockSpec((early_rows, width), lambda i, _: (0, 0)),
            pl.BlockSpec((8, width), lambda i, _: (early_rows // 8, 0)),
        ],
        [shape_of((early_rows + 8, 128), F32), shape_of((8, 128), F32)],
        [fixed((early_rows + 8, 128)), fixed((8, 128))],
    )(info, vectors, vectors)
    pick = lambda i: small[i, :per_vec]
    d_upbias = up_bias[0, :per_up]
    d_outbias, d_midgain, d_midbias, d_downbias = (pick(i) for i in range(4))
    d_pregain, d_prebias, d_qbias, d_vbias = (pick(early_rows + i) for i in range(4))

    if halving:

        def finish(named):
            operands = [v for pair, _ in named for v in pair]
            shapes = [s for _, s in named]
            return call(
                functools.partial(finish_kernel, factor),
                (1,),
                [fixed(v.shape) for v in operands],
                [shape_of(s, F32) for s in shapes],
                [fixed(s) for s in shapes],
            )(info, *operands)

        d_wup, d_wdown, d_wout = finish(
            [(up_pair, (per, ff)), (down_pair, (per_down, width)), (out_pair, (per, width))]
        )
        d_q, d_k, d_v = finish([(pair, (per, width)) for pair in (q_pair, k_pair, v_pair)])
        d_qkv = jnp.concatenate([d_q, d_k, d_v], axis=1)
    else:

        def scatter(value):
            return lax.psum_scatter(value, ("dp", "seq"), scatter_dimension=0, tiled=True) * factor

        d_wup = scatter(
            natural(s_up, k_up).transpose(0, 1, 3, 2, 4).reshape(width, ff)
        )
        d_wdown = scatter(natural(s_down, k_down).reshape(ff, width))
        d_wout = scatter(natural(s_out, k_out).reshape(width, width))
        d_qkv = scatter(
            jnp.concatenate(
                [natural(s, k).reshape(width, width) for s, k in ((s_q, k_q), (s_k, k_k), (s_v, k_v))],
                axis=1,
            )
        )
    return (
        layer_out,
        in_grad,
        d_pregain,
        d_prebias,
        d_qkv,
        d_qbias,
        d_vbias,
        d_wout,
        d_outbias,
        d_midgain,
        d_midbias,
        d_wup,
        d_upbias,
        d_wdown,
        d_downbias,
    )


def solution(mesh):
    both = ("dp", "seq")
    rows = P("dp", "seq", None)
    return jax.shard_map(
        on_device,
        mesh=mesh,
        in_specs=(rows, rows) + (P(),) * 13 + (P("dp", None), P("dp")),
        out_specs=(
            rows,
            rows,
            P(both),
            P(both),
            P(both, None),
            P(both),
            P(both),
            P(both, None),
            P(both),
            P(both),
            P(both),
            P(both, None),
            P(both),
            P(both, None),
            P(both),
        ),
        check_vma=False,
    )
```

```python
import functools
import math

import jax
import jax.numpy as jnp
from jax import lax
from jax.experimental import pallas as pl
from jax.experimental.pallas import tpu as pltpu
from jax.sharding import PartitionSpec as P

HEADS = 12
HEAD_DIM = 64
PATCHES = 196
TEXT = 512
F32 = jnp.float32
BF16 = jnp.bfloat16
VMEM_BYTES = 60 * 1024 * 1024


def dot(lhs, rhs, lhs_dim=1, rhs_dim=0):
    return lax.dot_general(
        lhs, rhs, (((lhs_dim,), (rhs_dim,)), ((), ())), preferred_element_type=F32
    )


def normalize(values):
    center = values - jnp.mean(values, axis=-1, keepdims=True)
    spread = jnp.mean(center * center, axis=-1, keepdims=True)
    scale = lax.rsqrt(spread + 1e-06)
    return center * scale, scale


def normalize_back(unit, scale, gain, cotangent):
    inner = cotangent * gain
    mean_inner = jnp.mean(inner, axis=-1, keepdims=True)
    mean_unit = jnp.mean(inner * unit, axis=-1, keepdims=True)
    return scale * (inner - mean_inner - unit * mean_unit)


def column_sum(values):
    return jnp.sum(values, axis=0, keepdims=True)


def call(kernel, grid, in_specs, out_shape, out_specs, scratch=(), flops=0, nbytes=0, trans=0):
    return pl.pallas_call(
        kernel,
        grid_spec=pltpu.PrefetchScalarGridSpec(
            num_scalar_prefetch=1,
            grid=grid,
            in_specs=in_specs,
            out_specs=out_specs,
            scratch_shapes=list(scratch),
        ),
        out_shape=out_shape,
        compiler_params=pltpu.CompilerParams(vmem_limit_bytes=VMEM_BYTES),
        cost_estimate=pl.CostEstimate(flops=flops, bytes_accessed=nbytes, transcendentals=trans),
    )


def fixed(shape):
    zeros = (0,) * len(shape)
    return pl.BlockSpec(shape, lambda *_: zeros)


def shape_of(shape, dtype):
    return jax.ShapeDtypeStruct(shape, dtype)


def place(number, order):
    out = 0
    for bit in order:
        out = out * 2 + ((number >> (bit - 1)) & 1)
    return out


def store_shards(tile_ref, send_ref, keep_ref, info_ref, slot, order, rows, pairs, at):
    core = info_ref[1]
    for pair in range(pairs):
        number = pair if at is None else at * pairs + pair
        index = place(number, order) ^ info_ref[slot]
        sent = tile_ref[pl.ds(pl.multiple_of(rows * (2 * pair + 1 - core), 8), rows), :]
        kept = tile_ref[pl.ds(pl.multiple_of(rows * (2 * pair + core), 8), rows), :]
        send_ref[index] = sent.astype(send_ref.dtype).reshape(send_ref.shape[1:])
        keep_ref[index] = kept.reshape(keep_ref.shape[1:])


def qkv_kernel(info_ref, own_ref, other_ref, gain_ref, shift_ref, w_ref, bias_ref, n1_ref, kv_ref):
    @pl.when(pl.program_id(0) == 0)
    def _():
        rows = jnp.concatenate([own_ref[0], other_ref[...]], axis=0).astype(F32)
        unit, _ = normalize(rows)
        n1_ref[...] = (unit * gain_ref[...] + shift_ref[...]).astype(BF16)

    kv_ref[0] = (dot(n1_ref[...], w_ref[...]) + bias_ref[0]).astype(BF16)


def query_kernel(info_ref, n1_ref, w_ref, bias_ref, q_ref):
    q_ref[...] = ((dot(n1_ref[...], w_ref[...]) + bias_ref[...]) * 0.125).astype(BF16)


def halves(value):
    lane = lax.broadcasted_iota(jnp.int32, value.shape, 1)
    zero = jnp.zeros_like(value)
    return jnp.where(lane < HEAD_DIM, value, zero), jnp.where(lane < HEAD_DIM, zero, value)


def join(first, second):
    lane = lax.broadcasted_iota(jnp.int32, first.shape, 1)
    return jnp.where(lane < HEAD_DIM, first, second)


def attention_kernel(info_ref, q_ref, own_ref, other_ref, mask_ref, ctx_ref, att_ref):
    keys = jnp.concatenate([own_ref[0], other_ref[0]], axis=0)
    values = jnp.concatenate([own_ref[1], other_ref[1]], axis=0)
    parts = []
    for head, query in enumerate(halves(q_ref[...])):
        scores = dot(query, keys, 1, 1) + mask_ref[...]
        exponent = jnp.exp(scores - jnp.max(scores, axis=-1, keepdims=True))
        total = jnp.sum(exponent, axis=-1, keepdims=True)
        att = (exponent * (1.0 / total)).astype(BF16)
        att_ref[head] = att
        parts.append(dot(att, values))
    ctx_ref[...] = join(*parts).astype(BF16)


def attention_back_kernel(
    info_ref, att_ref, q_ref, own_ref, other_ref, gctx_ref, dq_ref, dbq_ref, down_ref, dother_ref
):
    keys = jnp.concatenate([own_ref[0], other_ref[0]], axis=0)
    values = jnp.concatenate([own_ref[1], other_ref[1]], axis=0)
    queries = q_ref[...]
    gctx = gctx_ref[...]
    dq, dk, dv = [], [], []
    for head, grad in enumerate(halves(gctx)):
        att = att_ref[head]
        wide = att.astype(F32)
        datt = dot(grad, values, 1, 1)
        inner = jnp.sum(wide * datt, axis=-1, keepdims=True)
        dscore = (wide * (datt - inner)).astype(BF16)
        dq.append(dot(dscore, keys))
        dk.append(dot(dscore, queries, 0, 0))
        dv.append(dot(att, gctx, 0, 0))
    dquery = join(*dq) * 0.125
    dq_ref[...] = dquery.astype(BF16)
    dbq_ref[...] = column_sum(dquery)
    rows = queries.shape[0]
    for i, grad in enumerate((join(*dk), join(*dv))):
        down_ref[i] = grad[:rows]
        dother_ref[i] = grad[rows:].astype(BF16)


def mlp_kernel(
    orders,
    rows_up,
    rows_down,
    steps,
    info_ref,
    x_ref,
    xo_ref,
    g_ref,
    go_ref,
    ctx_ref,
    wo_ref,
    bo_ref,
    gain_ref,
    shift_ref,
    wu_ref,
    bu_ref,
    wd_ref,
    bd_ref,
    out_ref,
    outo_ref,
    gmid_ref,
    gctx_ref,
    vec_ref,
    su_ref,
    ku_ref,
    sd_ref,
    kd_ref,
    so_ref,
    ko_ref,
    mid_ref,
    n2_ref,
    acc_ref,
    dn_ref,
    tile_ref,
):
    step = pl.program_id(0)
    half = xo_ref.shape[0]
    grad_low = jnp.concatenate([g_ref[0], go_ref[...]], axis=0)

    @pl.when(step == 0)
    def _():
        rows = jnp.concatenate([x_ref[0], xo_ref[...]], axis=0).astype(F32)
        middle = rows + dot(ctx_ref[...], wo_ref[...]) + bo_ref[...]
        mid_ref[...] = middle
        unit, _ = normalize(middle)
        n2_ref[...] = (unit * gain_ref[...] + shift_ref[...]).astype(BF16)
        acc_ref[...] = middle + bd_ref[...]
        dn_ref[...] = jnp.zeros_like(dn_ref)

    normed = n2_ref[...]
    pre = dot(normed, wu_ref[...]) + bu_ref[0]
    phi = 0.5 * (1.0 + lax.erf(pre * math.sqrt(0.5)))
    hidden = (pre * phi).astype(BF16)
    slope = phi + pre * (jnp.exp(-0.5 * pre * pre) * (1.0 / math.sqrt(2 * math.pi)))
    acc_ref[...] += dot(hidden, wd_ref[...])
    grad_pre = dot(grad_low, wd_ref[...], 1, 1) * slope
    vec_ref[pl.ds(4 + step, 1), :] = column_sum(grad_pre)
    gpre_low = grad_pre.astype(BF16)
    dn_ref[...] += dot(gpre_low, wu_ref[...], 1, 1)
    tile_ref[...] = dot(normed, gpre_low, 0, 0)
    n_up = tile_ref.shape[0] // (2 * rows_up)
    store_shards(tile_ref, su_ref, ku_ref, info_ref, 2, orders[0], rows_up, n_up, None)
    tile_ref[...] = dot(hidden, grad_low, 0, 0)
    n_down = tile_ref.shape[0] // (2 * rows_down)
    for at in range(steps):

        @pl.when(step == at)
        def _(at=at):
            store_shards(tile_ref, sd_ref, kd_ref, info_ref, 3, orders[1], rows_down, n_down, at)

    @pl.when(step == steps - 1)
    def _():
        result = acc_ref[...].astype(BF16)
        out_ref[...] = result[:half]
        outo_ref[...] = result[half:]
        unit, scale = normalize(mid_ref[...])
        dn = dn_ref[...]
        grad = grad_low.astype(F32)
        gmid = grad + normalize_back(unit, scale, gain_ref[...], dn)
        gmid_ref[...] = gmid
        vec_ref[0:1, :] = column_sum(gmid)
        vec_ref[1:2, :] = column_sum(dn * unit)
        vec_ref[2:3, :] = column_sum(dn)
        vec_ref[3:4, :] = column_sum(grad)
        low = gmid.astype(BF16)
        gctx_ref[...] = dot(low, wo_ref[...], 1, 1).astype(BF16)
        tile_ref[...] = dot(ctx_ref[...], low, 0, 0)
        store_shards(tile_ref, so_ref, ko_ref, info_ref, 4, orders[2], rows_up, n_up, None)


def query_back_kernel(order, rows, info_ref, n1_ref, dq_ref, w_ref, dn_ref, s_ref, k_ref, tile_ref):
    tile_ref[...] = dot(n1_ref[...], dq_ref[...], 0, 0)
    pairs = tile_ref.shape[0] // (2 * rows)
    store_shards(tile_ref, s_ref, k_ref, info_ref, 2, order, rows, pairs, None)
    dn_ref[...] = dot(dq_ref[...], w_ref[...], 1, 1)


def key_value_back_kernel(
    orders, rows, info_ref, n1_ref, own_ref, other_ref, dkv_ref, dbv_ref, sk_ref, kk_ref, sv_ref, kv_ref, tile_ref
):
    pairs = tile_ref.shape[0] // (2 * rows)
    for i, (s_ref, k_ref, slot) in enumerate(((sk_ref, kk_ref, 2), (sv_ref, kv_ref, 3))):
        grad = own_ref[i] + other_ref[i].astype(F32)
        low = grad.astype(BF16)
        dkv_ref[i] = low
        if i == 1:
            dbv_ref[...] = column_sum(grad)
        tile_ref[...] = dot(n1_ref[...], low, 0, 0)
        store_shards(tile_ref, s_ref, k_ref, info_ref, slot, orders[i], rows, pairs, None)


def input_back_kernel(
    info_ref, x_ref, xo_ref, gain_ref, dkv_ref, w_ref, dnq_ref, gmid_ref, dbq_ref, dbv_ref, own_ref, other_ref, vec_ref
):
    half = xo_ref.shape[0]
    dn = dnq_ref[...]
    for i in range(2):
        width = dn.shape[1]
        dn = dn + dot(dkv_ref[i], w_ref[:, (i + 1) * width : (i + 2) * width], 1, 1)
    rows = jnp.concatenate([x_ref[0], xo_ref[...]], axis=0).astype(F32)
    unit, scale = normalize(rows)
    result = (gmid_ref[...] + normalize_back(unit, scale, gain_ref[...], dn)).astype(BF16)
    own_ref[...] = result[:half]
    other_ref[...] = result[half:]
    vec_ref[0:1, :] = column_sum(dn * unit)
    vec_ref[1:2, :] = column_sum(dn)
    vec_ref[2:3, :] = dbq_ref[...]
    vec_ref[3:4, :] = dbv_ref[...]
    vec_ref[4:8, :] = jnp.zeros_like(vec_ref[4:8, :])


def finish_kernel(factor, info_ref, *refs):
    count = len(refs) // 3
    for i in range(count):
        keep, recv, out = refs[2 * i], refs[2 * i + 1], refs[2 * count + i]
        total = (keep[0] + recv[0].astype(F32)) * factor
        if total.ndim == 3:
            width = total.shape[-1]
            for block in range(total.shape[0]):
                out[:, block * width : (block + 1) * width] = total[block]
        else:
            out[...] = total


def vector_kernel(factor, per, per_up, info_ref, early_ref, late_ref, out_ref, up_ref):
    me = info_ref[5]
    width = early_ref.shape[1]
    both = jnp.concatenate([early_ref[...], late_ref[...]], axis=0) * factor
    turned = pltpu.roll(both, lax.rem(width - me * per, width), 1)
    out_ref[...] = turned[:, : out_ref.shape[1]]
    row = (me * per_up) // width
    up = early_ref[pl.ds(4 + row, 1), :] * factor
    up = jnp.broadcast_to(up, (8, width))
    shift = lax.rem(width - (me * per_up - row * width), width)
    up_ref[...] = pltpu.roll(up, shift, 1)[:, : up_ref.shape[1]]


SEND_AT = (0, 8, 0, 8)
LAND_AT = (None, 0, 8, 12)


def differs(bit, mine):
    return bit + mine - 2 * bit * mine


def back_kernel(
    factor,
    plan,
    layer_in_ref,
    out_grad_ref,
    qkv_w_ref,
    out_w_ref,
    up_w_ref,
    down_w_ref,
    out_b_ref,
    mid_gain_ref,
    mid_bias_ref,
    down_b_ref,
    pre_gain_ref,
    pre_bias_ref,
    q_bias_ref,
    v_bias_ref,
    up_b_ref,
    patch_ref,
    length_ref,
    layer_out_ref,
    in_grad_ref,
    dup_ref,
    ddown_ref,
    dout_ref,
    dqkv_ref,
    small_ref,
    upb_ref,
    att_hbm_ref,
    par_ref,
    mask_ref,
    x_ref,
    g_ref,
    ctx_ref,
    n1_ref,
    q_ref,
    kv_ref,
    kvo_ref,
    att_ref,
    wo_ref,
    w_ref,
    mid_ref,
    acc_ref,
    dn_ref,
    n2_ref,
    gctx_ref,
    dg_ref,
    down_ref,
    dsend_ref,
    drecv_ref,
    res_ref,
    ve_ref,
    vl_ref,
    verecv_ref,
    vlrecv_ref,
    u_ref,
    r0_ref,
    r_ref,
    uh_ref,
    r0h_ref,
    rh_ref,
    rz_ref,
    in_sem,
    w_sem,
    att_sem,
    send_sem,
    recv_sem,
    dk_send_sem,
    dk_recv_sem,
    v_send_sem,
    v_recv_sem,
    io_sem,
    io_send_sem,
    io_recv_sem,
    x_send_sem,
    x_recv_sem,
    kv_send_sem,
    kv_recv_sem,
):
    _, half, width = layer_in_ref.shape
    rows = 2 * half
    steps = up_w_ref.shape[1] // width
    dp, seq = lax.axis_index("dp"), lax.axis_index("seq")
    core, mine = seq % 2, seq // 2
    y, z = dp % 2, dp // 2
    bits = (mine, y)
    partner_core = {"seq": seq + 1 - 2 * core}
    partner_x = {"seq": seq + 2 - 4 * mine}
    partner_y = {"dp": dp + 1 - 2 * y}
    partner_xy = {"dp": dp + 1 - 2 * y, "seq": seq + 2 - 4 * mine}
    along_z = [{"dp": (dp + 2 * turn) % 8} for turn in (1, 2, 3)]
    plane = (partner_x, partner_y)
    mesh_ids = pl.DeviceIdType.MESH

    barrier = pltpu.get_barrier_semaphore()
    friends = [partner_core, partner_x, partner_y, partner_xy] + along_z
    for other in friends:
        pl.semaphore_signal(barrier, inc=1, device_id=other, device_id_type=mesh_ids)

    loads = [
        (layer_in_ref.at[mine], x_ref.at[pl.ds(0, half)]),
        (out_w_ref, wo_ref),
        (out_grad_ref.at[mine], g_ref.at[pl.ds(0, half)]),
    ]

    def load(i):
        return pltpu.make_async_copy(loads[i][0], loads[i][1], in_sem.at[i])

    def weights(j, slot):
        at = pl.multiple_of(j * width, width)
        return (
            pltpu.make_async_copy(up_w_ref.at[:, pl.ds(at, width)], w_ref.at[slot], w_sem.at[slot]),
            pltpu.make_async_copy(down_w_ref.at[pl.ds(at, width), :], w_ref.at[2 + slot], w_sem.at[2 + slot]),
        )

    def proj_weights(i):
        return pltpu.make_async_copy(qkv_w_ref.at[:, i * width : (i + 1) * width], w_ref.at[i], w_sem.at[4 + i])

    def attention_load(p, slot):
        return pltpu.make_async_copy(att_hbm_ref.at[pl.ds(2 * p, 2)], att_ref.at[slot], att_sem.at[slot])

    def attention_store(p, slot):
        return pltpu.make_async_copy(att_ref.at[slot], att_hbm_ref.at[pl.ds(2 * p, 2)], att_sem.at[2 + slot])

    load(0).start()
    for i in (1, 2, 0):
        proj_weights(i).start()
    for i in (1, 2):
        load(i).start()

    part = half // 2

    def rows_copy(n):
        source, landing = ((layer_in_ref, x_ref), (out_grad_ref, g_ref))[n % 2]
        return pltpu.make_async_remote_copy(
            src_ref=source.at[1 - mine, pl.ds(n // 2 * part, part)],
            dst_ref=landing.at[pl.ds(half + n // 2 * part, part)],
            send_sem=x_send_sem.at[n],
            recv_sem=x_recv_sem.at[n],
            device_id=partner_x,
            device_id_type=mesh_ids,
        )

    def keys_copy(b):
        at = pl.ds(pl.multiple_of(b * part, 8), part)
        return pltpu.make_async_remote_copy(
            src_ref=kv_ref.at[:, at],
            dst_ref=kvo_ref.at[:, at],
            send_sem=kv_send_sem.at[b],
            recv_sem=kv_recv_sem.at[b],
            device_id=partner_core,
            device_id_type=mesh_ids,
        )

    pl.semaphore_wait(barrier, len(friends))
    for n in (0, 2, 1, 3):
        rows_copy(n).start()
    for i, ref in enumerate(
        (out_b_ref, mid_gain_ref, mid_bias_ref, down_b_ref, pre_gain_ref, pre_bias_ref, q_bias_ref, v_bias_ref)
    ):
        par_ref[i : i + 1, :] = ref[...].reshape(1, width)
    for j in range(steps):
        par_ref[8 + j : 9 + j, :] = up_b_ref[j * width : (j + 1) * width].reshape(1, width)

    full = 4 * half
    chunks = (seq, seq + 2 - 4 * mine, seq + 1 - 2 * core, 3 - seq)
    mask_ref[...] = jnp.zeros_like(mask_ref)
    mask_ref[0:1, 2 : 2 + PATCHES] = patch_ref[pl.ds(mine, 1), :].astype(F32)
    first_chunk = core * 2 + mine
    kept = pltpu.roll(mask_ref[...], first_chunk * half, 1)[:, :full]
    lane = lax.broadcasted_iota(jnp.int32, kept.shape, 1)
    chunk = lane // half
    start_row = jnp.where(chunk < 2, jnp.where(chunk < 1, chunks[0], chunks[1]), jnp.where(chunk < 3, chunks[2], chunks[3]))
    number = start_row * half + lane - chunk * half
    token = number - (3 + PATCHES)
    valid = (
        (kept > 0.5)
        | (number < 2)
        | (number == 2 + PATCHES)
        | ((token >= 0) & (token < TEXT) & (token < length_ref[mine]))
    )
    mask_ref[:, :full] = jnp.where(valid, 0.0, -1e30)

    @pl.loop(0, 4)
    def _(b):
        @pl.when(b == 0)
        def _():
            load(0).wait()
            for i in (1, 2, 0):
                proj_weights(i).wait()

        for n in range(2):

            @pl.when(b == 2 + n)
            def _(n=n):
                rows_copy(2 * n).wait()

        at = pl.ds(pl.multiple_of(b * part, 8), part)
        unit_in, _ = normalize(x_ref[at, :].astype(F32))
        n1_ref[at, :] = (unit_in * par_ref[4:5, :] + par_ref[5:6, :]).astype(BF16)
        kv_ref[0, at, :] = dot(n1_ref[at, :], w_ref[1]).astype(BF16)
        kv_ref[1, at, :] = (dot(n1_ref[at, :], w_ref[2]) + par_ref[7:8, :]).astype(BF16)
        keys_copy(b).start()
        q_ref[at, :] = ((dot(n1_ref[at, :], w_ref[0]) + par_ref[6:7, :]) * 0.125).astype(BF16)

    for copy in weights(0, 0):
        copy.start()
    for b in range(4):
        keys_copy(b).wait()

    @pl.loop(0, HEADS // 2)
    def _(p):
        slot = p % 2
        lanes = pl.ds(pl.multiple_of(p * 2 * HEAD_DIM, 2 * HEAD_DIM), 2 * HEAD_DIM)
        keys = jnp.concatenate([kv_ref[0, :, lanes], kvo_ref[0, :, lanes]], axis=0)
        values = jnp.concatenate([kv_ref[1, :, lanes], kvo_ref[1, :, lanes]], axis=0)

        @pl.when(p >= 2)
        def _():
            attention_store(p - 2, slot).wait()

        parts = []
        for head, query in enumerate(halves(q_ref[:, lanes])):
            scores = dot(query, keys, 1, 1) + mask_ref[0:1, :full]
            exponent = jnp.exp(scores - jnp.max(scores, axis=-1, keepdims=True))
            norm = jnp.sum(exponent, axis=-1, keepdims=True)
            att = (exponent * (1.0 / norm)).astype(BF16)
            att_ref[slot, head] = att
            parts.append(dot(att, values))
        ctx_ref[:, lanes] = join(*parts).astype(BF16)
        attention_store(p, slot).start()

    for p in (HEADS // 2 - 2, HEADS // 2 - 1):
        attention_store(p, p % 2).wait()
    for p in range(2):
        attention_load(p, p).start()

    per = u_ref.shape[3]
    up, down, out, qkv = 0, steps, 2 * steps, 2 * steps + 1
    last = qkv + 3
    pair_width = 2 * HEAD_DIM

    def buffer(unit):
        if isinstance(unit, int) and unit >= last - 1:
            return uh_ref.at[unit - last + 1], r0h_ref.at[unit - last + 1], rh_ref.at[unit - last + 1]
        return u_ref.at[unit], r0_ref.at[unit], r_ref.at[unit]

    def is_last(unit):
        return isinstance(unit, int) and unit == last

    def remote(unit, sem, sent, landing, target):
        return pltpu.make_async_remote_copy(
            src_ref=sent,
            dst_ref=landing,
            send_sem=send_sem.at[unit, sem],
            recv_sem=recv_sem.at[unit, sem],
            device_id=target,
            device_id_type=mesh_ids,
        )

    def remaining(axes, stage):
        count = 16
        for axis in axes[: stage - 1]:
            count //= 4 if axis == 2 else 2
        return count

    def land_at(axes, stage):
        return 14 if stage == 3 and axes[2] != 2 else LAND_AT[stage]

    def is_down(unit):
        return isinstance(unit, int) and down <= unit < out

    def natural(i, unit, axes):
        count, number, rest = 16, 0, i
        for axis in axes:
            count //= 4 if axis == 2 else 2
            digit, rest = rest // count, rest % count
            if axis == 2:
                number = number + (digit if is_down(unit) else 4 * digit)
            else:
                number = number + (1, 2)[axis] * (4 if is_down(unit) else 1) * differs(digit, bits[axis])
        return number

    def arrived(unit, stage, axes):
        held_ref, first_ref, later_ref = buffer(unit)
        if stage == 0:

            def fresh(i):
                n = natural(i, unit, axes)
                return held_ref[core, n] + first_ref[n]

            return 16, fresh
        if is_last(unit):
            axis, count, held, landing = (None, 4, 0, 0) if stage == 1 else (2, 1, z, LAND_AT[3])
        else:
            axis, landing = axes[stage - 1], land_at(axes, stage)
            count = remaining(axes, stage + 1)
            held = z * count if axis == 2 else 0

        def piece(i):
            if stage < 3 and axis in (0, 1):
                return held_ref[1 - core, held + i] + later_ref[landing + i]
            value = held_ref[1 - core, held + i].astype(F32)
            for n in range(3 if axis in (None, 2) else 1):
                value = value + later_ref[landing + n * count + i].astype(F32)
            return value

        return count, piece

    def transfers(unit, stage, axes):
        held_ref, first_ref, later_ref = buffer(unit)
        if stage == 0:
            return [remote(unit, 0, held_ref.at[1 - core], first_ref, partner_core)]
        if stage < 3 and is_last(unit):
            targets = (partner_y, partner_x, partner_xy)
            return [
                remote(
                    unit,
                    1 + i,
                    held_ref.at[1 - core, pl.ds(4 + 4 * i, 4)],
                    later_ref.at[pl.ds(4 * i, 4)],
                    targets[i],
                )
                for i in range(3)
            ]
        where = 1 - core if stage == 1 else core
        if is_last(unit):
            sent, landing, count = SEND_AT[3], LAND_AT[3], 4
        else:
            sent, landing, count = SEND_AT[stage], land_at(axes, stage), remaining(axes, stage)
            if axes[stage - 1] != 2:
                half_count = count // 2
                return [
                    remote(
                        unit,
                        stage,
                        held_ref.at[where, pl.ds(sent, half_count)],
                        later_ref.at[pl.ds(landing, half_count)],
                        plane[axes[stage - 1]],
                    )
                ]
        count //= 4
        return [
            remote(
                unit,
                4 + i,
                held_ref.at[where, pl.ds(sent + (z + 1 + i) % 4 * count, count)],
                later_ref.at[pl.ds(landing + i * count, count)],
                along_z[i],
            )
            for i in range(3)
        ]

    def start(unit, stage, axes):
        for copy in transfers(unit, stage, axes):
            copy.start()

    def finish(unit, stage, axes):
        for copy in transfers(unit, stage, axes):
            copy.wait()

    def down_send(j, unit):
        place = (j - z + 3) % 4
        return [
            remote(
                unit,
                4 + place,
                u_ref.at[unit, core, pl.ds(SEND_AT[3], 4)],
                rz_ref.at[place],
                {"dp": 2 * j + y},
            )
        ]

    def add_up(unit, stage, axes):
        held_ref, first_ref, later_ref = buffer(unit)
        count, piece = arrived(unit, stage, axes)
        following = 3 if is_last(unit) and stage == 1 else stage + 1
        sent, where = SEND_AT[following], 1 - core if following == 1 else core
        if is_last(unit) and stage == 0:

            @pl.loop(0, 16)
            def _(i):
                held_ref[1 - core, i] = piece(i).astype(BF16)

        elif is_last(unit) or axes[following - 1] == 2:

            @pl.loop(0, count)
            def _(i):
                value = piece(i).astype(BF16)
                held_ref[1 - core, i] = value
                held_ref[where, sent + i] = value

        else:

            @pl.loop(0, count // 2)
            def _(i):
                stays, goes = piece(i), piece(count // 2 + i)
                held_ref[1 - core, i] = stays.astype(BF16)
                held_ref[where, sent + i] = goes.astype(BF16)

    def go_on(unit, stage, axes):
        following = 3 if is_last(unit) and stage == 1 else stage + 1
        if following == 3 and is_down(unit):
            chunk = unit - down

            @pl.when(z != chunk)
            def _():
                for copy in down_send(chunk, unit):
                    copy.start()

        else:
            start(unit, following, axes)

    def total(unit, axes):
        finish(unit, 3, axes)
        _, piece = arrived(unit, 3, axes)
        return piece(0) * factor

    def store_unit(unit, value, first=0, chunk=False):
        held_ref, lanes = buffer(unit)[0], value.shape[1]
        for n in range(32):
            piece, side = (4 * (n // 8) + n % 4, n // 4 % 2) if chunk else (n // 2, n % 2)
            held_ref[side, piece, :, first : first + lanes] = value[n * per : (n + 1) * per].astype(BF16)

    def vector_copy(late, n):
        ref, recv = (vl_ref, vlrecv_ref) if late else (ve_ref, verecv_ref)
        if late:
            target = ([partner_core, partner_x, partner_y, partner_xy] + along_z)[n]
        else:
            target = ([partner_core, partner_x, partner_y] + along_z)[n]
        return pltpu.make_async_remote_copy(
            src_ref=ref,
            dst_ref=recv.at[n],
            send_sem=v_send_sem.at[late, n],
            recv_sem=v_recv_sem.at[late, n],
            device_id=target,
            device_id_type=mesh_ids,
        )

    STEPS = (((0,), (1,), (2,), (3, 4, 5)), ((0,), (1, 2, 3), (4, 5, 6)))

    def vector_wait(late, n):
        for i in STEPS[late][n - 1] if n else ():
            vector_copy(late, i).wait()

    def vector_add(late, n):
        ref, recv = (vl_ref, vlrecv_ref) if late else (ve_ref, verecv_ref)
        for i in STEPS[late][n - 1] if n else ():
            ref[...] += recv[i]

    def vector_go_on(late, n):
        for i in STEPS[late][n] if n < len(STEPS[late]) else ():
            vector_copy(late, i).start()

    orders, in_chunk, after_mlp, in_pair, after_proj, tail = plan

    def run(events):
        for unit, stage in events:
            if unit == "give":
                for copy in give(*((layer_out_ref, 0), (in_grad_ref, 1))[stage]):
                    copy.start()
            elif unit in ("early", "late"):
                late = int(unit == "late")
                vector_wait(late, stage)
                vector_add(late, stage)
                vector_go_on(late, stage)
            else:
                finish(unit, stage, orders[unit])
                add_up(unit, stage, orders[unit])
                go_on(unit, stage, orders[unit])

    load(1).wait()
    middle = x_ref[...].astype(F32) + dot(ctx_ref[...], wo_ref[...]) + par_ref[0:1, :]
    mid_ref[...] = middle
    unit_mid, _ = normalize(middle)
    n2_ref[...] = (unit_mid * par_ref[1:2, :] + par_ref[2:3, :]).astype(BF16)
    acc_ref[...] = middle + par_ref[3:4, :]
    dn_ref[...] = jnp.zeros_like(dn_ref)
    vl_ref[...] = jnp.zeros_like(vl_ref)
    load(2).wait()
    rows_copy(1).wait()
    rows_copy(3).wait()

    def chunk_events(j, where):
        for n in range(steps):
            if in_chunk[n][where]:

                @pl.when(j == n)
                def _(n=n):
                    run(in_chunk[n][where])

    @pl.loop(0, steps)
    def _(j):
        slot = j % 2
        for copy in weights(j, slot):
            copy.wait()

        @pl.when(j + 1 < steps)
        def _():
            for copy in weights(j + 1, 1 - slot):
                copy.start()

        normed = n2_ref[...]
        grad_low = g_ref[...]
        wu, wd = w_ref.at[slot], w_ref.at[2 + slot]
        pre = dot(normed, wu[...]) + par_ref[pl.ds(8 + j, 1), :]
        phi = 0.5 * (1.0 + lax.erf(pre * math.sqrt(0.5)))
        hidden = (pre * phi).astype(BF16)
        slope = phi + pre * (jnp.exp(-0.5 * pre * pre) * (1.0 / math.sqrt(2 * math.pi)))
        chunk_events(j, 0)
        acc_ref[...] += dot(hidden, wd[...])
        store_unit(down + j, dot(hidden, grad_low, 0, 0), chunk=True)
        grad_pre = dot(grad_low, wd[...], 1, 1) * slope
        ve_ref[pl.ds(4 + j, 1), :] = column_sum(grad_pre)
        gpre_low = grad_pre.astype(BF16)
        chunk_events(j, 1)
        store_unit(up + j, dot(normed, gpre_low, 0, 0))
        dn_ref[...] += dot(gpre_low, wu[...], 1, 1)
        start(down + j, 0, orders[down])
        start(up + j, 0, orders[up])
        chunk_events(j, 2)

    for i in range(3):
        proj_weights(i).start()
    res_ref[0] = acc_ref[...].astype(BF16)

    def give(ref, n):
        mine_copy = pltpu.make_async_copy(res_ref.at[n, pl.ds(0, half)], ref.at[mine], io_sem.at[n])
        other_copy = pltpu.make_async_remote_copy(
            src_ref=res_ref.at[n, pl.ds(half, half)],
            dst_ref=ref.at[mine],
            send_sem=io_send_sem.at[n],
            recv_sem=io_recv_sem.at[n],
            device_id=partner_x,
            device_id_type=mesh_ids,
        )
        return mine_copy, other_copy

    unit_mid, scale = normalize(mid_ref[...])
    dn = dn_ref[...]
    grad = g_ref[...].astype(F32)
    gmid = grad + normalize_back(unit_mid, scale, par_ref[1:2, :], dn)
    ve_ref[0:1, :] = column_sum(gmid)
    ve_ref[1:2, :] = column_sum(dn * unit_mid)
    ve_ref[2:3, :] = column_sum(dn)
    ve_ref[3:4, :] = column_sum(grad)
    acc_ref[...] = gmid
    low = gmid.astype(BF16)
    store_unit(out, dot(ctx_ref[...], low, 0, 0))
    gctx_ref[...] = dot(low, wo_ref[...], 1, 1).astype(BF16)
    start(out, 0, orders[out])
    dn_ref[...] = jnp.zeros_like(dn_ref)
    run(after_mlp)

    third = 2 * pair_width

    def exchange(p):
        return pltpu.make_async_remote_copy(
            src_ref=dsend_ref.at[p % 3],
            dst_ref=drecv_ref.at[p],
            send_sem=dk_send_sem.at[p],
            recv_sem=dk_recv_sem.at[p],
            device_id=partner_core,
            device_id_type=mesh_ids,
        )

    def project(pairs, unit):
        span = len(pairs) * pair_width
        for i, p in enumerate(pairs):
            exchange(p).wait()
            lane = slice(p * pair_width, (p + 1) * pair_width)
            here = slice(i * pair_width, (i + 1) * pair_width)
            for n in range(2):
                grad = down_ref[p % 3, n] + drecv_ref[p, n].astype(F32)
                if n == 1:
                    vl_ref[3:4, lane] = column_sum(grad)
                dg_ref[1 + n, :, here] = grad.astype(BF16)
            dg_ref[0, :, here] = dq_of(p)
        cols = slice(pairs[0] * pair_width, pairs[0] * pair_width + span)
        for n in range(3):
            store_unit(unit, dot(n1_ref[...], dg_ref[n, :, :span], 0, 0), n * span)
        more = dot(dg_ref[0, :, :span], w_ref[0, :, cols], 1, 1)
        for n in range(1, 3):
            more = more + dot(dg_ref[n, :, :span], w_ref[n, :, cols], 1, 1)
        dn_ref[...] += more
        start(unit, 0, orders[unit])

    def dq_of(p):
        return dg_ref[3, :, (p % 3) * pair_width : (p % 3 + 1) * pair_width]

    def attention_pair(p, slot, third_slot, between):
        attention_load(p, slot).wait()
        lanes = pl.ds(pl.multiple_of(p * pair_width, pair_width), pair_width)
        keys = jnp.concatenate([kv_ref[0, :, lanes], kvo_ref[0, :, lanes]], axis=0)
        values = jnp.concatenate([kv_ref[1, :, lanes], kvo_ref[1, :, lanes]], axis=0)
        queries = q_ref[:, lanes]
        gctx = gctx_ref[:, lanes]
        dq, dk, dv = [], [], []
        for head, grad in enumerate(halves(gctx)):
            att = att_ref[slot, head]
            wide = att.astype(F32)
            datt = dot(grad, values, 1, 1)
            inner = jnp.sum(wide * datt, axis=-1, keepdims=True)
            dscore = (wide * (datt - inner)).astype(BF16)
            dq.append(dot(dscore, keys))
            dk.append(dot(dscore, queries, 0, 0))
            dv.append(dot(att, gctx, 0, 0))
            if head == 0:
                between()
        dquery = join(*dq) * 0.125
        dg_ref[3, :, pl.ds(pl.multiple_of(third_slot * pair_width, pair_width), pair_width)] = dquery.astype(BF16)
        vl_ref[2:3, lanes] = column_sum(dquery)
        for n, grad in enumerate((join(*dk), join(*dv))):
            down_ref[third_slot, n] = grad[:rows]
            dsend_ref[third_slot, n] = grad[rows:].astype(BF16)
        exchange(p).start()

    def pairs_loop(first, count):
        def pair_events(i, where):
            for n in range(count):
                if in_pair[first + n][where]:

                    @pl.when(i == n)
                    def _(n=n):
                        run(in_pair[first + n][where])

        @pl.loop(0, count)
        def _(i):
            p = first + i
            attention_pair(p, p % 2, p % 3, lambda: pair_events(i, 0))

            @pl.when(p + 2 < HEADS // 2)
            def _():
                attention_load(p + 2, p % 2).start()

            pair_events(i, 1)

    pairs_loop(0, 3)
    for i in range(3):
        proj_weights(i).wait()
    project((0, 1), qkv)
    run(after_proj[0])
    pairs_loop(3, 2)
    project((2, 3), qkv + 1)
    run(after_proj[1])
    pairs_loop(5, 1)
    project((4,), last - 1)
    run(after_proj[2])
    project((5,), last)
    run(after_proj[3])

    unit_in, scale = normalize(x_ref[...].astype(F32))
    dn = dn_ref[...]
    res_ref[1] = (acc_ref[...] + normalize_back(unit_in, scale, par_ref[4:5, :], dn)).astype(BF16)
    vl_ref[0:1, :] = column_sum(dn * unit_in)
    vl_ref[1:2, :] = column_sum(dn)
    vector_go_on(1, 0)
    run(tail)

    me = dp * lax.axis_size("seq") + seq
    both = jnp.concatenate([ve_ref[...], vl_ref[...]], axis=0) * factor
    turned = pltpu.roll(both, (width - me * per) % width, 1)
    small_ref[...] = turned[:, : small_ref.shape[1]]
    per_up = steps * per
    row = (me * per_up) // width
    up_bias = jnp.broadcast_to(ve_ref[pl.ds(4 + row, 1), :] * factor, (8, width))
    shift = (width - (me * per_up - row * width)) % width
    upb_ref[...] = pltpu.roll(up_bias, shift, 1)[:, : upb_ref.shape[1]]

    for j in range(steps):
        dup_ref[:, j * width : (j + 1) * width] = total(up + j, orders[up + j])
    for j in range(steps):

        @pl.when(z == j)
        def _(j=j):
            for i in range(3):
                remote(down + j, 4 + i, rz_ref.at[i], rz_ref.at[i], along_z[i]).wait_recv()
            for part in range(steps):
                value = u_ref[down + j, 1 - core, part].astype(F32)
                for i in range(3):
                    value = value + rz_ref[i, part].astype(F32)
                ddown_ref[part * per : (part + 1) * per, :] = value * factor

        @pl.when(z != j)
        def _(j=j):
            for copy in down_send(j, down + j):
                copy.wait_send()

    dout_ref[...] = total(out, orders[out])
    for pairs, unit in (((0, 1), qkv), ((2, 3), qkv + 1), ((4,), last - 1), ((5,), last)):
        value = total(unit, orders[unit])
        span = len(pairs) * pair_width
        for n in range(3):
            at = n * width + pairs[0] * pair_width
            dqkv_ref[:, at : at + span] = value[:, n * span : (n + 1) * span]
    for n, ref in enumerate((layer_out_ref, in_grad_ref)):
        for copy in give(ref, n):
            copy.wait()

def results_kernel(small_ref, upb_ref, *refs):
    count = (len(refs) - 11) // 3
    big_in, outs, vectors, rooms = refs[:count], refs[count : 2 * count], refs[2 * count : -2 - count], refs[-2 - count : -2]
    in_sem, out_sem = refs[-2:]
    reads = [pltpu.make_async_copy(big_in[i], rooms[i], in_sem.at[i]) for i in range(count)]
    writes = [pltpu.make_async_copy(rooms[i], outs[i], out_sem.at[i]) for i in range(count)]
    for copy in reads:
        copy.start()
    for i, row in enumerate((8, 9, 10, 11, 0, 1, 2, 3)):
        vectors[i][...] = small_ref[row : row + 1, : vectors[i].shape[1]]
    vectors[8][...] = upb_ref[0:1, : vectors[8].shape[1]]
    for read, write in zip(reads, writes):
        read.wait()
        write.start()
    for copy in writes:
        copy.wait()


PLAN = (((0, 2, 1), (1, 2, 0), (0, 2, 1), (1, 2, 0), (1, 0, 2), (0, 1, 2), (1, 0, 2), (1, 0, 2), (1, 0, 2), (0, 1, 2), (0, 1, 2), (1, 0, 2), (0, 1, 2)), (((), (), ()), ((), (), ((0, 0), (4, 0))), ((), (), ((1, 0), (5, 0))), ((), (), ((2, 0), (6, 0), (0, 1), (4, 1)))), (('early', 0), (3, 0), (7, 0), (5, 1), (1, 1)), (((), (('early', 1), (8, 0), ('give', 0))), ((), ((2, 1), (0, 2), (6, 1), (4, 2), ('early', 2))), ((), ((1, 2), (3, 1))), ((), ((2, 2), (7, 1), (6, 2), (9, 0))), ((), ((5, 2),)), ((), ((8, 1), ('early', 3)))), ((), ((7, 2),), ((10, 0), (3, 2), (9, 1)), ((11, 0),)), ((8, 2), (12, 0), (9, 2), ('late', 1), ('early', 4), (10, 1), (11, 1), (12, 1), ('late', 2), ('give', 1), (11, 2), (10, 2), ('late', 3)))


def on_device(
    layer_in,
    out_grad,
    pre_gain,
    pre_bias,
    qkv_w,
    q_bias,
    v_bias,
    out_w,
    out_b,
    mid_gain,
    mid_bias,
    up_w,
    up_b,
    down_w,
    down_b,
    patch_keep,
    text_len,
):
    seq_here, half, width = layer_in.shape
    dp, seq = lax.axis_size("dp"), lax.axis_size("seq")
    assert seq_here == 2 and seq == 4
    full = half * seq
    rows = 2 * half
    ff = up_w.shape[1]
    steps = ff // width
    devices = dp * seq
    place_seq = lax.axis_index("seq")
    me = lax.axis_index("dp") * seq + place_seq
    mine, core = place_seq // 2, place_seq % 2

    bits = devices.bit_length() - 1
    halving = (dp, seq) == (8, 4) and width % (8 * devices) == 0
    if halving:
        shards, at_me, at_core = devices, me, core
        dp_bits = list(range(2, bits))
        order_x = [1] + dp_bits
        order_y = dp_bits[:1] + [1] + dp_bits[1:]
        order_z = dp_bits[1:] + [1] + dp_bits[:1]
    else:
        shards, at_me, at_core = 32, 0, 0
        order_x = order_y = order_z = [4, 3, 2, 1]
    per = width // shards
    per_down = ff // shards
    pairs = shards // 2
    info = jnp.stack(
        [
            jnp.asarray(v, jnp.int32)
            for v in (
                mine,
                at_core,
                place(at_me >> 1, order_x),
                place(at_me >> 1, order_y),
                place(at_me >> 1, order_z),
                me,
            )
        ]
    )

    def swap(value, bit):
        if bit < 2:
            return lax.ppermute(value, "seq", [(i, i ^ (1 << bit)) for i in range(seq)])
        return lax.ppermute(value, "dp", [(i, i ^ (1 << (bit - 2))) for i in range(dp)])

    row = lambda v: v.reshape(-1, width)
    own_rows = pl.BlockSpec((1, half, width), lambda i, info: (info[0], 0, 0))
    vec = fixed((1, width))
    act = fixed((rows, width))

    factor = 1.0 / math.sqrt(seq_here * full * dp)
    per_vec, per_up = width // devices, ff // devices
    if halving:
        hbm = pl.BlockSpec(memory_space=pl.ANY)
        units = 2 * steps + 4
        big = lambda *shape: pltpu.VMEM(shape, F32)
        low = lambda *shape: pltpu.VMEM(shape, BF16)
        dma = lambda *shape: pltpu.SemaphoreType.DMA(shape)
        operands = (layer_in, out_grad, qkv_w, out_w, up_w, down_w)
        vectors = (out_b, mid_gain, mid_bias, down_b, pre_gain, pre_bias, q_bias, v_bias, up_b, patch_keep)
        results = [(per, ff), (per_down, width), (per, width), (per, 3 * width), (16, 128), (8, 128)]
        *large, small, up_bias, _ = pl.pallas_call(
            functools.partial(back_kernel, factor, PLAN),
            in_specs=[hbm] * len(operands)
            + [fixed(v.shape) for v in vectors]
            + [pl.BlockSpec(memory_space=pltpu.SMEM)],
            out_shape=[shape_of(layer_in.shape, BF16)] * 2 + [shape_of(s, F32) for s in results]
            + [shape_of((HEADS, rows, full), BF16)],
            out_specs=[hbm] * 2 + [fixed(s) for s in results] + [hbm],
            scratch_shapes=[
                big(16, width),
                big(8, pl.cdiv(full, 128) * 128),
                low(rows, width),
                low(rows, width),
                low(rows, width),
                low(rows, width),
                low(rows, width),
                low(2, rows, width),
                low(2, rows, width),
                low(2, 2, rows, full),
                low(width, width),
                low(4, width, width),
                big(rows, width),
                big(rows, width),
                big(rows, width),
                low(rows, width),
                low(rows, width),
                low(4, rows, 6 * HEAD_DIM),
                big(3, 2, rows, 2 * HEAD_DIM),
                low(3, 2, rows, 2 * HEAD_DIM),
                low(6, 2, rows, 2 * HEAD_DIM),
                low(2, rows, width),
                big(8, width),
                big(8, width),
                big(6, 8, width),
                big(7, 8, width),
                low(units - 1, 2, 16, per, width),
                low(units - 1, 16, per, width),
                low(units - 1, 16, per, width),
                low(2, 2, 16, per, width // 2),
                low(2, 16, per, width // 2),
                low(2, 16, per, width // 2),
                low(3, steps, per, width),
                dma(3),
                dma(7),
                dma(4),
                dma(units + 1, 7),
                dma(units + 1, 7),
                dma(6),
                dma(6),
                dma(2, 7),
                dma(2, 7),
                dma(2),
                dma(2),
                dma(2),
                dma(4),
                dma(4),
                dma(4),
                dma(4),
            ],
            compiler_params=pltpu.CompilerParams(
                vmem_limit_bytes=64 * 1024 * 1024, collective_id=0, has_side_effects=True
            ),
        )(*operands, *vectors, text_len)
        vec_shapes = [(1, per_vec)] * 8 + [(1, per_up)]
        whole = pl.pallas_call(
            results_kernel,
            in_specs=[pl.BlockSpec(memory_space=pltpu.VMEM)] * 2 + [hbm] * len(large),
            out_shape=[shape_of(v.shape, v.dtype) for v in large] + [shape_of(s, F32) for s in vec_shapes],
            out_specs=[hbm] * len(large) + [pl.BlockSpec(memory_space=pltpu.VMEM)] * len(vec_shapes),
            scratch_shapes=[pltpu.VMEM(v.shape, v.dtype) for v in large] + [dma(len(large)), dma(len(large))],
        )(small, up_bias, *large)
        layer_out, in_grad, d_wup, d_wdown, d_wout, d_qkv = whole[:6]
        d_pregain, d_prebias, d_qbias, d_vbias, d_outbias, d_midgain, d_midbias, d_downbias, d_upbias = (
            v.reshape(-1) for v in whole[6:]
        )
        return (
            layer_out,
            in_grad,
            d_pregain,
            d_prebias,
            d_qkv,
            d_qbias,
            d_vbias,
            d_wout,
            d_outbias,
            d_midgain,
            d_midbias,
            d_wup,
            d_upbias,
            d_wdown,
            d_downbias,
        )

    x_other = swap(lax.dynamic_index_in_dim(layer_in, 1 - mine, 0, False), 1)
    g_other = swap(lax.dynamic_index_in_dim(out_grad, 1 - mine, 0, False), 1)

    patches = lax.dynamic_index_in_dim(patch_keep, mine, 0, False)
    length = lax.dynamic_index_in_dim(text_len, mine, 0, False)
    valid = jnp.concatenate(
        [
            jnp.ones((2,), jnp.int32),
            patches,
            jnp.ones((1,), jnp.int32),
            (jnp.arange(TEXT, dtype=jnp.int32) < length).astype(jnp.int32),
            jnp.zeros((full - 3 - PATCHES - TEXT,), jnp.int32),
        ]
    )
    valid = valid.reshape(seq, half)
    valid = jnp.concatenate(
        [lax.dynamic_index_in_dim(valid, place_seq ^ turn, 0, True) for turn in (0, 2, 1, 3)], axis=1
    )
    mask = jnp.where(valid > 0, 0.0, -1e30).astype(F32)

    square = 2 * rows * width * width
    kv_bias = jnp.concatenate([jnp.zeros((1, 1, width), F32), v_bias.reshape(1, 1, width)], axis=0)
    n1, kv = call(
        qkv_kernel,
        (2,),
        [
            own_rows,
            fixed((half, width)),
            vec,
            vec,
            pl.BlockSpec((width, width), lambda i, _: (0, i + 1)),
            pl.BlockSpec((1, 1, width), lambda i, _: (i, 0, 0)),
        ],
        [shape_of((rows, width), BF16), shape_of((2, rows, width), BF16)],
        [act, pl.BlockSpec((1, rows, width), lambda i, _: (i, 0, 0))],
        flops=2 * square,
        nbytes=5 * 10**6,
    )(info, layer_in, x_other, row(pre_gain), row(pre_bias), qkv_w, kv_bias)
    kv_other = swap(kv, 0)
    q = call(
        query_kernel,
        (1,),
        [act, pl.BlockSpec((width, width), lambda i, _: (0, 0)), vec],
        shape_of((rows, width), BF16),
        act,
        flops=square,
        nbytes=3 * 10**6,
    )(info, n1, qkv_w, row(q_bias))

    pair_width = 2 * HEAD_DIM
    blocks = width // pair_width
    col = pl.BlockSpec((rows, pair_width), lambda i, _: (0, i))
    col2 = pl.BlockSpec((2, rows, pair_width), lambda i, _: (0, 0, i))
    att_spec = pl.BlockSpec((2, rows, full), lambda i, _: (i, 0, 0))
    head_flops = 2 * rows * full * pair_width * HEADS
    ctx, att = call(
        attention_kernel,
        (blocks,),
        [col, col2, col2, fixed((1, full))],
        [shape_of((rows, width), BF16), shape_of((HEADS, rows, full), BF16)],
        [col, att_spec],
        flops=4 * head_flops,
        nbytes=12 * 10**6,
        trans=HEADS * rows * full,
    )(info, q, kv, kv_other, mask)

    orders = (order_x, order_y, order_z)
    mlp_out = call(
        functools.partial(mlp_kernel, orders, per, per_down, steps),
        (steps,),
        [
            own_rows,
            fixed((half, width)),
            own_rows,
            fixed((half, width)),
            act,
            fixed((width, width)),
            vec,
            vec,
            vec,
            pl.BlockSpec((width, width), lambda i, _: (0, i)),
            pl.BlockSpec((1, 1, width), lambda i, _: (i, 0, 0)),
            pl.BlockSpec((width, width), lambda i, _: (i, 0)),
            vec,
        ],
        [
            shape_of((half, width), BF16),
            shape_of((half, width), BF16),
            shape_of((rows, width), F32),
            shape_of((rows, width), BF16),
            shape_of((4 + steps, width), F32),
            shape_of((pairs, steps, per, width), BF16),
            shape_of((pairs, steps, per, width), F32),
            shape_of((pairs, per_down, width), BF16),
            shape_of((pairs, per_down, width), F32),
            shape_of((pairs, per, width), BF16),
            shape_of((pairs, per, width), F32),
        ],
        [
            fixed((half, width)),
            fixed((half, width)),
            act,
            act,
            fixed((4 + steps, width)),
            pl.BlockSpec((pairs, 1, per, width), lambda i, _: (0, i, 0, 0)),
            pl.BlockSpec((pairs, 1, per, width), lambda i, _: (0, i, 0, 0)),
            fixed((pairs, per_down, width)),
            fixed((pairs, per_down, width)),
            fixed((pairs, per, width)),
            fixed((pairs, per, width)),
        ],
        scratch=[
            pltpu.VMEM((rows, width), F32),
            pltpu.VMEM((rows, width), BF16),
            pltpu.VMEM((rows, width), F32),
            pltpu.VMEM((rows, width), F32),
            pltpu.VMEM((width, width), F32),
        ],
        flops=(6 * steps + 3) * square,
        nbytes=40 * 10**6,
        trans=2 * rows * ff,
    )(
        info,
        layer_in,
        x_other,
        out_grad,
        g_other,
        ctx,
        out_w,
        row(out_b),
        row(mid_gain),
        row(mid_bias),
        up_w,
        up_b.reshape(steps, 1, width),
        down_w,
        row(down_b),
    )
    out_own, out_other, gmid, gctx, early, s_up, k_up, s_down, k_down, s_out, k_out = mlp_out
    out_back = swap(out_other, 1)

    def reduce(sent, kept, order):
        got = swap(sent, 0)
        for bit in order:
            total = kept + got.astype(F32)
            cut = total.shape[0] // 2
            kept = total[:cut]
            got = swap(total[cut:].astype(BF16), bit)
        return kept, got

    def natural(sent, kept):
        return jnp.stack([kept, sent.astype(F32)], axis=1)

    if halving:
        up_pair = reduce(s_up, k_up, order_x)
        down_pair = reduce(s_down, k_down, order_y)
        out_pair = reduce(s_out, k_out, order_z)

    dq, dbq, dkv_own, dkv_send = call(
        attention_back_kernel,
        (blocks,),
        [att_spec, col, col2, col2, col],
        [
            shape_of((rows, width), BF16),
            shape_of((1, width), F32),
            shape_of((2, rows, width), F32),
            shape_of((2, rows, width), BF16),
        ],
        [col, pl.BlockSpec((1, pair_width), lambda i, _: (0, i)), col2, col2],
        flops=8 * head_flops,
        nbytes=16 * 10**6,
    )(info, att, q, kv, kv_other, gctx)
    dkv_other = swap(dkv_send, 0)
    shard = fixed((pairs, per, width))
    tile = pltpu.VMEM((width, width), F32)
    dn_q, s_q, k_q = call(
        functools.partial(query_back_kernel, order_x, per),
        (1,),
        [act, act, pl.BlockSpec((width, width), lambda i, _: (0, 0))],
        [shape_of((rows, width), F32), shape_of((pairs, per, width), BF16), shape_of((pairs, per, width), F32)],
        [act, shard, shard],
        scratch=[tile],
        flops=2 * square,
        nbytes=6 * 10**6,
    )(info, n1, dq, qkv_w)
    dkv, dbv, s_k, k_k, s_v, k_v = call(
        functools.partial(key_value_back_kernel, (order_x, order_y), per),
        (1,),
        [act, fixed((2, rows, width)), fixed((2, rows, width))],
        [
            shape_of((2, rows, width), BF16),
            shape_of((1, width), F32),
            shape_of((pairs, per, width), BF16),
            shape_of((pairs, per, width), F32),
            shape_of((pairs, per, width), BF16),
            shape_of((pairs, per, width), F32),
        ],
        [fixed((2, rows, width)), vec, shard, shard, shard, shard],
        scratch=[tile],
        flops=2 * square,
        nbytes=10 * 10**6,
    )(info, n1, dkv_own, dkv_other)
    if halving:
        q_pair = reduce(s_q, k_q, order_x)
        k_pair = reduce(s_k, k_k, order_x)
        v_pair = reduce(s_v, k_v, order_y)
    in_own, in_other, late = call(
        input_back_kernel,
        (1,),
        [
            own_rows,
            fixed((half, width)),
            vec,
            fixed((2, rows, width)),
            fixed((width, 3 * width)),
            act,
            act,
            vec,
            vec,
        ],
        [shape_of((half, width), BF16), shape_of((half, width), BF16), shape_of((8, width), F32)],
        [fixed((half, width)), fixed((half, width)), fixed((8, width))],
        flops=2 * square,
        nbytes=10 * 10**6,
    )(info, layer_in, x_other, row(pre_gain), dkv, qkv_w, dn_q, gmid, dbq, dbv)
    in_back = swap(in_other, 1)

    def give_back(own, other):
        first = jnp.where(mine == 0, own, other)
        second = jnp.where(mine == 0, other, own)
        return jnp.stack([first, second])

    layer_out = give_back(out_own, out_back)
    in_grad = give_back(in_own, in_back)

    factor = 1.0 / math.sqrt(seq_here * full * dp)
    vectors = jnp.concatenate([early, late], axis=0)
    if halving:
        for bit in range(bits):
            vectors = vectors + swap(vectors, bit)
    else:
        vectors = lax.psum(vectors, ("dp", "seq"))
    per_vec, per_up = width // devices, ff // devices
    early_rows = 4 + steps
    small, up_bias = call(
        functools.partial(vector_kernel, factor, per_vec, per_up),
        (1,),
        [
            pl.BlockSpec((early_rows, width), lambda i, _: (0, 0)),
            pl.BlockSpec((8, width), lambda i, _: (early_rows // 8, 0)),
        ],
        [shape_of((early_rows + 8, 128), F32), shape_of((8, 128), F32)],
        [fixed((early_rows + 8, 128)), fixed((8, 128))],
    )(info, vectors, vectors)
    pick = lambda i: small[i, :per_vec]
    d_upbias = up_bias[0, :per_up]
    d_outbias, d_midgain, d_midbias, d_downbias = (pick(i) for i in range(4))
    d_pregain, d_prebias, d_qbias, d_vbias = (pick(early_rows + i) for i in range(4))

    if halving:

        def finish(named):
            operands = [v for pair, _ in named for v in pair]
            shapes = [s for _, s in named]
            return call(
                functools.partial(finish_kernel, factor),
                (1,),
                [fixed(v.shape) for v in operands],
                [shape_of(s, F32) for s in shapes],
                [fixed(s) for s in shapes],
            )(info, *operands)

        d_wup, d_wdown, d_wout = finish(
            [(up_pair, (per, ff)), (down_pair, (per_down, width)), (out_pair, (per, width))]
        )
        d_q, d_k, d_v = finish([(pair, (per, width)) for pair in (q_pair, k_pair, v_pair)])
        d_qkv = jnp.concatenate([d_q, d_k, d_v], axis=1)
    else:

        def scatter(value):
            return lax.psum_scatter(value, ("dp", "seq"), scatter_dimension=0, tiled=True) * factor

        d_wup = scatter(
            natural(s_up, k_up).transpose(0, 1, 3, 2, 4).reshape(width, ff)
        )
        d_wdown = scatter(natural(s_down, k_down).reshape(ff, width))
        d_wout = scatter(natural(s_out, k_out).reshape(width, width))
        d_qkv = scatter(
            jnp.concatenate(
                [natural(s, k).reshape(width, width) for s, k in ((s_q, k_q), (s_k, k_k), (s_v, k_v))],
                axis=1,
            )
        )
    return (
        layer_out,
        in_grad,
        d_pregain,
        d_prebias,
        d_qkv,
        d_qbias,
        d_vbias,
        d_wout,
        d_outbias,
        d_midgain,
        d_midbias,
        d_wup,
        d_upbias,
        d_wdown,
        d_downbias,
    )


def solution(mesh):
    both = ("dp", "seq")
    rows = P("dp", "seq", None)
    return jax.shard_map(
        on_device,
        mesh=mesh,
        in_specs=(rows, rows) + (P(),) * 13 + (P("dp", None), P("dp")),
        out_specs=(
            rows,
            rows,
            P(both),
            P(both),
            P(both, None),
            P(both),
            P(both),
            P(both, None),
            P(both),
            P(both),
            P(both),
            P(both, None),
            P(both),
            P(both, None),
            P(both),
        ),
        check_vma=False,
    )
```

```python
import functools
import math

import jax
import jax.numpy as jnp
from jax import lax
from jax.experimental import pallas as pl
from jax.experimental.pallas import tpu as pltpu
from jax.sharding import PartitionSpec as P

HEADS = 12
HEAD_DIM = 64
PATCHES = 196
TEXT = 512
F32 = jnp.float32
BF16 = jnp.bfloat16
VMEM_BYTES = 60 * 1024 * 1024


def dot(lhs, rhs, lhs_dim=1, rhs_dim=0):
    return lax.dot_general(
        lhs, rhs, (((lhs_dim,), (rhs_dim,)), ((), ())), preferred_element_type=F32
    )


def normalize(values):
    center = values - jnp.mean(values, axis=-1, keepdims=True)
    spread = jnp.mean(center * center, axis=-1, keepdims=True)
    scale = lax.rsqrt(spread + 1e-06)
    return center * scale, scale


def normalize_back(unit, scale, gain, cotangent):
    inner = cotangent * gain
    mean_inner = jnp.mean(inner, axis=-1, keepdims=True)
    mean_unit = jnp.mean(inner * unit, axis=-1, keepdims=True)
    return scale * (inner - mean_inner - unit * mean_unit)


def column_sum(values):
    return jnp.sum(values, axis=0, keepdims=True)


def call(kernel, grid, in_specs, out_shape, out_specs, scratch=(), flops=0, nbytes=0, trans=0):
    return pl.pallas_call(
        kernel,
        grid_spec=pltpu.PrefetchScalarGridSpec(
            num_scalar_prefetch=1,
            grid=grid,
            in_specs=in_specs,
            out_specs=out_specs,
            scratch_shapes=list(scratch),
        ),
        out_shape=out_shape,
        compiler_params=pltpu.CompilerParams(vmem_limit_bytes=VMEM_BYTES),
        cost_estimate=pl.CostEstimate(flops=flops, bytes_accessed=nbytes, transcendentals=trans),
    )


def fixed(shape):
    zeros = (0,) * len(shape)
    return pl.BlockSpec(shape, lambda *_: zeros)


def shape_of(shape, dtype):
    return jax.ShapeDtypeStruct(shape, dtype)


def place(number, order):
    out = 0
    for bit in order:
        out = out * 2 + ((number >> (bit - 1)) & 1)
    return out


def store_shards(tile_ref, send_ref, keep_ref, info_ref, slot, order, rows, pairs, at):
    core = info_ref[1]
    for pair in range(pairs):
        number = pair if at is None else at * pairs + pair
        index = place(number, order) ^ info_ref[slot]
        sent = tile_ref[pl.ds(pl.multiple_of(rows * (2 * pair + 1 - core), 8), rows), :]
        kept = tile_ref[pl.ds(pl.multiple_of(rows * (2 * pair + core), 8), rows), :]
        send_ref[index] = sent.astype(send_ref.dtype).reshape(send_ref.shape[1:])
        keep_ref[index] = kept.reshape(keep_ref.shape[1:])


def qkv_kernel(info_ref, own_ref, other_ref, gain_ref, shift_ref, w_ref, bias_ref, n1_ref, kv_ref):
    @pl.when(pl.program_id(0) == 0)
    def _():
        rows = jnp.concatenate([own_ref[0], other_ref[...]], axis=0).astype(F32)
        unit, _ = normalize(rows)
        n1_ref[...] = (unit * gain_ref[...] + shift_ref[...]).astype(BF16)

    kv_ref[0] = (dot(n1_ref[...], w_ref[...]) + bias_ref[0]).astype(BF16)


def query_kernel(info_ref, n1_ref, w_ref, bias_ref, q_ref):
    q_ref[...] = ((dot(n1_ref[...], w_ref[...]) + bias_ref[...]) * 0.125).astype(BF16)


def halves(value):
    lane = lax.broadcasted_iota(jnp.int32, value.shape, 1)
    zero = jnp.zeros_like(value)
    return jnp.where(lane < HEAD_DIM, value, zero), jnp.where(lane < HEAD_DIM, zero, value)


def join(first, second):
    lane = lax.broadcasted_iota(jnp.int32, first.shape, 1)
    return jnp.where(lane < HEAD_DIM, first, second)


def attention_kernel(info_ref, q_ref, own_ref, other_ref, mask_ref, ctx_ref, att_ref):
    keys = jnp.concatenate([own_ref[0], other_ref[0]], axis=0)
    values = jnp.concatenate([own_ref[1], other_ref[1]], axis=0)
    parts = []
    for head, query in enumerate(halves(q_ref[...])):
        scores = dot(query, keys, 1, 1) + mask_ref[...]
        exponent = jnp.exp(scores - jnp.max(scores, axis=-1, keepdims=True))
        total = jnp.sum(exponent, axis=-1, keepdims=True)
        att = (exponent * (1.0 / total)).astype(BF16)
        att_ref[head] = att
        parts.append(dot(att, values))
    ctx_ref[...] = join(*parts).astype(BF16)


def attention_back_kernel(
    info_ref, att_ref, q_ref, own_ref, other_ref, gctx_ref, dq_ref, dbq_ref, down_ref, dother_ref
):
    keys = jnp.concatenate([own_ref[0], other_ref[0]], axis=0)
    values = jnp.concatenate([own_ref[1], other_ref[1]], axis=0)
    queries = q_ref[...]
    gctx = gctx_ref[...]
    dq, dk, dv = [], [], []
    for head, grad in enumerate(halves(gctx)):
        att = att_ref[head]
        wide = att.astype(F32)
        datt = dot(grad, values, 1, 1)
        inner = jnp.sum(wide * datt, axis=-1, keepdims=True)
        dscore = (wide * (datt - inner)).astype(BF16)
        dq.append(dot(dscore, keys))
        dk.append(dot(dscore, queries, 0, 0))
        dv.append(dot(att, gctx, 0, 0))
    dquery = join(*dq) * 0.125
    dq_ref[...] = dquery.astype(BF16)
    dbq_ref[...] = column_sum(dquery)
    rows = queries.shape[0]
    for i, grad in enumerate((join(*dk), join(*dv))):
        down_ref[i] = grad[:rows]
        dother_ref[i] = grad[rows:].astype(BF16)


def mlp_kernel(
    orders,
    rows_up,
    rows_down,
    steps,
    info_ref,
    x_ref,
    xo_ref,
    g_ref,
    go_ref,
    ctx_ref,
    wo_ref,
    bo_ref,
    gain_ref,
    shift_ref,
    wu_ref,
    bu_ref,
    wd_ref,
    bd_ref,
    out_ref,
    outo_ref,
    gmid_ref,
    gctx_ref,
    vec_ref,
    su_ref,
    ku_ref,
    sd_ref,
    kd_ref,
    so_ref,
    ko_ref,
    mid_ref,
    n2_ref,
    acc_ref,
    dn_ref,
    tile_ref,
):
    step = pl.program_id(0)
    half = xo_ref.shape[0]
    grad_low = jnp.concatenate([g_ref[0], go_ref[...]], axis=0)

    @pl.when(step == 0)
    def _():
        rows = jnp.concatenate([x_ref[0], xo_ref[...]], axis=0).astype(F32)
        middle = rows + dot(ctx_ref[...], wo_ref[...]) + bo_ref[...]
        mid_ref[...] = middle
        unit, _ = normalize(middle)
        n2_ref[...] = (unit * gain_ref[...] + shift_ref[...]).astype(BF16)
        acc_ref[...] = middle + bd_ref[...]
        dn_ref[...] = jnp.zeros_like(dn_ref)

    normed = n2_ref[...]
    pre = dot(normed, wu_ref[...]) + bu_ref[0]
    phi = 0.5 * (1.0 + lax.erf(pre * math.sqrt(0.5)))
    hidden = (pre * phi).astype(BF16)
    slope = phi + pre * (jnp.exp(-0.5 * pre * pre) * (1.0 / math.sqrt(2 * math.pi)))
    acc_ref[...] += dot(hidden, wd_ref[...])
    grad_pre = dot(grad_low, wd_ref[...], 1, 1) * slope
    vec_ref[pl.ds(4 + step, 1), :] = column_sum(grad_pre)
    gpre_low = grad_pre.astype(BF16)
    dn_ref[...] += dot(gpre_low, wu_ref[...], 1, 1)
    tile_ref[...] = dot(normed, gpre_low, 0, 0)
    n_up = tile_ref.shape[0] // (2 * rows_up)
    store_shards(tile_ref, su_ref, ku_ref, info_ref, 2, orders[0], rows_up, n_up, None)
    tile_ref[...] = dot(hidden, grad_low, 0, 0)
    n_down = tile_ref.shape[0] // (2 * rows_down)
    for at in range(steps):

        @pl.when(step == at)
        def _(at=at):
            store_shards(tile_ref, sd_ref, kd_ref, info_ref, 3, orders[1], rows_down, n_down, at)

    @pl.when(step == steps - 1)
    def _():
        result = acc_ref[...].astype(BF16)
        out_ref[...] = result[:half]
        outo_ref[...] = result[half:]
        unit, scale = normalize(mid_ref[...])
        dn = dn_ref[...]
        grad = grad_low.astype(F32)
        gmid = grad + normalize_back(unit, scale, gain_ref[...], dn)
        gmid_ref[...] = gmid
        vec_ref[0:1, :] = column_sum(gmid)
        vec_ref[1:2, :] = column_sum(dn * unit)
        vec_ref[2:3, :] = column_sum(dn)
        vec_ref[3:4, :] = column_sum(grad)
        low = gmid.astype(BF16)
        gctx_ref[...] = dot(low, wo_ref[...], 1, 1).astype(BF16)
        tile_ref[...] = dot(ctx_ref[...], low, 0, 0)
        store_shards(tile_ref, so_ref, ko_ref, info_ref, 4, orders[2], rows_up, n_up, None)


def query_back_kernel(order, rows, info_ref, n1_ref, dq_ref, w_ref, dn_ref, s_ref, k_ref, tile_ref):
    tile_ref[...] = dot(n1_ref[...], dq_ref[...], 0, 0)
    pairs = tile_ref.shape[0] // (2 * rows)
    store_shards(tile_ref, s_ref, k_ref, info_ref, 2, order, rows, pairs, None)
    dn_ref[...] = dot(dq_ref[...], w_ref[...], 1, 1)


def key_value_back_kernel(
    orders, rows, info_ref, n1_ref, own_ref, other_ref, dkv_ref, dbv_ref, sk_ref, kk_ref, sv_ref, kv_ref, tile_ref
):
    pairs = tile_ref.shape[0] // (2 * rows)
    for i, (s_ref, k_ref, slot) in enumerate(((sk_ref, kk_ref, 2), (sv_ref, kv_ref, 3))):
        grad = own_ref[i] + other_ref[i].astype(F32)
        low = grad.astype(BF16)
        dkv_ref[i] = low
        if i == 1:
            dbv_ref[...] = column_sum(grad)
        tile_ref[...] = dot(n1_ref[...], low, 0, 0)
        store_shards(tile_ref, s_ref, k_ref, info_ref, slot, orders[i], rows, pairs, None)


def input_back_kernel(
    info_ref, x_ref, xo_ref, gain_ref, dkv_ref, w_ref, dnq_ref, gmid_ref, dbq_ref, dbv_ref, own_ref, other_ref, vec_ref
):
    half = xo_ref.shape[0]
    dn = dnq_ref[...]
    for i in range(2):
        width = dn.shape[1]
        dn = dn + dot(dkv_ref[i], w_ref[:, (i + 1) * width : (i + 2) * width], 1, 1)
    rows = jnp.concatenate([x_ref[0], xo_ref[...]], axis=0).astype(F32)
    unit, scale = normalize(rows)
    result = (gmid_ref[...] + normalize_back(unit, scale, gain_ref[...], dn)).astype(BF16)
    own_ref[...] = result[:half]
    other_ref[...] = result[half:]
    vec_ref[0:1, :] = column_sum(dn * unit)
    vec_ref[1:2, :] = column_sum(dn)
    vec_ref[2:3, :] = dbq_ref[...]
    vec_ref[3:4, :] = dbv_ref[...]
    vec_ref[4:8, :] = jnp.zeros_like(vec_ref[4:8, :])


def finish_kernel(factor, info_ref, *refs):
    count = len(refs) // 3
    for i in range(count):
        keep, recv, out = refs[2 * i], refs[2 * i + 1], refs[2 * count + i]
        total = (keep[0] + recv[0].astype(F32)) * factor
        if total.ndim == 3:
            width = total.shape[-1]
            for block in range(total.shape[0]):
                out[:, block * width : (block + 1) * width] = total[block]
        else:
            out[...] = total


def vector_kernel(factor, per, per_up, info_ref, early_ref, late_ref, out_ref, up_ref):
    me = info_ref[5]
    width = early_ref.shape[1]
    both = jnp.concatenate([early_ref[...], late_ref[...]], axis=0) * factor
    turned = pltpu.roll(both, lax.rem(width - me * per, width), 1)
    out_ref[...] = turned[:, : out_ref.shape[1]]
    row = (me * per_up) // width
    up = early_ref[pl.ds(4 + row, 1), :] * factor
    up = jnp.broadcast_to(up, (8, width))
    shift = lax.rem(width - (me * per_up - row * width), width)
    up_ref[...] = pltpu.roll(up, shift, 1)[:, : up_ref.shape[1]]


SEND_AT = (0, 8, 0, 8)
LAND_AT = (None, 0, 8, 12)


def differs(bit, mine):
    return bit + mine - 2 * bit * mine


def back_kernel(
    factor,
    plan,
    layer_in_ref,
    out_grad_ref,
    qkv_w_ref,
    out_w_ref,
    up_w_ref,
    down_w_ref,
    out_b_ref,
    mid_gain_ref,
    mid_bias_ref,
    down_b_ref,
    pre_gain_ref,
    pre_bias_ref,
    q_bias_ref,
    v_bias_ref,
    up_b_ref,
    patch_ref,
    length_ref,
    layer_out_ref,
    in_grad_ref,
    dup_ref,
    ddown_ref,
    dout_ref,
    dqkv_ref,
    small_ref,
    upb_ref,
    att_hbm_ref,
    par_ref,
    mask_ref,
    x_ref,
    g_ref,
    ctx_ref,
    n1_ref,
    q_ref,
    kv_ref,
    kvo_ref,
    att_ref,
    wo_ref,
    w_ref,
    mid_ref,
    acc_ref,
    dn_ref,
    n2_ref,
    gctx_ref,
    dg_ref,
    down_ref,
    dsend_ref,
    drecv_ref,
    res_ref,
    ve_ref,
    vl_ref,
    verecv_ref,
    vlrecv_ref,
    u_ref,
    r0_ref,
    r_ref,
    uh_ref,
    r0h_ref,
    rh_ref,
    rz_ref,
    in_sem,
    w_sem,
    att_sem,
    send_sem,
    recv_sem,
    dk_send_sem,
    dk_recv_sem,
    v_send_sem,
    v_recv_sem,
    io_sem,
    io_send_sem,
    io_recv_sem,
    x_send_sem,
    x_recv_sem,
    kv_send_sem,
    kv_recv_sem,
):
    _, half, width = layer_in_ref.shape
    rows = 2 * half
    steps = up_w_ref.shape[1] // width
    dp, seq = lax.axis_index("dp"), lax.axis_index("seq")
    core, mine = seq % 2, seq // 2
    y, z = dp % 2, dp // 2
    bits = (mine, y)
    partner_core = {"seq": seq + 1 - 2 * core}
    partner_x = {"seq": seq + 2 - 4 * mine}
    partner_y = {"dp": dp + 1 - 2 * y}
    partner_xy = {"dp": dp + 1 - 2 * y, "seq": seq + 2 - 4 * mine}
    along_z = [{"dp": (dp + 2 * turn) % 8} for turn in (1, 2, 3)]
    plane = (partner_x, partner_y)
    mesh_ids = pl.DeviceIdType.MESH

    barrier = pltpu.get_barrier_semaphore()
    friends = [partner_core, partner_x, partner_y, partner_xy] + along_z
    for other in friends:
        pl.semaphore_signal(barrier, inc=1, device_id=other, device_id_type=mesh_ids)

    loads = [
        (layer_in_ref.at[mine], x_ref.at[pl.ds(0, half)]),
        (out_w_ref, wo_ref),
        (out_grad_ref.at[mine], g_ref.at[pl.ds(0, half)]),
    ]

    def load(i):
        return pltpu.make_async_copy(loads[i][0], loads[i][1], in_sem.at[i])

    def weights(j, slot):
        at = pl.multiple_of(j * width, width)
        return (
            pltpu.make_async_copy(up_w_ref.at[:, pl.ds(at, width)], w_ref.at[slot], w_sem.at[slot]),
            pltpu.make_async_copy(down_w_ref.at[pl.ds(at, width), :], w_ref.at[2 + slot], w_sem.at[2 + slot]),
        )

    def proj_weights(i):
        return pltpu.make_async_copy(qkv_w_ref.at[:, i * width : (i + 1) * width], w_ref.at[i], w_sem.at[4 + i])

    def attention_load(p, slot):
        return pltpu.make_async_copy(att_hbm_ref.at[pl.ds(2 * p, 2)], att_ref.at[slot], att_sem.at[slot])

    def attention_store(p, slot):
        return pltpu.make_async_copy(att_ref.at[slot], att_hbm_ref.at[pl.ds(2 * p, 2)], att_sem.at[2 + slot])

    load(0).start()
    for i in (1, 2, 0):
        proj_weights(i).start()
    for i in (1, 2):
        load(i).start()

    part = half // 2

    def rows_copy(n):
        source, landing = ((layer_in_ref, x_ref), (out_grad_ref, g_ref))[n % 2]
        return pltpu.make_async_remote_copy(
            src_ref=source.at[1 - mine, pl.ds(n // 2 * part, part)],
            dst_ref=landing.at[pl.ds(half + n // 2 * part, part)],
            send_sem=x_send_sem.at[n],
            recv_sem=x_recv_sem.at[n],
            device_id=partner_x,
            device_id_type=mesh_ids,
        )

    def keys_copy(b):
        at = pl.ds(pl.multiple_of(b * part, 8), part)
        return pltpu.make_async_remote_copy(
            src_ref=kv_ref.at[:, at],
            dst_ref=kvo_ref.at[:, at],
            send_sem=kv_send_sem.at[b],
            recv_sem=kv_recv_sem.at[b],
            device_id=partner_core,
            device_id_type=mesh_ids,
        )

    pl.semaphore_wait(barrier, len(friends))
    for n in (0, 2, 1, 3):
        rows_copy(n).start()
    for i, ref in enumerate(
        (out_b_ref, mid_gain_ref, mid_bias_ref, down_b_ref, pre_gain_ref, pre_bias_ref, q_bias_ref, v_bias_ref)
    ):
        par_ref[i : i + 1, :] = ref[...].reshape(1, width)
    for j in range(steps):
        par_ref[8 + j : 9 + j, :] = up_b_ref[j * width : (j + 1) * width].reshape(1, width)

    full = 4 * half
    chunks = (seq, seq + 2 - 4 * mine, seq + 1 - 2 * core, 3 - seq)
    mask_ref[...] = jnp.zeros_like(mask_ref)
    mask_ref[0:1, 2 : 2 + PATCHES] = patch_ref[pl.ds(mine, 1), :].astype(F32)
    first_chunk = core * 2 + mine
    kept = pltpu.roll(mask_ref[...], first_chunk * half, 1)[:, :full]
    lane = lax.broadcasted_iota(jnp.int32, kept.shape, 1)
    chunk = lane // half
    start_row = jnp.where(chunk < 2, jnp.where(chunk < 1, chunks[0], chunks[1]), jnp.where(chunk < 3, chunks[2], chunks[3]))
    number = start_row * half + lane - chunk * half
    token = number - (3 + PATCHES)
    valid = (
        (kept > 0.5)
        | (number < 2)
        | (number == 2 + PATCHES)
        | ((token >= 0) & (token < TEXT) & (token < length_ref[mine]))
    )
    mask_ref[:, :full] = jnp.where(valid, 0.0, -1e30)

    @pl.loop(0, 4)
    def _(b):
        @pl.when(b == 0)
        def _():
            load(0).wait()
            for i in (1, 2, 0):
                proj_weights(i).wait()

        for n in range(2):

            @pl.when(b == 2 + n)
            def _(n=n):
                rows_copy(2 * n).wait()

        at = pl.ds(pl.multiple_of(b * part, 8), part)
        unit_in, _ = normalize(x_ref[at, :].astype(F32))
        n1_ref[at, :] = (unit_in * par_ref[4:5, :] + par_ref[5:6, :]).astype(BF16)
        kv_ref[0, at, :] = dot(n1_ref[at, :], w_ref[1]).astype(BF16)
        kv_ref[1, at, :] = (dot(n1_ref[at, :], w_ref[2]) + par_ref[7:8, :]).astype(BF16)
        keys_copy(b).start()
        q_ref[at, :] = ((dot(n1_ref[at, :], w_ref[0]) + par_ref[6:7, :]) * 0.125).astype(BF16)

    for copy in weights(0, 0):
        copy.start()
    for b in range(4):
        keys_copy(b).wait()

    @pl.loop(0, HEADS // 2)
    def _(p):
        slot = p % 2
        lanes = pl.ds(pl.multiple_of(p * 2 * HEAD_DIM, 2 * HEAD_DIM), 2 * HEAD_DIM)
        keys = jnp.concatenate([kv_ref[0, :, lanes], kvo_ref[0, :, lanes]], axis=0)
        values = jnp.concatenate([kv_ref[1, :, lanes], kvo_ref[1, :, lanes]], axis=0)

        @pl.when(p >= 2)
        def _():
            attention_store(p - 2, slot).wait()

        parts = []
        for head, query in enumerate(halves(q_ref[:, lanes])):
            scores = dot(query, keys, 1, 1) + mask_ref[0:1, :full]
            exponent = jnp.exp(scores - jnp.max(scores, axis=-1, keepdims=True))
            norm = jnp.sum(exponent, axis=-1, keepdims=True)
            att = (exponent * (1.0 / norm)).astype(BF16)
            att_ref[slot, head] = att
            parts.append(dot(att, values))
        ctx_ref[:, lanes] = join(*parts).astype(BF16)
        attention_store(p, slot).start()

    for p in (HEADS // 2 - 2, HEADS // 2 - 1):
        attention_store(p, p % 2).wait()
    for p in range(2):
        attention_load(p, p).start()

    per = u_ref.shape[3]
    up, down, out, qkv = 0, steps, 2 * steps, 2 * steps + 1
    last = qkv + 3
    pair_width = 2 * HEAD_DIM

    def buffer(unit):
        if isinstance(unit, int) and unit >= last - 1:
            return uh_ref.at[unit - last + 1], r0h_ref.at[unit - last + 1], rh_ref.at[unit - last + 1]
        return u_ref.at[unit], r0_ref.at[unit], r_ref.at[unit]

    def is_last(unit):
        return isinstance(unit, int) and unit == last

    def remote(unit, sem, sent, landing, target):
        return pltpu.make_async_remote_copy(
            src_ref=sent,
            dst_ref=landing,
            send_sem=send_sem.at[unit, sem],
            recv_sem=recv_sem.at[unit, sem],
            device_id=target,
            device_id_type=mesh_ids,
        )

    def remaining(axes, stage):
        count = 16
        for axis in axes[: stage - 1]:
            count //= 4 if axis == 2 else 2
        return count

    def land_at(axes, stage):
        return 14 if stage == 3 and axes[2] != 2 else LAND_AT[stage]

    def is_down(unit):
        return isinstance(unit, int) and down <= unit < out

    def natural(i, unit, axes):
        count, number, rest = 16, 0, i
        for axis in axes:
            count //= 4 if axis == 2 else 2
            digit, rest = rest // count, rest % count
            if axis == 2:
                number = number + (digit if is_down(unit) else 4 * digit)
            else:
                number = number + (1, 2)[axis] * (4 if is_down(unit) else 1) * differs(digit, bits[axis])
        return number

    def arrived(unit, stage, axes):
        held_ref, first_ref, later_ref = buffer(unit)
        if stage == 0:

            def fresh(i):
                n = natural(i, unit, axes)
                return held_ref[core, n] + first_ref[n]

            return 16, fresh
        if is_last(unit):
            axis, count, held, landing = (None, 4, 0, 0) if stage == 1 else (2, 1, z, LAND_AT[3])
        else:
            axis, landing = axes[stage - 1], land_at(axes, stage)
            count = remaining(axes, stage + 1)
            held = z * count if axis == 2 else 0

        def piece(i):
            if stage < 3 and axis in (0, 1):
                return held_ref[1 - core, held + i] + later_ref[landing + i]
            value = held_ref[1 - core, held + i].astype(F32)
            for n in range(3 if axis in (None, 2) else 1):
                value = value + later_ref[landing + n * count + i].astype(F32)
            return value

        return count, piece

    def transfers(unit, stage, axes):
        held_ref, first_ref, later_ref = buffer(unit)
        if stage == 0:
            return [remote(unit, 0, held_ref.at[1 - core], first_ref, partner_core)]
        if stage < 3 and is_last(unit):
            targets = (partner_y, partner_x, partner_xy)
            return [
                remote(
                    unit,
                    1 + i,
                    held_ref.at[1 - core, pl.ds(4 + 4 * i, 4)],
                    later_ref.at[pl.ds(4 * i, 4)],
                    targets[i],
                )
                for i in range(3)
            ]
        where = 1 - core if stage == 1 else core
        if is_last(unit):
            sent, landing, count = SEND_AT[3], LAND_AT[3], 4
        else:
            sent, landing, count = SEND_AT[stage], land_at(axes, stage), remaining(axes, stage)
            if axes[stage - 1] != 2:
                half_count = count // 2
                return [
                    remote(
                        unit,
                        stage,
                        held_ref.at[where, pl.ds(sent, half_count)],
                        later_ref.at[pl.ds(landing, half_count)],
                        plane[axes[stage - 1]],
                    )
                ]
        count //= 4
        return [
            remote(
                unit,
                4 + i,
                held_ref.at[where, pl.ds(sent + (z + 1 + i) % 4 * count, count)],
                later_ref.at[pl.ds(landing + i * count, count)],
                along_z[i],
            )
            for i in range(3)
        ]

    def start(unit, stage, axes):
        for copy in transfers(unit, stage, axes):
            copy.start()

    def finish(unit, stage, axes):
        for copy in transfers(unit, stage, axes):
            copy.wait()

    def down_send(j, unit):
        place = (j - z + 3) % 4
        return [
            remote(
                unit,
                4 + place,
                u_ref.at[unit, core, pl.ds(SEND_AT[3], 4)],
                rz_ref.at[place],
                {"dp": 2 * j + y},
            )
        ]

    def add_up(unit, stage, axes):
        held_ref, first_ref, later_ref = buffer(unit)
        count, piece = arrived(unit, stage, axes)
        following = 3 if is_last(unit) and stage == 1 else stage + 1
        sent, where = SEND_AT[following], 1 - core if following == 1 else core
        if is_last(unit) and stage == 0:

            @pl.loop(0, 16)
            def _(i):
                held_ref[1 - core, i] = piece(i).astype(BF16)

        elif is_last(unit) or axes[following - 1] == 2:

            @pl.loop(0, count)
            def _(i):
                value = piece(i).astype(BF16)
                held_ref[1 - core, i] = value
                held_ref[where, sent + i] = value

        else:

            @pl.loop(0, count // 2)
            def _(i):
                stays, goes = piece(i), piece(count // 2 + i)
                held_ref[1 - core, i] = stays.astype(BF16)
                held_ref[where, sent + i] = goes.astype(BF16)

    def go_on(unit, stage, axes):
        following = 3 if is_last(unit) and stage == 1 else stage + 1
        if following == 3 and is_down(unit):
            chunk = unit - down

            @pl.when(z != chunk)
            def _():
                for copy in down_send(chunk, unit):
                    copy.start()

        else:
            start(unit, following, axes)

    def total(unit, axes):
        finish(unit, 3, axes)
        _, piece = arrived(unit, 3, axes)
        return piece(0) * factor

    def store_unit(unit, value, first=0, chunk=False):
        held_ref, lanes = buffer(unit)[0], value.shape[1]
        for n in range(32):
            piece, side = (4 * (n // 8) + n % 4, n // 4 % 2) if chunk else (n // 2, n % 2)
            held_ref[side, piece, :, first : first + lanes] = value[n * per : (n + 1) * per].astype(BF16)

    def vector_copy(late, n):
        ref, recv = (vl_ref, vlrecv_ref) if late else (ve_ref, verecv_ref)
        if late:
            target = ([partner_core, partner_x, partner_y, partner_xy] + along_z)[n]
        else:
            target = ([partner_core, partner_x, partner_y] + along_z)[n]
        return pltpu.make_async_remote_copy(
            src_ref=ref,
            dst_ref=recv.at[n],
            send_sem=v_send_sem.at[late, n],
            recv_sem=v_recv_sem.at[late, n],
            device_id=target,
            device_id_type=mesh_ids,
        )

    STEPS = (((0,), (1,), (2,), (3, 4, 5)), ((0,), (1, 2, 3), (4, 5, 6)))

    def vector_wait(late, n):
        for i in STEPS[late][n - 1] if n else ():
            vector_copy(late, i).wait()

    def vector_add(late, n):
        ref, recv = (vl_ref, vlrecv_ref) if late else (ve_ref, verecv_ref)
        for i in STEPS[late][n - 1] if n else ():
            ref[...] += recv[i]

    def vector_go_on(late, n):
        for i in STEPS[late][n] if n < len(STEPS[late]) else ():
            vector_copy(late, i).start()

    orders, in_chunk, after_mlp, in_pair, after_proj, tail = plan

    def run(events):
        for unit, stage in events:
            if unit == "give":
                for copy in give(*((layer_out_ref, 0), (in_grad_ref, 1))[stage]):
                    copy.start()
            elif unit in ("early", "late"):
                late = int(unit == "late")
                vector_wait(late, stage)
                vector_add(late, stage)
                vector_go_on(late, stage)
            else:
                finish(unit, stage, orders[unit])
                add_up(unit, stage, orders[unit])
                go_on(unit, stage, orders[unit])

    load(1).wait()
    middle = x_ref[...].astype(F32) + dot(ctx_ref[...], wo_ref[...]) + par_ref[0:1, :]
    mid_ref[...] = middle
    unit_mid, _ = normalize(middle)
    n2_ref[...] = (unit_mid * par_ref[1:2, :] + par_ref[2:3, :]).astype(BF16)
    acc_ref[...] = middle + par_ref[3:4, :]
    dn_ref[...] = jnp.zeros_like(dn_ref)
    vl_ref[...] = jnp.zeros_like(vl_ref)
    load(2).wait()
    rows_copy(1).wait()
    rows_copy(3).wait()

    def chunk_events(j, where):
        for n in range(steps):
            if in_chunk[n][where]:

                @pl.when(j == n)
                def _(n=n):
                    run(in_chunk[n][where])

    @pl.loop(0, steps)
    def _(j):
        slot = j % 2
        for copy in weights(j, slot):
            copy.wait()

        @pl.when(j + 1 < steps)
        def _():
            for copy in weights(j + 1, 1 - slot):
                copy.start()

        normed = n2_ref[...]
        grad_low = g_ref[...]
        wu, wd = w_ref.at[slot], w_ref.at[2 + slot]
        pre = dot(normed, wu[...]) + par_ref[pl.ds(8 + j, 1), :]
        phi = 0.5 * (1.0 + lax.erf(pre * math.sqrt(0.5)))
        hidden = (pre * phi).astype(BF16)
        slope = phi + pre * (jnp.exp(-0.5 * pre * pre) * (1.0 / math.sqrt(2 * math.pi)))
        chunk_events(j, 0)
        acc_ref[...] += dot(hidden, wd[...])
        store_unit(down + j, dot(hidden, grad_low, 0, 0), chunk=True)
        grad_pre = dot(grad_low, wd[...], 1, 1) * slope
        ve_ref[pl.ds(4 + j, 1), :] = column_sum(grad_pre)
        gpre_low = grad_pre.astype(BF16)
        chunk_events(j, 1)
        store_unit(up + j, dot(normed, gpre_low, 0, 0))
        dn_ref[...] += dot(gpre_low, wu[...], 1, 1)
        start(down + j, 0, orders[down])
        start(up + j, 0, orders[up])
        chunk_events(j, 2)

    for i in range(3):
        proj_weights(i).start()
    res_ref[0] = acc_ref[...].astype(BF16)

    def give(ref, n):
        mine_copy = pltpu.make_async_copy(res_ref.at[n, pl.ds(0, half)], ref.at[mine], io_sem.at[n])
        other_copy = pltpu.make_async_remote_copy(
            src_ref=res_ref.at[n, pl.ds(half, half)],
            dst_ref=ref.at[mine],
            send_sem=io_send_sem.at[n],
            recv_sem=io_recv_sem.at[n],
            device_id=partner_x,
            device_id_type=mesh_ids,
        )
        return mine_copy, other_copy

    unit_mid, scale = normalize(mid_ref[...])
    dn = dn_ref[...]
    grad = g_ref[...].astype(F32)
    gmid = grad + normalize_back(unit_mid, scale, par_ref[1:2, :], dn)
    ve_ref[0:1, :] = column_sum(gmid)
    ve_ref[1:2, :] = column_sum(dn * unit_mid)
    ve_ref[2:3, :] = column_sum(dn)
    ve_ref[3:4, :] = column_sum(grad)
    acc_ref[...] = gmid
    low = gmid.astype(BF16)
    store_unit(out, dot(ctx_ref[...], low, 0, 0))
    gctx_ref[...] = dot(low, wo_ref[...], 1, 1).astype(BF16)
    start(out, 0, orders[out])
    dn_ref[...] = jnp.zeros_like(dn_ref)
    run(after_mlp)

    third = 2 * pair_width

    def exchange(p):
        return pltpu.make_async_remote_copy(
            src_ref=dsend_ref.at[p % 3],
            dst_ref=drecv_ref.at[p],
            send_sem=dk_send_sem.at[p],
            recv_sem=dk_recv_sem.at[p],
            device_id=partner_core,
            device_id_type=mesh_ids,
        )

    def project(pairs, unit):
        span = len(pairs) * pair_width
        for i, p in enumerate(pairs):
            exchange(p).wait()
            lane = slice(p * pair_width, (p + 1) * pair_width)
            here = slice(i * pair_width, (i + 1) * pair_width)
            for n in range(2):
                grad = down_ref[p % 3, n] + drecv_ref[p, n].astype(F32)
                if n == 1:
                    vl_ref[3:4, lane] = column_sum(grad)
                dg_ref[1 + n, :, here] = grad.astype(BF16)
            dg_ref[0, :, here] = dq_of(p)
        cols = slice(pairs[0] * pair_width, pairs[0] * pair_width + span)
        for n in range(3):
            store_unit(unit, dot(n1_ref[...], dg_ref[n, :, :span], 0, 0), n * span)
        more = dot(dg_ref[0, :, :span], w_ref[0, :, cols], 1, 1)
        for n in range(1, 3):
            more = more + dot(dg_ref[n, :, :span], w_ref[n, :, cols], 1, 1)
        dn_ref[...] += more
        start(unit, 0, orders[unit])

    def dq_of(p):
        return dg_ref[3, :, (p % 3) * pair_width : (p % 3 + 1) * pair_width]

    def attention_pair(p, slot, third_slot, between):
        attention_load(p, slot).wait()
        lanes = pl.ds(pl.multiple_of(p * pair_width, pair_width), pair_width)
        keys = jnp.concatenate([kv_ref[0, :, lanes], kvo_ref[0, :, lanes]], axis=0)
        values = jnp.concatenate([kv_ref[1, :, lanes], kvo_ref[1, :, lanes]], axis=0)
        queries = q_ref[:, lanes]
        gctx = gctx_ref[:, lanes]
        dq, dk, dv = [], [], []
        for head, grad in enumerate(halves(gctx)):
            att = att_ref[slot, head]
            wide = att.astype(F32)
            datt = dot(grad, values, 1, 1)
            inner = jnp.sum(wide * datt, axis=-1, keepdims=True)
            dscore = (wide * (datt - inner)).astype(BF16)
            dq.append(dot(dscore, keys))
            dk.append(dot(dscore, queries, 0, 0))
            dv.append(dot(att, gctx, 0, 0))
            if head == 0:
                between()
        dquery = join(*dq) * 0.125
        dg_ref[3, :, pl.ds(pl.multiple_of(third_slot * pair_width, pair_width), pair_width)] = dquery.astype(BF16)
        vl_ref[2:3, lanes] = column_sum(dquery)
        for n, grad in enumerate((join(*dk), join(*dv))):
            down_ref[third_slot, n] = grad[:rows]
            dsend_ref[third_slot, n] = grad[rows:].astype(BF16)
        exchange(p).start()

    def pairs_loop(first, count):
        def pair_events(i, where):
            for n in range(count):
                if in_pair[first + n][where]:

                    @pl.when(i == n)
                    def _(n=n):
                        run(in_pair[first + n][where])

        @pl.loop(0, count)
        def _(i):
            p = first + i
            attention_pair(p, p % 2, p % 3, lambda: pair_events(i, 0))

            @pl.when(p + 2 < HEADS // 2)
            def _():
                attention_load(p + 2, p % 2).start()

            pair_events(i, 1)

    pairs_loop(0, 3)
    for i in range(3):
        proj_weights(i).wait()
    project((0, 1), qkv)
    run(after_proj[0])
    pairs_loop(3, 2)
    project((2, 3), qkv + 1)
    run(after_proj[1])
    pairs_loop(5, 1)
    project((4,), last - 1)
    run(after_proj[2])
    project((5,), last)
    run(after_proj[3])

    unit_in, scale = normalize(x_ref[...].astype(F32))
    dn = dn_ref[...]
    vl_ref[0:1, :] = column_sum(dn * unit_in)
    vl_ref[1:2, :] = column_sum(dn)
    vector_go_on(1, 0)
    res_ref[1] = (acc_ref[...] + normalize_back(unit_in, scale, par_ref[4:5, :], dn)).astype(BF16)
    run(tail)

    me = dp * lax.axis_size("seq") + seq
    both = jnp.concatenate([ve_ref[...], vl_ref[...]], axis=0) * factor
    turned = pltpu.roll(both, (width - me * per) % width, 1)
    small_ref[...] = turned[:, : small_ref.shape[1]]
    per_up = steps * per
    row = (me * per_up) // width
    up_bias = jnp.broadcast_to(ve_ref[pl.ds(4 + row, 1), :] * factor, (8, width))
    shift = (width - (me * per_up - row * width)) % width
    upb_ref[...] = pltpu.roll(up_bias, shift, 1)[:, : upb_ref.shape[1]]

    for j in range(steps):
        dup_ref[:, j * width : (j + 1) * width] = total(up + j, orders[up + j])
    for j in range(steps):

        @pl.when(z == j)
        def _(j=j):
            for i in range(3):
                remote(down + j, 4 + i, rz_ref.at[i], rz_ref.at[i], along_z[i]).wait_recv()
            for part in range(steps):
                value = u_ref[down + j, 1 - core, part].astype(F32)
                for i in range(3):
                    value = value + rz_ref[i, part].astype(F32)
                ddown_ref[part * per : (part + 1) * per, :] = value * factor

        @pl.when(z != j)
        def _(j=j):
            for copy in down_send(j, down + j):
                copy.wait_send()

    dout_ref[...] = total(out, orders[out])
    for pairs, unit in (((0, 1), qkv), ((2, 3), qkv + 1), ((4,), last - 1), ((5,), last)):
        value = total(unit, orders[unit])
        span = len(pairs) * pair_width
        for n in range(3):
            at = n * width + pairs[0] * pair_width
            dqkv_ref[:, at : at + span] = value[:, n * span : (n + 1) * span]
    for n, ref in enumerate((layer_out_ref, in_grad_ref)):
        for copy in give(ref, n):
            copy.wait()

def results_kernel(small_ref, upb_ref, *refs):
    count = (len(refs) - 11) // 3
    big_in, outs, vectors, rooms = refs[:count], refs[count : 2 * count], refs[2 * count : -2 - count], refs[-2 - count : -2]
    in_sem, out_sem = refs[-2:]
    reads = [pltpu.make_async_copy(big_in[i], rooms[i], in_sem.at[i]) for i in range(count)]
    writes = [pltpu.make_async_copy(rooms[i], outs[i], out_sem.at[i]) for i in range(count)]
    for copy in reads:
        copy.start()
    for i, row in enumerate((8, 9, 10, 11, 0, 1, 2, 3)):
        vectors[i][...] = small_ref[row : row + 1, : vectors[i].shape[1]]
    vectors[8][...] = upb_ref[0:1, : vectors[8].shape[1]]
    for read, write in zip(reads, writes):
        read.wait()
        write.start()
    for copy in writes:
        copy.wait()


PLAN = (((1, 2, 0), (1, 2, 0), (0, 2, 1), (1, 2, 0), (0, 1, 2), (0, 1, 2), (0, 1, 2), (1, 0, 2), (0, 1, 2), (1, 0, 2), (1, 0, 2), (0, 1, 2), (0, 1, 2)), (((), (), ()), ((), (), ((0, 0), (4, 0))), ((), (), ((1, 0), (5, 0))), ((), (), ((2, 0), (6, 0), (0, 1), (4, 1)))), (('early', 0), (3, 0), (7, 0), (1, 1), (5, 1), ('early', 1)), (((), ((8, 0), (4, 2), (0, 2), (2, 1))), ((), ()), ((), ((3, 1), (1, 2))), ((), ((9, 0), (5, 2))), ((), ((8, 1), (6, 2), ('early', 3), ('give', 0))), ((), ((10, 0), (9, 1)))), (((6, 1), ('early', 2), (7, 1)), ((2, 2), (7, 2)), ((3, 2), (8, 2)), ((11, 0),)), ((9, 2), (12, 0), ('late', 1), (10, 1), ('early', 4), (11, 1), (12, 1), ('late', 2), ('give', 1), (11, 2), (10, 2), ('late', 3)))


def on_device(
    layer_in,
    out_grad,
    pre_gain,
    pre_bias,
    qkv_w,
    q_bias,
    v_bias,
    out_w,
    out_b,
    mid_gain,
    mid_bias,
    up_w,
    up_b,
    down_w,
    down_b,
    patch_keep,
    text_len,
):
    seq_here, half, width = layer_in.shape
    dp, seq = lax.axis_size("dp"), lax.axis_size("seq")
    assert seq_here == 2 and seq == 4
    full = half * seq
    rows = 2 * half
    ff = up_w.shape[1]
    steps = ff // width
    devices = dp * seq
    place_seq = lax.axis_index("seq")
    me = lax.axis_index("dp") * seq + place_seq
    mine, core = place_seq // 2, place_seq % 2

    bits = devices.bit_length() - 1
    halving = (dp, seq) == (8, 4) and width % (8 * devices) == 0
    if halving:
        shards, at_me, at_core = devices, me, core
        dp_bits = list(range(2, bits))
        order_x = [1] + dp_bits
        order_y = dp_bits[:1] + [1] + dp_bits[1:]
        order_z = dp_bits[1:] + [1] + dp_bits[:1]
    else:
        shards, at_me, at_core = 32, 0, 0
        order_x = order_y = order_z = [4, 3, 2, 1]
    per = width // shards
    per_down = ff // shards
    pairs = shards // 2
    info = jnp.stack(
        [
            jnp.asarray(v, jnp.int32)
            for v in (
                mine,
                at_core,
                place(at_me >> 1, order_x),
                place(at_me >> 1, order_y),
                place(at_me >> 1, order_z),
                me,
            )
        ]
    )

    def swap(value, bit):
        if bit < 2:
            return lax.ppermute(value, "seq", [(i, i ^ (1 << bit)) for i in range(seq)])
        return lax.ppermute(value, "dp", [(i, i ^ (1 << (bit - 2))) for i in range(dp)])

    row = lambda v: v.reshape(-1, width)
    own_rows = pl.BlockSpec((1, half, width), lambda i, info: (info[0], 0, 0))
    vec = fixed((1, width))
    act = fixed((rows, width))

    factor = 1.0 / math.sqrt(seq_here * full * dp)
    per_vec, per_up = width // devices, ff // devices
    if halving:
        hbm = pl.BlockSpec(memory_space=pl.ANY)
        units = 2 * steps + 4
        big = lambda *shape: pltpu.VMEM(shape, F32)
        low = lambda *shape: pltpu.VMEM(shape, BF16)
        dma = lambda *shape: pltpu.SemaphoreType.DMA(shape)
        operands = (layer_in, out_grad, qkv_w, out_w, up_w, down_w)
        vectors = (out_b, mid_gain, mid_bias, down_b, pre_gain, pre_bias, q_bias, v_bias, up_b, patch_keep)
        results = [(per, ff), (per_down, width), (per, width), (per, 3 * width), (16, 128), (8, 128)]
        *large, small, up_bias, _ = pl.pallas_call(
            functools.partial(back_kernel, factor, PLAN),
            in_specs=[hbm] * len(operands)
            + [fixed(v.shape) for v in vectors]
            + [pl.BlockSpec(memory_space=pltpu.SMEM)],
            out_shape=[shape_of(layer_in.shape, BF16)] * 2 + [shape_of(s, F32) for s in results]
            + [shape_of((HEADS, rows, full), BF16)],
            out_specs=[hbm] * 2 + [fixed(s) for s in results] + [hbm],
            scratch_shapes=[
                big(16, width),
                big(8, pl.cdiv(full, 128) * 128),
                low(rows, width),
                low(rows, width),
                low(rows, width),
                low(rows, width),
                low(rows, width),
                low(2, rows, width),
                low(2, rows, width),
                low(2, 2, rows, full),
                low(width, width),
                low(4, width, width),
                big(rows, width),
                big(rows, width),
                big(rows, width),
                low(rows, width),
                low(rows, width),
                low(4, rows, 6 * HEAD_DIM),
                big(3, 2, rows, 2 * HEAD_DIM),
                low(3, 2, rows, 2 * HEAD_DIM),
                low(6, 2, rows, 2 * HEAD_DIM),
                low(2, rows, width),
                big(8, width),
                big(8, width),
                big(6, 8, width),
                big(7, 8, width),
                low(units - 1, 2, 16, per, width),
                low(units - 1, 16, per, width),
                low(units - 1, 16, per, width),
                low(2, 2, 16, per, width // 2),
                low(2, 16, per, width // 2),
                low(2, 16, per, width // 2),
                low(3, steps, per, width),
                dma(3),
                dma(7),
                dma(4),
                dma(units + 1, 7),
                dma(units + 1, 7),
                dma(6),
                dma(6),
                dma(2, 7),
                dma(2, 7),
                dma(2),
                dma(2),
                dma(2),
                dma(4),
                dma(4),
                dma(4),
                dma(4),
            ],
            compiler_params=pltpu.CompilerParams(
                vmem_limit_bytes=64 * 1024 * 1024, collective_id=0, has_side_effects=True
            ),
        )(*operands, *vectors, text_len)
        vec_shapes = [(1, per_vec)] * 8 + [(1, per_up)]
        whole = pl.pallas_call(
            results_kernel,
            in_specs=[pl.BlockSpec(memory_space=pltpu.VMEM)] * 2 + [hbm] * len(large),
            out_shape=[shape_of(v.shape, v.dtype) for v in large] + [shape_of(s, F32) for s in vec_shapes],
            out_specs=[hbm] * len(large) + [pl.BlockSpec(memory_space=pltpu.VMEM)] * len(vec_shapes),
            scratch_shapes=[pltpu.VMEM(v.shape, v.dtype) for v in large] + [dma(len(large)), dma(len(large))],
        )(small, up_bias, *large)
        layer_out, in_grad, d_wup, d_wdown, d_wout, d_qkv = whole[:6]
        d_pregain, d_prebias, d_qbias, d_vbias, d_outbias, d_midgain, d_midbias, d_downbias, d_upbias = (
            v.reshape(-1) for v in whole[6:]
        )
        return (
            layer_out,
            in_grad,
            d_pregain,
            d_prebias,
            d_qkv,
            d_qbias,
            d_vbias,
            d_wout,
            d_outbias,
            d_midgain,
            d_midbias,
            d_wup,
            d_upbias,
            d_wdown,
            d_downbias,
        )

    x_other = swap(lax.dynamic_index_in_dim(layer_in, 1 - mine, 0, False), 1)
    g_other = swap(lax.dynamic_index_in_dim(out_grad, 1 - mine, 0, False), 1)

    patches = lax.dynamic_index_in_dim(patch_keep, mine, 0, False)
    length = lax.dynamic_index_in_dim(text_len, mine, 0, False)
    valid = jnp.concatenate(
        [
            jnp.ones((2,), jnp.int32),
            patches,
            jnp.ones((1,), jnp.int32),
            (jnp.arange(TEXT, dtype=jnp.int32) < length).astype(jnp.int32),
            jnp.zeros((full - 3 - PATCHES - TEXT,), jnp.int32),
        ]
    )
    valid = valid.reshape(seq, half)
    valid = jnp.concatenate(
        [lax.dynamic_index_in_dim(valid, place_seq ^ turn, 0, True) for turn in (0, 2, 1, 3)], axis=1
    )
    mask = jnp.where(valid > 0, 0.0, -1e30).astype(F32)

    square = 2 * rows * width * width
    kv_bias = jnp.concatenate([jnp.zeros((1, 1, width), F32), v_bias.reshape(1, 1, width)], axis=0)
    n1, kv = call(
        qkv_kernel,
        (2,),
        [
            own_rows,
            fixed((half, width)),
            vec,
            vec,
            pl.BlockSpec((width, width), lambda i, _: (0, i + 1)),
            pl.BlockSpec((1, 1, width), lambda i, _: (i, 0, 0)),
        ],
        [shape_of((rows, width), BF16), shape_of((2, rows, width), BF16)],
        [act, pl.BlockSpec((1, rows, width), lambda i, _: (i, 0, 0))],
        flops=2 * square,
        nbytes=5 * 10**6,
    )(info, layer_in, x_other, row(pre_gain), row(pre_bias), qkv_w, kv_bias)
    kv_other = swap(kv, 0)
    q = call(
        query_kernel,
        (1,),
        [act, pl.BlockSpec((width, width), lambda i, _: (0, 0)), vec],
        shape_of((rows, width), BF16),
        act,
        flops=square,
        nbytes=3 * 10**6,
    )(info, n1, qkv_w, row(q_bias))

    pair_width = 2 * HEAD_DIM
    blocks = width // pair_width
    col = pl.BlockSpec((rows, pair_width), lambda i, _: (0, i))
    col2 = pl.BlockSpec((2, rows, pair_width), lambda i, _: (0, 0, i))
    att_spec = pl.BlockSpec((2, rows, full), lambda i, _: (i, 0, 0))
    head_flops = 2 * rows * full * pair_width * HEADS
    ctx, att = call(
        attention_kernel,
        (blocks,),
        [col, col2, col2, fixed((1, full))],
        [shape_of((rows, width), BF16), shape_of((HEADS, rows, full), BF16)],
        [col, att_spec],
        flops=4 * head_flops,
        nbytes=12 * 10**6,
        trans=HEADS * rows * full,
    )(info, q, kv, kv_other, mask)

    orders = (order_x, order_y, order_z)
    mlp_out = call(
        functools.partial(mlp_kernel, orders, per, per_down, steps),
        (steps,),
        [
            own_rows,
            fixed((half, width)),
            own_rows,
            fixed((half, width)),
            act,
            fixed((width, width)),
            vec,
            vec,
            vec,
            pl.BlockSpec((width, width), lambda i, _: (0, i)),
            pl.BlockSpec((1, 1, width), lambda i, _: (i, 0, 0)),
            pl.BlockSpec((width, width), lambda i, _: (i, 0)),
            vec,
        ],
        [
            shape_of((half, width), BF16),
            shape_of((half, width), BF16),
            shape_of((rows, width), F32),
            shape_of((rows, width), BF16),
            shape_of((4 + steps, width), F32),
            shape_of((pairs, steps, per, width), BF16),
            shape_of((pairs, steps, per, width), F32),
            shape_of((pairs, per_down, width), BF16),
            shape_of((pairs, per_down, width), F32),
            shape_of((pairs, per, width), BF16),
            shape_of((pairs, per, width), F32),
        ],
        [
            fixed((half, width)),
            fixed((half, width)),
            act,
            act,
            fixed((4 + steps, width)),
            pl.BlockSpec((pairs, 1, per, width), lambda i, _: (0, i, 0, 0)),
            pl.BlockSpec((pairs, 1, per, width), lambda i, _: (0, i, 0, 0)),
            fixed((pairs, per_down, width)),
            fixed((pairs, per_down, width)),
            fixed((pairs, per, width)),
            fixed((pairs, per, width)),
        ],
        scratch=[
            pltpu.VMEM((rows, width), F32),
            pltpu.VMEM((rows, width), BF16),
            pltpu.VMEM((rows, width), F32),
            pltpu.VMEM((rows, width), F32),
            pltpu.VMEM((width, width), F32),
        ],
        flops=(6 * steps + 3) * square,
        nbytes=40 * 10**6,
        trans=2 * rows * ff,
    )(
        info,
        layer_in,
        x_other,
        out_grad,
        g_other,
        ctx,
        out_w,
        row(out_b),
        row(mid_gain),
        row(mid_bias),
        up_w,
        up_b.reshape(steps, 1, width),
        down_w,
        row(down_b),
    )
    out_own, out_other, gmid, gctx, early, s_up, k_up, s_down, k_down, s_out, k_out = mlp_out
    out_back = swap(out_other, 1)

    def reduce(sent, kept, order):
        got = swap(sent, 0)
        for bit in order:
            total = kept + got.astype(F32)
            cut = total.shape[0] // 2
            kept = total[:cut]
            got = swap(total[cut:].astype(BF16), bit)
        return kept, got

    def natural(sent, kept):
        return jnp.stack([kept, sent.astype(F32)], axis=1)

    if halving:
        up_pair = reduce(s_up, k_up, order_x)
        down_pair = reduce(s_down, k_down, order_y)
        out_pair = reduce(s_out, k_out, order_z)

    dq, dbq, dkv_own, dkv_send = call(
        attention_back_kernel,
        (blocks,),
        [att_spec, col, col2, col2, col],
        [
            shape_of((rows, width), BF16),
            shape_of((1, width), F32),
            shape_of((2, rows, width), F32),
            shape_of((2, rows, width), BF16),
        ],
        [col, pl.BlockSpec((1, pair_width), lambda i, _: (0, i)), col2, col2],
        flops=8 * head_flops,
        nbytes=16 * 10**6,
    )(info, att, q, kv, kv_other, gctx)
    dkv_other = swap(dkv_send, 0)
    shard = fixed((pairs, per, width))
    tile = pltpu.VMEM((width, width), F32)
    dn_q, s_q, k_q = call(
        functools.partial(query_back_kernel, order_x, per),
        (1,),
        [act, act, pl.BlockSpec((width, width), lambda i, _: (0, 0))],
        [shape_of((rows, width), F32), shape_of((pairs, per, width), BF16), shape_of((pairs, per, width), F32)],
        [act, shard, shard],
        scratch=[tile],
        flops=2 * square,
        nbytes=6 * 10**6,
    )(info, n1, dq, qkv_w)
    dkv, dbv, s_k, k_k, s_v, k_v = call(
        functools.partial(key_value_back_kernel, (order_x, order_y), per),
        (1,),
        [act, fixed((2, rows, width)), fixed((2, rows, width))],
        [
            shape_of((2, rows, width), BF16),
            shape_of((1, width), F32),
            shape_of((pairs, per, width), BF16),
            shape_of((pairs, per, width), F32),
            shape_of((pairs, per, width), BF16),
            shape_of((pairs, per, width), F32),
        ],
        [fixed((2, rows, width)), vec, shard, shard, shard, shard],
        scratch=[tile],
        flops=2 * square,
        nbytes=10 * 10**6,
    )(info, n1, dkv_own, dkv_other)
    if halving:
        q_pair = reduce(s_q, k_q, order_x)
        k_pair = reduce(s_k, k_k, order_x)
        v_pair = reduce(s_v, k_v, order_y)
    in_own, in_other, late = call(
        input_back_kernel,
        (1,),
        [
            own_rows,
            fixed((half, width)),
            vec,
            fixed((2, rows, width)),
            fixed((width, 3 * width)),
            act,
            act,
            vec,
            vec,
        ],
        [shape_of((half, width), BF16), shape_of((half, width), BF16), shape_of((8, width), F32)],
        [fixed((half, width)), fixed((half, width)), fixed((8, width))],
        flops=2 * square,
        nbytes=10 * 10**6,
    )(info, layer_in, x_other, row(pre_gain), dkv, qkv_w, dn_q, gmid, dbq, dbv)
    in_back = swap(in_other, 1)

    def give_back(own, other):
        first = jnp.where(mine == 0, own, other)
        second = jnp.where(mine == 0, other, own)
        return jnp.stack([first, second])

    layer_out = give_back(out_own, out_back)
    in_grad = give_back(in_own, in_back)

    factor = 1.0 / math.sqrt(seq_here * full * dp)
    vectors = jnp.concatenate([early, late], axis=0)
    if halving:
        for bit in range(bits):
            vectors = vectors + swap(vectors, bit)
    else:
        vectors = lax.psum(vectors, ("dp", "seq"))
    per_vec, per_up = width // devices, ff // devices
    early_rows = 4 + steps
    small, up_bias = call(
        functools.partial(vector_kernel, factor, per_vec, per_up),
        (1,),
        [
            pl.BlockSpec((early_rows, width), lambda i, _: (0, 0)),
            pl.BlockSpec((8, width), lambda i, _: (early_rows // 8, 0)),
        ],
        [shape_of((early_rows + 8, 128), F32), shape_of((8, 128), F32)],
        [fixed((early_rows + 8, 128)), fixed((8, 128))],
    )(info, vectors, vectors)
    pick = lambda i: small[i, :per_vec]
    d_upbias = up_bias[0, :per_up]
    d_outbias, d_midgain, d_midbias, d_downbias = (pick(i) for i in range(4))
    d_pregain, d_prebias, d_qbias, d_vbias = (pick(early_rows + i) for i in range(4))

    if halving:

        def finish(named):
            operands = [v for pair, _ in named for v in pair]
            shapes = [s for _, s in named]
            return call(
                functools.partial(finish_kernel, factor),
                (1,),
                [fixed(v.shape) for v in operands],
                [shape_of(s, F32) for s in shapes],
                [fixed(s) for s in shapes],
            )(info, *operands)

        d_wup, d_wdown, d_wout = finish(
            [(up_pair, (per, ff)), (down_pair, (per_down, width)), (out_pair, (per, width))]
        )
        d_q, d_k, d_v = finish([(pair, (per, width)) for pair in (q_pair, k_pair, v_pair)])
        d_qkv = jnp.concatenate([d_q, d_k, d_v], axis=1)
    else:

        def scatter(value):
            return lax.psum_scatter(value, ("dp", "seq"), scatter_dimension=0, tiled=True) * factor

        d_wup = scatter(
            natural(s_up, k_up).transpose(0, 1, 3, 2, 4).reshape(width, ff)
        )
        d_wdown = scatter(natural(s_down, k_down).reshape(ff, width))
        d_wout = scatter(natural(s_out, k_out).reshape(width, width))
        d_qkv = scatter(
            jnp.concatenate(
                [natural(s, k).reshape(width, width) for s, k in ((s_q, k_q), (s_k, k_k), (s_v, k_v))],
                axis=1,
            )
        )
    return (
        layer_out,
        in_grad,
        d_pregain,
        d_prebias,
        d_qkv,
        d_qbias,
        d_vbias,
        d_wout,
        d_outbias,
        d_midgain,
        d_midbias,
        d_wup,
        d_upbias,
        d_wdown,
        d_downbias,
    )


def solution(mesh):
    both = ("dp", "seq")
    rows = P("dp", "seq", None)
    return jax.shard_map(
        on_device,
        mesh=mesh,
        in_specs=(rows, rows) + (P(),) * 13 + (P("dp", None), P("dp")),
        out_specs=(
            rows,
            rows,
            P(both),
            P(both),
            P(both, None),
            P(both),
            P(both),
            P(both, None),
            P(both),
            P(both),
            P(both),
            P(both, None),
            P(both),
            P(both, None),
            P(both),
        ),
        check_vma=False,
    )
```

```python
import functools
import math

import jax
import jax.numpy as jnp
from jax import lax
from jax.experimental import pallas as pl
from jax.experimental.pallas import tpu as pltpu
from jax.sharding import PartitionSpec as P

HEADS = 12
HEAD_DIM = 64
PATCHES = 196
TEXT = 512
F32 = jnp.float32
BF16 = jnp.bfloat16
VMEM_BYTES = 60 * 1024 * 1024


def dot(lhs, rhs, lhs_dim=1, rhs_dim=0):
    return lax.dot_general(
        lhs, rhs, (((lhs_dim,), (rhs_dim,)), ((), ())), preferred_element_type=F32
    )


def normalize(values):
    center = values - jnp.mean(values, axis=-1, keepdims=True)
    spread = jnp.mean(center * center, axis=-1, keepdims=True)
    scale = lax.rsqrt(spread + 1e-06)
    return center * scale, scale


def normalize_back(unit, scale, gain, cotangent):
    inner = cotangent * gain
    mean_inner = jnp.mean(inner, axis=-1, keepdims=True)
    mean_unit = jnp.mean(inner * unit, axis=-1, keepdims=True)
    return scale * (inner - mean_inner - unit * mean_unit)


def column_sum(values):
    return jnp.sum(values, axis=0, keepdims=True)


def call(kernel, grid, in_specs, out_shape, out_specs, scratch=(), flops=0, nbytes=0, trans=0):
    return pl.pallas_call(
        kernel,
        grid_spec=pltpu.PrefetchScalarGridSpec(
            num_scalar_prefetch=1,
            grid=grid,
            in_specs=in_specs,
            out_specs=out_specs,
            scratch_shapes=list(scratch),
        ),
        out_shape=out_shape,
        compiler_params=pltpu.CompilerParams(vmem_limit_bytes=VMEM_BYTES),
        cost_estimate=pl.CostEstimate(flops=flops, bytes_accessed=nbytes, transcendentals=trans),
    )


def fixed(shape):
    zeros = (0,) * len(shape)
    return pl.BlockSpec(shape, lambda *_: zeros)


def shape_of(shape, dtype):
    return jax.ShapeDtypeStruct(shape, dtype)


def place(number, order):
    out = 0
    for bit in order:
        out = out * 2 + ((number >> (bit - 1)) & 1)
    return out


def store_shards(tile_ref, send_ref, keep_ref, info_ref, slot, order, rows, pairs, at):
    core = info_ref[1]
    for pair in range(pairs):
        number = pair if at is None else at * pairs + pair
        index = place(number, order) ^ info_ref[slot]
        sent = tile_ref[pl.ds(pl.multiple_of(rows * (2 * pair + 1 - core), 8), rows), :]
        kept = tile_ref[pl.ds(pl.multiple_of(rows * (2 * pair + core), 8), rows), :]
        send_ref[index] = sent.astype(send_ref.dtype).reshape(send_ref.shape[1:])
        keep_ref[index] = kept.reshape(keep_ref.shape[1:])


def qkv_kernel(info_ref, own_ref, other_ref, gain_ref, shift_ref, w_ref, bias_ref, n1_ref, kv_ref):
    @pl.when(pl.program_id(0) == 0)
    def _():
        rows = jnp.concatenate([own_ref[0], other_ref[...]], axis=0).astype(F32)
        unit, _ = normalize(rows)
        n1_ref[...] = (unit * gain_ref[...] + shift_ref[...]).astype(BF16)

    kv_ref[0] = (dot(n1_ref[...], w_ref[...]) + bias_ref[0]).astype(BF16)


def query_kernel(info_ref, n1_ref, w_ref, bias_ref, q_ref):
    q_ref[...] = ((dot(n1_ref[...], w_ref[...]) + bias_ref[...]) * 0.125).astype(BF16)


def halves(value):
    lane = lax.broadcasted_iota(jnp.int32, value.shape, 1)
    zero = jnp.zeros_like(value)
    return jnp.where(lane < HEAD_DIM, value, zero), jnp.where(lane < HEAD_DIM, zero, value)


def join(first, second):
    lane = lax.broadcasted_iota(jnp.int32, first.shape, 1)
    return jnp.where(lane < HEAD_DIM, first, second)


def attention_kernel(info_ref, q_ref, own_ref, other_ref, mask_ref, ctx_ref, att_ref):
    keys = jnp.concatenate([own_ref[0], other_ref[0]], axis=0)
    values = jnp.concatenate([own_ref[1], other_ref[1]], axis=0)
    parts = []
    for head, query in enumerate(halves(q_ref[...])):
        scores = dot(query, keys, 1, 1) + mask_ref[...]
        exponent = jnp.exp(scores - jnp.max(scores, axis=-1, keepdims=True))
        total = jnp.sum(exponent, axis=-1, keepdims=True)
        att = (exponent * (1.0 / total)).astype(BF16)
        att_ref[head] = att
        parts.append(dot(att, values))
    ctx_ref[...] = join(*parts).astype(BF16)


def attention_back_kernel(
    info_ref, att_ref, q_ref, own_ref, other_ref, gctx_ref, dq_ref, dbq_ref, down_ref, dother_ref
):
    keys = jnp.concatenate([own_ref[0], other_ref[0]], axis=0)
    values = jnp.concatenate([own_ref[1], other_ref[1]], axis=0)
    queries = q_ref[...]
    gctx = gctx_ref[...]
    dq, dk, dv = [], [], []
    for head, grad in enumerate(halves(gctx)):
        att = att_ref[head]
        wide = att.astype(F32)
        datt = dot(grad, values, 1, 1)
        inner = jnp.sum(wide * datt, axis=-1, keepdims=True)
        dscore = (wide * (datt - inner)).astype(BF16)
        dq.append(dot(dscore, keys))
        dk.append(dot(dscore, queries, 0, 0))
        dv.append(dot(att, gctx, 0, 0))
    dquery = join(*dq) * 0.125
    dq_ref[...] = dquery.astype(BF16)
    dbq_ref[...] = column_sum(dquery)
    rows = queries.shape[0]
    for i, grad in enumerate((join(*dk), join(*dv))):
        down_ref[i] = grad[:rows]
        dother_ref[i] = grad[rows:].astype(BF16)


def mlp_kernel(
    orders,
    rows_up,
    rows_down,
    steps,
    info_ref,
    x_ref,
    xo_ref,
    g_ref,
    go_ref,
    ctx_ref,
    wo_ref,
    bo_ref,
    gain_ref,
    shift_ref,
    wu_ref,
    bu_ref,
    wd_ref,
    bd_ref,
    out_ref,
    outo_ref,
    gmid_ref,
    gctx_ref,
    vec_ref,
    su_ref,
    ku_ref,
    sd_ref,
    kd_ref,
    so_ref,
    ko_ref,
    mid_ref,
    n2_ref,
    acc_ref,
    dn_ref,
    tile_ref,
):
    step = pl.program_id(0)
    half = xo_ref.shape[0]
    grad_low = jnp.concatenate([g_ref[0], go_ref[...]], axis=0)

    @pl.when(step == 0)
    def _():
        rows = jnp.concatenate([x_ref[0], xo_ref[...]], axis=0).astype(F32)
        middle = rows + dot(ctx_ref[...], wo_ref[...]) + bo_ref[...]
        mid_ref[...] = middle
        unit, _ = normalize(middle)
        n2_ref[...] = (unit * gain_ref[...] + shift_ref[...]).astype(BF16)
        acc_ref[...] = middle + bd_ref[...]
        dn_ref[...] = jnp.zeros_like(dn_ref)

    normed = n2_ref[...]
    pre = dot(normed, wu_ref[...]) + bu_ref[0]
    phi = 0.5 * (1.0 + lax.erf(pre * math.sqrt(0.5)))
    hidden = (pre * phi).astype(BF16)
    slope = phi + pre * (jnp.exp(-0.5 * pre * pre) * (1.0 / math.sqrt(2 * math.pi)))
    acc_ref[...] += dot(hidden, wd_ref[...])
    grad_pre = dot(grad_low, wd_ref[...], 1, 1) * slope
    vec_ref[pl.ds(4 + step, 1), :] = column_sum(grad_pre)
    gpre_low = grad_pre.astype(BF16)
    dn_ref[...] += dot(gpre_low, wu_ref[...], 1, 1)
    tile_ref[...] = dot(normed, gpre_low, 0, 0)
    n_up = tile_ref.shape[0] // (2 * rows_up)
    store_shards(tile_ref, su_ref, ku_ref, info_ref, 2, orders[0], rows_up, n_up, None)
    tile_ref[...] = dot(hidden, grad_low, 0, 0)
    n_down = tile_ref.shape[0] // (2 * rows_down)
    for at in range(steps):

        @pl.when(step == at)
        def _(at=at):
            store_shards(tile_ref, sd_ref, kd_ref, info_ref, 3, orders[1], rows_down, n_down, at)

    @pl.when(step == steps - 1)
    def _():
        result = acc_ref[...].astype(BF16)
        out_ref[...] = result[:half]
        outo_ref[...] = result[half:]
        unit, scale = normalize(mid_ref[...])
        dn = dn_ref[...]
        grad = grad_low.astype(F32)
        gmid = grad + normalize_back(unit, scale, gain_ref[...], dn)
        gmid_ref[...] = gmid
        vec_ref[0:1, :] = column_sum(gmid)
        vec_ref[1:2, :] = column_sum(dn * unit)
        vec_ref[2:3, :] = column_sum(dn)
        vec_ref[3:4, :] = column_sum(grad)
        low = gmid.astype(BF16)
        gctx_ref[...] = dot(low, wo_ref[...], 1, 1).astype(BF16)
        tile_ref[...] = dot(ctx_ref[...], low, 0, 0)
        store_shards(tile_ref, so_ref, ko_ref, info_ref, 4, orders[2], rows_up, n_up, None)


def query_back_kernel(order, rows, info_ref, n1_ref, dq_ref, w_ref, dn_ref, s_ref, k_ref, tile_ref):
    tile_ref[...] = dot(n1_ref[...], dq_ref[...], 0, 0)
    pairs = tile_ref.shape[0] // (2 * rows)
    store_shards(tile_ref, s_ref, k_ref, info_ref, 2, order, rows, pairs, None)
    dn_ref[...] = dot(dq_ref[...], w_ref[...], 1, 1)


def key_value_back_kernel(
    orders, rows, info_ref, n1_ref, own_ref, other_ref, dkv_ref, dbv_ref, sk_ref, kk_ref, sv_ref, kv_ref, tile_ref
):
    pairs = tile_ref.shape[0] // (2 * rows)
    for i, (s_ref, k_ref, slot) in enumerate(((sk_ref, kk_ref, 2), (sv_ref, kv_ref, 3))):
        grad = own_ref[i] + other_ref[i].astype(F32)
        low = grad.astype(BF16)
        dkv_ref[i] = low
        if i == 1:
            dbv_ref[...] = column_sum(grad)
        tile_ref[...] = dot(n1_ref[...], low, 0, 0)
        store_shards(tile_ref, s_ref, k_ref, info_ref, slot, orders[i], rows, pairs, None)


def input_back_kernel(
    info_ref, x_ref, xo_ref, gain_ref, dkv_ref, w_ref, dnq_ref, gmid_ref, dbq_ref, dbv_ref, own_ref, other_ref, vec_ref
):
    half = xo_ref.shape[0]
    dn = dnq_ref[...]
    for i in range(2):
        width = dn.shape[1]
        dn = dn + dot(dkv_ref[i], w_ref[:, (i + 1) * width : (i + 2) * width], 1, 1)
    rows = jnp.concatenate([x_ref[0], xo_ref[...]], axis=0).astype(F32)
    unit, scale = normalize(rows)
    result = (gmid_ref[...] + normalize_back(unit, scale, gain_ref[...], dn)).astype(BF16)
    own_ref[...] = result[:half]
    other_ref[...] = result[half:]
    vec_ref[0:1, :] = column_sum(dn * unit)
    vec_ref[1:2, :] = column_sum(dn)
    vec_ref[2:3, :] = dbq_ref[...]
    vec_ref[3:4, :] = dbv_ref[...]
    vec_ref[4:8, :] = jnp.zeros_like(vec_ref[4:8, :])


def finish_kernel(factor, info_ref, *refs):
    count = len(refs) // 3
    for i in range(count):
        keep, recv, out = refs[2 * i], refs[2 * i + 1], refs[2 * count + i]
        total = (keep[0] + recv[0].astype(F32)) * factor
        if total.ndim == 3:
            width = total.shape[-1]
            for block in range(total.shape[0]):
                out[:, block * width : (block + 1) * width] = total[block]
        else:
            out[...] = total


def vector_kernel(factor, per, per_up, info_ref, early_ref, late_ref, out_ref, up_ref):
    me = info_ref[5]
    width = early_ref.shape[1]
    both = jnp.concatenate([early_ref[...], late_ref[...]], axis=0) * factor
    turned = pltpu.roll(both, lax.rem(width - me * per, width), 1)
    out_ref[...] = turned[:, : out_ref.shape[1]]
    row = (me * per_up) // width
    up = early_ref[pl.ds(4 + row, 1), :] * factor
    up = jnp.broadcast_to(up, (8, width))
    shift = lax.rem(width - (me * per_up - row * width), width)
    up_ref[...] = pltpu.roll(up, shift, 1)[:, : up_ref.shape[1]]


SEND_AT = (0, 8, 0, 8)
LAND_AT = (None, 0, 8, 12)


def differs(bit, mine):
    return bit + mine - 2 * bit * mine


def back_kernel(
    factor,
    plan,
    layer_in_ref,
    out_grad_ref,
    qkv_w_ref,
    out_w_ref,
    up_w_ref,
    down_w_ref,
    out_b_ref,
    mid_gain_ref,
    mid_bias_ref,
    down_b_ref,
    pre_gain_ref,
    pre_bias_ref,
    q_bias_ref,
    v_bias_ref,
    up_b_ref,
    patch_ref,
    length_ref,
    layer_out_ref,
    in_grad_ref,
    dup_ref,
    ddown_ref,
    dout_ref,
    dqkv_ref,
    small_ref,
    upb_ref,
    att_hbm_ref,
    par_ref,
    mask_ref,
    x_ref,
    g_ref,
    ctx_ref,
    n1_ref,
    q_ref,
    kv_ref,
    kvo_ref,
    att_ref,
    wo_ref,
    w_ref,
    mid_ref,
    acc_ref,
    dn_ref,
    n2_ref,
    gctx_ref,
    dg_ref,
    down_ref,
    dsend_ref,
    drecv_ref,
    res_ref,
    ve_ref,
    vl_ref,
    verecv_ref,
    vlrecv_ref,
    u_ref,
    r0_ref,
    r_ref,
    uh_ref,
    r0h_ref,
    rh_ref,
    rz_ref,
    in_sem,
    w_sem,
    att_sem,
    send_sem,
    recv_sem,
    dk_send_sem,
    dk_recv_sem,
    v_send_sem,
    v_recv_sem,
    io_sem,
    io_send_sem,
    io_recv_sem,
    x_send_sem,
    x_recv_sem,
    kv_send_sem,
    kv_recv_sem,
):
    _, half, width = layer_in_ref.shape
    rows = 2 * half
    steps = up_w_ref.shape[1] // width
    dp, seq = lax.axis_index("dp"), lax.axis_index("seq")
    core, mine = seq % 2, seq // 2
    y, z = dp % 2, dp // 2
    bits = (mine, y)
    partner_core = {"seq": seq + 1 - 2 * core}
    partner_x = {"seq": seq + 2 - 4 * mine}
    partner_y = {"dp": dp + 1 - 2 * y}
    partner_xy = {"dp": dp + 1 - 2 * y, "seq": seq + 2 - 4 * mine}
    along_z = [{"dp": (dp + 2 * turn) % 8} for turn in (1, 2, 3)]
    plane = (partner_x, partner_y)
    mesh_ids = pl.DeviceIdType.MESH

    barrier = pltpu.get_barrier_semaphore()
    friends = [partner_core, partner_x, partner_y, partner_xy] + along_z
    for other in friends:
        pl.semaphore_signal(barrier, inc=1, device_id=other, device_id_type=mesh_ids)

    loads = [
        (layer_in_ref.at[mine], x_ref.at[pl.ds(0, half)]),
        (out_w_ref, wo_ref),
        (out_grad_ref.at[mine], g_ref.at[pl.ds(0, half)]),
    ]

    def load(i):
        return pltpu.make_async_copy(loads[i][0], loads[i][1], in_sem.at[i])

    def weights(j, slot):
        at = pl.multiple_of(j * width, width)
        return (
            pltpu.make_async_copy(up_w_ref.at[:, pl.ds(at, width)], w_ref.at[slot], w_sem.at[slot]),
            pltpu.make_async_copy(down_w_ref.at[pl.ds(at, width), :], w_ref.at[2 + slot], w_sem.at[2 + slot]),
        )

    def proj_weights(i):
        return pltpu.make_async_copy(qkv_w_ref.at[:, i * width : (i + 1) * width], w_ref.at[i], w_sem.at[4 + i])

    def attention_load(p, slot):
        return pltpu.make_async_copy(att_hbm_ref.at[pl.ds(2 * p, 2)], att_ref.at[slot], att_sem.at[slot])

    def attention_store(p, slot):
        return pltpu.make_async_copy(att_ref.at[slot], att_hbm_ref.at[pl.ds(2 * p, 2)], att_sem.at[2 + slot])

    load(0).start()
    for i in (1, 2, 0):
        proj_weights(i).start()
    for i in (1, 2):
        load(i).start()

    part = half // 2

    def rows_copy(n):
        source, landing = ((layer_in_ref, x_ref), (out_grad_ref, g_ref))[n % 2]
        return pltpu.make_async_remote_copy(
            src_ref=source.at[1 - mine, pl.ds(n // 2 * part, part)],
            dst_ref=landing.at[pl.ds(half + n // 2 * part, part)],
            send_sem=x_send_sem.at[n],
            recv_sem=x_recv_sem.at[n],
            device_id=partner_x,
            device_id_type=mesh_ids,
        )

    def keys_copy(b):
        at = pl.ds(pl.multiple_of(b * part, 8), part)
        return pltpu.make_async_remote_copy(
            src_ref=kv_ref.at[:, at],
            dst_ref=kvo_ref.at[:, at],
            send_sem=kv_send_sem.at[b],
            recv_sem=kv_recv_sem.at[b],
            device_id=partner_core,
            device_id_type=mesh_ids,
        )

    pl.semaphore_wait(barrier, len(friends))
    for n in (0, 2, 1, 3):
        rows_copy(n).start()
    for i, ref in enumerate(
        (out_b_ref, mid_gain_ref, mid_bias_ref, down_b_ref, pre_gain_ref, pre_bias_ref, q_bias_ref, v_bias_ref)
    ):
        par_ref[i : i + 1, :] = ref[...].reshape(1, width)
    for j in range(steps):
        par_ref[8 + j : 9 + j, :] = up_b_ref[j * width : (j + 1) * width].reshape(1, width)

    full = 4 * half
    chunks = (seq, seq + 2 - 4 * mine, seq + 1 - 2 * core, 3 - seq)
    mask_ref[...] = jnp.zeros_like(mask_ref)
    mask_ref[0:1, 2 : 2 + PATCHES] = patch_ref[pl.ds(mine, 1), :].astype(F32)
    first_chunk = core * 2 + mine
    kept = pltpu.roll(mask_ref[...], first_chunk * half, 1)[:, :full]
    lane = lax.broadcasted_iota(jnp.int32, kept.shape, 1)
    chunk = lane // half
    start_row = jnp.where(chunk < 2, jnp.where(chunk < 1, chunks[0], chunks[1]), jnp.where(chunk < 3, chunks[2], chunks[3]))
    number = start_row * half + lane - chunk * half
    token = number - (3 + PATCHES)
    valid = (
        (kept > 0.5)
        | (number < 2)
        | (number == 2 + PATCHES)
        | ((token >= 0) & (token < TEXT) & (token < length_ref[mine]))
    )
    mask_ref[:, :full] = jnp.where(valid, 0.0, -1e30)

    @pl.loop(0, 4)
    def _(b):
        @pl.when(b == 0)
        def _():
            load(0).wait()
            for i in (1, 2, 0):
                proj_weights(i).wait()

        for n in range(2):

            @pl.when(b == 2 + n)
            def _(n=n):
                rows_copy(2 * n).wait()

        at = pl.ds(pl.multiple_of(b * part, 8), part)
        unit_in, _ = normalize(x_ref[at, :].astype(F32))
        n1_ref[at, :] = (unit_in * par_ref[4:5, :] + par_ref[5:6, :]).astype(BF16)
        kv_ref[0, at, :] = dot(n1_ref[at, :], w_ref[1]).astype(BF16)
        kv_ref[1, at, :] = (dot(n1_ref[at, :], w_ref[2]) + par_ref[7:8, :]).astype(BF16)
        keys_copy(b).start()
        q_ref[at, :] = ((dot(n1_ref[at, :], w_ref[0]) + par_ref[6:7, :]) * 0.125).astype(BF16)

    for copy in weights(0, 0):
        copy.start()
    for b in range(4):
        keys_copy(b).wait()

    @pl.loop(0, HEADS // 2)
    def _(p):
        slot = p % 2
        lanes = pl.ds(pl.multiple_of(p * 2 * HEAD_DIM, 2 * HEAD_DIM), 2 * HEAD_DIM)
        keys = jnp.concatenate([kv_ref[0, :, lanes], kvo_ref[0, :, lanes]], axis=0)
        values = jnp.concatenate([kv_ref[1, :, lanes], kvo_ref[1, :, lanes]], axis=0)

        @pl.when(p >= 2)
        def _():
            attention_store(p - 2, slot).wait()

        parts = []
        for head, query in enumerate(halves(q_ref[:, lanes])):
            scores = dot(query, keys, 1, 1) + mask_ref[0:1, :full]
            exponent = jnp.exp(scores - jnp.max(scores, axis=-1, keepdims=True))
            norm = jnp.sum(exponent, axis=-1, keepdims=True)
            att = (exponent * (1.0 / norm)).astype(BF16)
            att_ref[slot, head] = att
            parts.append(dot(att, values))
        ctx_ref[:, lanes] = join(*parts).astype(BF16)
        attention_store(p, slot).start()

    for p in (HEADS // 2 - 2, HEADS // 2 - 1):
        attention_store(p, p % 2).wait()
    for p in range(2):
        attention_load(p, p).start()

    per = u_ref.shape[3]
    up, down, out, qkv = 0, steps, 2 * steps, 2 * steps + 1
    last = qkv + 3
    pair_width = 2 * HEAD_DIM

    def buffer(unit):
        if isinstance(unit, int) and unit >= last - 1:
            return uh_ref.at[unit - last + 1], r0h_ref.at[unit - last + 1], rh_ref.at[unit - last + 1]
        return u_ref.at[unit], r0_ref.at[unit], r_ref.at[unit]

    def is_last(unit):
        return isinstance(unit, int) and unit == last

    def remote(unit, sem, sent, landing, target):
        return pltpu.make_async_remote_copy(
            src_ref=sent,
            dst_ref=landing,
            send_sem=send_sem.at[unit, sem],
            recv_sem=recv_sem.at[unit, sem],
            device_id=target,
            device_id_type=mesh_ids,
        )

    def remaining(axes, stage):
        count = 16
        for axis in axes[: stage - 1]:
            count //= 4 if axis == 2 else 2
        return count

    def land_at(axes, stage):
        return 14 if stage == 3 and axes[2] != 2 else LAND_AT[stage]

    def is_down(unit):
        return isinstance(unit, int) and down <= unit < out

    def natural(i, unit, axes):
        count, number, rest = 16, 0, i
        for axis in axes:
            count //= 4 if axis == 2 else 2
            digit, rest = rest // count, rest % count
            if axis == 2:
                number = number + (digit if is_down(unit) else 4 * digit)
            else:
                number = number + (1, 2)[axis] * (4 if is_down(unit) else 1) * differs(digit, bits[axis])
        return number

    def arrived(unit, stage, axes):
        held_ref, first_ref, later_ref = buffer(unit)
        if stage == 0:

            def fresh(i):
                n = natural(i, unit, axes)
                return held_ref[core, n] + first_ref[n]

            return 16, fresh
        if is_last(unit):
            axis, count, held, landing = (None, 4, 0, 0) if stage == 1 else (2, 1, z, LAND_AT[3])
        else:
            axis, landing = axes[stage - 1], land_at(axes, stage)
            count = remaining(axes, stage + 1)
            held = z * count if axis == 2 else 0

        def piece(i):
            if stage < 3 and axis in (0, 1):
                return held_ref[1 - core, held + i] + later_ref[landing + i]
            value = held_ref[1 - core, held + i].astype(F32)
            for n in range(3 if axis in (None, 2) else 1):
                value = value + later_ref[landing + n * count + i].astype(F32)
            return value

        return count, piece

    def transfers(unit, stage, axes):
        held_ref, first_ref, later_ref = buffer(unit)
        if stage == 0:
            return [remote(unit, 0, held_ref.at[1 - core], first_ref, partner_core)]
        if stage < 3 and is_last(unit):
            targets = (partner_y, partner_x, partner_xy)
            return [
                remote(
                    unit,
                    1 + i,
                    held_ref.at[1 - core, pl.ds(4 + 4 * i, 4)],
                    later_ref.at[pl.ds(4 * i, 4)],
                    targets[i],
                )
                for i in range(3)
            ]
        where = 1 - core if stage == 1 else core
        if is_last(unit):
            sent, landing, count = SEND_AT[3], LAND_AT[3], 4
        else:
            sent, landing, count = SEND_AT[stage], land_at(axes, stage), remaining(axes, stage)
            if axes[stage - 1] != 2:
                half_count = count // 2
                return [
                    remote(
                        unit,
                        stage,
                        held_ref.at[where, pl.ds(sent, half_count)],
                        later_ref.at[pl.ds(landing, half_count)],
                        plane[axes[stage - 1]],
                    )
                ]
        count //= 4
        return [
            remote(
                unit,
                4 + i,
                held_ref.at[where, pl.ds(sent + (z + 1 + i) % 4 * count, count)],
                later_ref.at[pl.ds(landing + i * count, count)],
                along_z[i],
            )
            for i in range(3)
        ]

    def start(unit, stage, axes):
        for copy in transfers(unit, stage, axes):
            copy.start()

    def finish(unit, stage, axes):
        for copy in transfers(unit, stage, axes):
            copy.wait()

    def down_send(j, unit):
        place = (j - z + 3) % 4
        return [
            remote(
                unit,
                4 + place,
                u_ref.at[unit, core, pl.ds(SEND_AT[3], 4)],
                rz_ref.at[place],
                {"dp": 2 * j + y},
            )
        ]

    def add_up(unit, stage, axes):
        held_ref, first_ref, later_ref = buffer(unit)
        count, piece = arrived(unit, stage, axes)
        following = 3 if is_last(unit) and stage == 1 else stage + 1
        sent, where = SEND_AT[following], 1 - core if following == 1 else core
        if is_last(unit) and stage == 0:

            @pl.loop(0, 16)
            def _(i):
                held_ref[1 - core, i] = piece(i).astype(BF16)

        elif is_last(unit) or axes[following - 1] == 2:

            @pl.loop(0, count)
            def _(i):
                value = piece(i).astype(BF16)
                held_ref[1 - core, i] = value
                held_ref[where, sent + i] = value

        else:

            @pl.loop(0, count // 2)
            def _(i):
                stays, goes = piece(i), piece(count // 2 + i)
                held_ref[1 - core, i] = stays.astype(BF16)
                held_ref[where, sent + i] = goes.astype(BF16)

    def go_on(unit, stage, axes):
        following = 3 if is_last(unit) and stage == 1 else stage + 1
        if following == 3 and is_down(unit):
            chunk = unit - down

            @pl.when(z != chunk)
            def _():
                for copy in down_send(chunk, unit):
                    copy.start()

        else:
            start(unit, following, axes)

    def total(unit, axes):
        finish(unit, 3, axes)
        _, piece = arrived(unit, 3, axes)
        return piece(0) * factor

    def store_unit(unit, value, first=0, chunk=False):
        held_ref, lanes = buffer(unit)[0], value.shape[1]
        for n in range(32):
            piece, side = (4 * (n // 8) + n % 4, n // 4 % 2) if chunk else (n // 2, n % 2)
            held_ref[side, piece, :, first : first + lanes] = value[n * per : (n + 1) * per].astype(BF16)

    def vector_copy(late, n):
        ref, recv = (vl_ref, vlrecv_ref) if late else (ve_ref, verecv_ref)
        if late:
            target = ([partner_core, partner_x, partner_y, partner_xy] + along_z)[n]
        else:
            target = ([partner_core, partner_x, partner_y] + along_z)[n]
        return pltpu.make_async_remote_copy(
            src_ref=ref,
            dst_ref=recv.at[n],
            send_sem=v_send_sem.at[late, n],
            recv_sem=v_recv_sem.at[late, n],
            device_id=target,
            device_id_type=mesh_ids,
        )

    STEPS = (((0,), (1,), (2,), (3, 4, 5)), ((0,), (1, 2, 3), (4, 5, 6)))

    def vector_wait(late, n):
        for i in STEPS[late][n - 1] if n else ():
            vector_copy(late, i).wait()

    def vector_add(late, n):
        ref, recv = (vl_ref, vlrecv_ref) if late else (ve_ref, verecv_ref)
        for i in STEPS[late][n - 1] if n else ():
            ref[...] += recv[i]

    def vector_go_on(late, n):
        for i in STEPS[late][n] if n < len(STEPS[late]) else ():
            vector_copy(late, i).start()

    orders, in_chunk, after_mlp, in_pair, after_proj, tail = plan

    def run(events):
        for unit, stage in events:
            if unit == "give":
                for copy in give(*((layer_out_ref, 0), (in_grad_ref, 1))[stage]):
                    copy.start()
            elif unit in ("early", "late"):
                late = int(unit == "late")
                vector_wait(late, stage)
                vector_add(late, stage)
                vector_go_on(late, stage)
            else:
                finish(unit, stage, orders[unit])
                add_up(unit, stage, orders[unit])
                go_on(unit, stage, orders[unit])

    load(1).wait()
    middle = x_ref[...].astype(F32) + dot(ctx_ref[...], wo_ref[...]) + par_ref[0:1, :]
    mid_ref[...] = middle
    unit_mid, _ = normalize(middle)
    n2_ref[...] = (unit_mid * par_ref[1:2, :] + par_ref[2:3, :]).astype(BF16)
    acc_ref[...] = middle + par_ref[3:4, :]
    dn_ref[...] = jnp.zeros_like(dn_ref)
    vl_ref[...] = jnp.zeros_like(vl_ref)
    load(2).wait()
    rows_copy(1).wait()
    rows_copy(3).wait()

    def chunk_events(j, where):
        for n in range(steps):
            if in_chunk[n][where]:

                @pl.when(j == n)
                def _(n=n):
                    run(in_chunk[n][where])

    @pl.loop(0, steps)
    def _(j):
        slot = j % 2
        for copy in weights(j, slot):
            copy.wait()

        @pl.when(j + 1 < steps)
        def _():
            for copy in weights(j + 1, 1 - slot):
                copy.start()

        normed = n2_ref[...]
        grad_low = g_ref[...]
        wu, wd = w_ref.at[slot], w_ref.at[2 + slot]
        pre = dot(normed, wu[...]) + par_ref[pl.ds(8 + j, 1), :]
        phi = 0.5 * (1.0 + lax.erf(pre * math.sqrt(0.5)))
        hidden = (pre * phi).astype(BF16)
        slope = phi + pre * (jnp.exp(-0.5 * pre * pre) * (1.0 / math.sqrt(2 * math.pi)))
        chunk_events(j, 0)
        acc_ref[...] += dot(hidden, wd[...])
        store_unit(down + j, dot(hidden, grad_low, 0, 0), chunk=True)
        grad_pre = dot(grad_low, wd[...], 1, 1) * slope
        ve_ref[pl.ds(4 + j, 1), :] = column_sum(grad_pre)
        gpre_low = grad_pre.astype(BF16)
        chunk_events(j, 1)
        store_unit(up + j, dot(normed, gpre_low, 0, 0))
        dn_ref[...] += dot(gpre_low, wu[...], 1, 1)
        start(down + j, 0, orders[down])
        start(up + j, 0, orders[up])
        chunk_events(j, 2)

    for i in range(3):
        proj_weights(i).start()
    res_ref[0] = acc_ref[...].astype(BF16)

    def give(ref, n):
        mine_copy = pltpu.make_async_copy(res_ref.at[n, pl.ds(0, half)], ref.at[mine], io_sem.at[n])
        other_copy = pltpu.make_async_remote_copy(
            src_ref=res_ref.at[n, pl.ds(half, half)],
            dst_ref=ref.at[mine],
            send_sem=io_send_sem.at[n],
            recv_sem=io_recv_sem.at[n],
            device_id=partner_x,
            device_id_type=mesh_ids,
        )
        return mine_copy, other_copy

    unit_mid, scale = normalize(mid_ref[...])
    dn = dn_ref[...]
    grad = g_ref[...].astype(F32)
    gmid = grad + normalize_back(unit_mid, scale, par_ref[1:2, :], dn)
    ve_ref[0:1, :] = column_sum(gmid)
    ve_ref[1:2, :] = column_sum(dn * unit_mid)
    ve_ref[2:3, :] = column_sum(dn)
    ve_ref[3:4, :] = column_sum(grad)
    acc_ref[...] = gmid
    low = gmid.astype(BF16)
    store_unit(out, dot(ctx_ref[...], low, 0, 0))
    gctx_ref[...] = dot(low, wo_ref[...], 1, 1).astype(BF16)
    start(out, 0, orders[out])
    dn_ref[...] = jnp.zeros_like(dn_ref)
    run(after_mlp)

    third = 2 * pair_width

    def exchange(p):
        return pltpu.make_async_remote_copy(
            src_ref=dsend_ref.at[p % 3],
            dst_ref=drecv_ref.at[p],
            send_sem=dk_send_sem.at[p],
            recv_sem=dk_recv_sem.at[p],
            device_id=partner_core,
            device_id_type=mesh_ids,
        )

    def project(pairs, unit):
        span = len(pairs) * pair_width
        for i, p in enumerate(pairs):
            exchange(p).wait()
            lane = slice(p * pair_width, (p + 1) * pair_width)
            here = slice(i * pair_width, (i + 1) * pair_width)
            for n in range(2):
                grad = down_ref[p % 3, n] + drecv_ref[p, n].astype(F32)
                if n == 1:
                    vl_ref[3:4, lane] = column_sum(grad)
                dg_ref[1 + n, :, here] = grad.astype(BF16)
            dg_ref[0, :, here] = dq_of(p)
        cols = slice(pairs[0] * pair_width, pairs[0] * pair_width + span)
        for n in range(3):
            store_unit(unit, dot(n1_ref[...], dg_ref[n, :, :span], 0, 0), n * span)
        more = dot(dg_ref[0, :, :span], w_ref[0, :, cols], 1, 1)
        for n in range(1, 3):
            more = more + dot(dg_ref[n, :, :span], w_ref[n, :, cols], 1, 1)
        dn_ref[...] += more
        start(unit, 0, orders[unit])

    def dq_of(p):
        return dg_ref[3, :, (p % 3) * pair_width : (p % 3 + 1) * pair_width]

    def attention_pair(p, slot, third_slot, between):
        attention_load(p, slot).wait()
        lanes = pl.ds(pl.multiple_of(p * pair_width, pair_width), pair_width)
        keys = jnp.concatenate([kv_ref[0, :, lanes], kvo_ref[0, :, lanes]], axis=0)
        values = jnp.concatenate([kv_ref[1, :, lanes], kvo_ref[1, :, lanes]], axis=0)
        queries = q_ref[:, lanes]
        gctx = gctx_ref[:, lanes]
        dq, dk, dv = [], [], []
        for head, grad in enumerate(halves(gctx)):
            att = att_ref[slot, head]
            wide = att.astype(F32)
            datt = dot(grad, values, 1, 1)
            inner = jnp.sum(wide * datt, axis=-1, keepdims=True)
            dscore = (wide * (datt - inner)).astype(BF16)
            dq.append(dot(dscore, keys))
            dk.append(dot(dscore, queries, 0, 0))
            dv.append(dot(att, gctx, 0, 0))
            if head == 0:
                between()
        dquery = join(*dq) * 0.125
        dg_ref[3, :, pl.ds(pl.multiple_of(third_slot * pair_width, pair_width), pair_width)] = dquery.astype(BF16)
        vl_ref[2:3, lanes] = column_sum(dquery)
        for n, grad in enumerate((join(*dk), join(*dv))):
            down_ref[third_slot, n] = grad[:rows]
            dsend_ref[third_slot, n] = grad[rows:].astype(BF16)
        exchange(p).start()

    def pairs_loop(first, count):
        def pair_events(i, where):
            for n in range(count):
                if in_pair[first + n][where]:

                    @pl.when(i == n)
                    def _(n=n):
                        run(in_pair[first + n][where])

        @pl.loop(0, count)
        def _(i):
            p = first + i
            attention_pair(p, p % 2, p % 3, lambda: pair_events(i, 0))

            @pl.when(p + 2 < HEADS // 2)
            def _():
                attention_load(p + 2, p % 2).start()

            pair_events(i, 1)

    pairs_loop(0, 3)
    for i in range(3):
        proj_weights(i).wait()
    project((0, 1), qkv)
    run(after_proj[0])
    pairs_loop(3, 2)
    project((2, 3), qkv + 1)
    run(after_proj[1])
    pairs_loop(5, 1)
    project((4,), last - 1)
    run(after_proj[2])
    project((5,), last)
    run(after_proj[3])

    unit_in, scale = normalize(x_ref[...].astype(F32))
    dn = dn_ref[...]
    vl_ref[0:1, :] = column_sum(dn * unit_in)
    vl_ref[1:2, :] = column_sum(dn)
    vector_go_on(1, 0)
    res_ref[1] = (acc_ref[...] + normalize_back(unit_in, scale, par_ref[4:5, :], dn)).astype(BF16)
    cut = tail.index(("give", 1)) + 1
    run(tail[:cut])
    for j in range(steps):
        dup_ref[:, j * width : (j + 1) * width] = total(up + j, orders[up + j])
    for j in range(steps):

        @pl.when(z == j)
        def _(j=j):
            for i in range(3):
                remote(down + j, 4 + i, rz_ref.at[i], rz_ref.at[i], along_z[i]).wait_recv()
            for part in range(steps):
                value = u_ref[down + j, 1 - core, part].astype(F32)
                for i in range(3):
                    value = value + rz_ref[i, part].astype(F32)
                ddown_ref[part * per : (part + 1) * per, :] = value * factor

        @pl.when(z != j)
        def _(j=j):
            for copy in down_send(j, down + j):
                copy.wait_send()

    dout_ref[...] = total(out, orders[out])
    run(tail[cut:])

    me = dp * lax.axis_size("seq") + seq
    both = jnp.concatenate([ve_ref[...], vl_ref[...]], axis=0) * factor
    turned = pltpu.roll(both, (width - me * per) % width, 1)
    small_ref[...] = turned[:, : small_ref.shape[1]]
    per_up = steps * per
    row = (me * per_up) // width
    up_bias = jnp.broadcast_to(ve_ref[pl.ds(4 + row, 1), :] * factor, (8, width))
    shift = (width - (me * per_up - row * width)) % width
    upb_ref[...] = pltpu.roll(up_bias, shift, 1)[:, : upb_ref.shape[1]]

    for pairs, unit in (((0, 1), qkv), ((2, 3), qkv + 1), ((4,), last - 1), ((5,), last)):
        value = total(unit, orders[unit])
        span = len(pairs) * pair_width
        for n in range(3):
            at = n * width + pairs[0] * pair_width
            dqkv_ref[:, at : at + span] = value[:, n * span : (n + 1) * span]
    for n, ref in enumerate((layer_out_ref, in_grad_ref)):
        for copy in give(ref, n):
            copy.wait()

def results_kernel(small_ref, upb_ref, *refs):
    count = (len(refs) - 11) // 3
    big_in, outs, vectors, rooms = refs[:count], refs[count : 2 * count], refs[2 * count : -2 - count], refs[-2 - count : -2]
    in_sem, out_sem = refs[-2:]
    reads = [pltpu.make_async_copy(big_in[i], rooms[i], in_sem.at[i]) for i in range(count)]
    writes = [pltpu.make_async_copy(rooms[i], outs[i], out_sem.at[i]) for i in range(count)]
    for copy in reads:
        copy.start()
    for i, row in enumerate((8, 9, 10, 11, 0, 1, 2, 3)):
        vectors[i][...] = small_ref[row : row + 1, : vectors[i].shape[1]]
    vectors[8][...] = upb_ref[0:1, : vectors[8].shape[1]]
    for read, write in zip(reads, writes):
        read.wait()
        write.start()
    for copy in writes:
        copy.wait()


PLAN = (((1, 2, 0), (1, 2, 0), (0, 2, 1), (1, 2, 0), (0, 1, 2), (0, 1, 2), (0, 1, 2), (1, 0, 2), (0, 1, 2), (1, 0, 2), (1, 0, 2), (0, 1, 2), (0, 1, 2)), (((), (), ()), ((), (), ((0, 0), (4, 0))), ((), (), ((1, 0), (5, 0))), ((), (), ((2, 0), (6, 0), (0, 1), (4, 1)))), (('early', 0), (3, 0), (7, 0), (1, 1), (5, 1), ('early', 1)), (((), ((8, 0), (4, 2), (0, 2), (2, 1))), ((), ()), ((), ((3, 1), (1, 2))), ((), ((9, 0), (5, 2))), ((), ((8, 1), (6, 2), ('early', 3), ('give', 0))), ((), ((10, 0), (9, 1)))), (((6, 1), ('early', 2), (7, 1)), ((2, 2), (7, 2)), ((3, 2), (8, 2)), ((11, 0),)), ((9, 2), (12, 0), ('late', 1), (10, 1), ('early', 4), (11, 1), (12, 1), ('late', 2), ('give', 1), (11, 2), (10, 2), ('late', 3)))


def on_device(
    layer_in,
    out_grad,
    pre_gain,
    pre_bias,
    qkv_w,
    q_bias,
    v_bias,
    out_w,
    out_b,
    mid_gain,
    mid_bias,
    up_w,
    up_b,
    down_w,
    down_b,
    patch_keep,
    text_len,
):
    seq_here, half, width = layer_in.shape
    dp, seq = lax.axis_size("dp"), lax.axis_size("seq")
    assert seq_here == 2 and seq == 4
    full = half * seq
    rows = 2 * half
    ff = up_w.shape[1]
    steps = ff // width
    devices = dp * seq
    place_seq = lax.axis_index("seq")
    me = lax.axis_index("dp") * seq + place_seq
    mine, core = place_seq // 2, place_seq % 2

    bits = devices.bit_length() - 1
    halving = (dp, seq) == (8, 4) and width % (8 * devices) == 0
    if halving:
        shards, at_me, at_core = devices, me, core
        dp_bits = list(range(2, bits))
        order_x = [1] + dp_bits
        order_y = dp_bits[:1] + [1] + dp_bits[1:]
        order_z = dp_bits[1:] + [1] + dp_bits[:1]
    else:
        shards, at_me, at_core = 32, 0, 0
        order_x = order_y = order_z = [4, 3, 2, 1]
    per = width // shards
    per_down = ff // shards
    pairs = shards // 2
    info = jnp.stack(
        [
            jnp.asarray(v, jnp.int32)
            for v in (
                mine,
                at_core,
                place(at_me >> 1, order_x),
                place(at_me >> 1, order_y),
                place(at_me >> 1, order_z),
                me,
            )
        ]
    )

    def swap(value, bit):
        if bit < 2:
            return lax.ppermute(value, "seq", [(i, i ^ (1 << bit)) for i in range(seq)])
        return lax.ppermute(value, "dp", [(i, i ^ (1 << (bit - 2))) for i in range(dp)])

    row = lambda v: v.reshape(-1, width)
    own_rows = pl.BlockSpec((1, half, width), lambda i, info: (info[0], 0, 0))
    vec = fixed((1, width))
    act = fixed((rows, width))

    factor = 1.0 / math.sqrt(seq_here * full * dp)
    per_vec, per_up = width // devices, ff // devices
    if halving:
        hbm = pl.BlockSpec(memory_space=pl.ANY)
        units = 2 * steps + 4
        big = lambda *shape: pltpu.VMEM(shape, F32)
        low = lambda *shape: pltpu.VMEM(shape, BF16)
        dma = lambda *shape: pltpu.SemaphoreType.DMA(shape)
        operands = (layer_in, out_grad, qkv_w, out_w, up_w, down_w)
        vectors = (out_b, mid_gain, mid_bias, down_b, pre_gain, pre_bias, q_bias, v_bias, up_b, patch_keep)
        results = [(per, ff), (per_down, width), (per, width), (per, 3 * width), (16, 128), (8, 128)]
        *large, small, up_bias, _ = pl.pallas_call(
            functools.partial(back_kernel, factor, PLAN),
            in_specs=[hbm] * len(operands)
            + [fixed(v.shape) for v in vectors]
            + [pl.BlockSpec(memory_space=pltpu.SMEM)],
            out_shape=[shape_of(layer_in.shape, BF16)] * 2 + [shape_of(s, F32) for s in results]
            + [shape_of((HEADS, rows, full), BF16)],
            out_specs=[hbm] * 2 + [fixed(s) for s in results] + [hbm],
            scratch_shapes=[
                big(16, width),
                big(8, pl.cdiv(full, 128) * 128),
                low(rows, width),
                low(rows, width),
                low(rows, width),
                low(rows, width),
                low(rows, width),
                low(2, rows, width),
                low(2, rows, width),
                low(2, 2, rows, full),
                low(width, width),
                low(4, width, width),
                big(rows, width),
                big(rows, width),
                big(rows, width),
                low(rows, width),
                low(rows, width),
                low(4, rows, 6 * HEAD_DIM),
                big(3, 2, rows, 2 * HEAD_DIM),
                low(3, 2, rows, 2 * HEAD_DIM),
                low(6, 2, rows, 2 * HEAD_DIM),
                low(2, rows, width),
                big(8, width),
                big(8, width),
                big(6, 8, width),
                big(7, 8, width),
                low(units - 1, 2, 16, per, width),
                low(units - 1, 16, per, width),
                low(units - 1, 16, per, width),
                low(2, 2, 16, per, width // 2),
                low(2, 16, per, width // 2),
                low(2, 16, per, width // 2),
                low(3, steps, per, width),
                dma(3),
                dma(7),
                dma(4),
                dma(units + 1, 7),
                dma(units + 1, 7),
                dma(6),
                dma(6),
                dma(2, 7),
                dma(2, 7),
                dma(2),
                dma(2),
                dma(2),
                dma(4),
                dma(4),
                dma(4),
                dma(4),
            ],
            compiler_params=pltpu.CompilerParams(
                vmem_limit_bytes=64 * 1024 * 1024, collective_id=0, has_side_effects=True
            ),
        )(*operands, *vectors, text_len)
        vec_shapes = [(1, per_vec)] * 8 + [(1, per_up)]
        whole = pl.pallas_call(
            results_kernel,
            in_specs=[pl.BlockSpec(memory_space=pltpu.VMEM)] * 2 + [hbm] * len(large),
            out_shape=[shape_of(v.shape, v.dtype) for v in large] + [shape_of(s, F32) for s in vec_shapes],
            out_specs=[hbm] * len(large) + [pl.BlockSpec(memory_space=pltpu.VMEM)] * len(vec_shapes),
            scratch_shapes=[pltpu.VMEM(v.shape, v.dtype) for v in large] + [dma(len(large)), dma(len(large))],
        )(small, up_bias, *large)
        layer_out, in_grad, d_wup, d_wdown, d_wout, d_qkv = whole[:6]
        d_pregain, d_prebias, d_qbias, d_vbias, d_outbias, d_midgain, d_midbias, d_downbias, d_upbias = (
            v.reshape(-1) for v in whole[6:]
        )
        return (
            layer_out,
            in_grad,
            d_pregain,
            d_prebias,
            d_qkv,
            d_qbias,
            d_vbias,
            d_wout,
            d_outbias,
            d_midgain,
            d_midbias,
            d_wup,
            d_upbias,
            d_wdown,
            d_downbias,
        )

    x_other = swap(lax.dynamic_index_in_dim(layer_in, 1 - mine, 0, False), 1)
    g_other = swap(lax.dynamic_index_in_dim(out_grad, 1 - mine, 0, False), 1)

    patches = lax.dynamic_index_in_dim(patch_keep, mine, 0, False)
    length = lax.dynamic_index_in_dim(text_len, mine, 0, False)
    valid = jnp.concatenate(
        [
            jnp.ones((2,), jnp.int32),
            patches,
            jnp.ones((1,), jnp.int32),
            (jnp.arange(TEXT, dtype=jnp.int32) < length).astype(jnp.int32),
            jnp.zeros((full - 3 - PATCHES - TEXT,), jnp.int32),
        ]
    )
    valid = valid.reshape(seq, half)
    valid = jnp.concatenate(
        [lax.dynamic_index_in_dim(valid, place_seq ^ turn, 0, True) for turn in (0, 2, 1, 3)], axis=1
    )
    mask = jnp.where(valid > 0, 0.0, -1e30).astype(F32)

    square = 2 * rows * width * width
    kv_bias = jnp.concatenate([jnp.zeros((1, 1, width), F32), v_bias.reshape(1, 1, width)], axis=0)
    n1, kv = call(
        qkv_kernel,
        (2,),
        [
            own_rows,
            fixed((half, width)),
            vec,
            vec,
            pl.BlockSpec((width, width), lambda i, _: (0, i + 1)),
            pl.BlockSpec((1, 1, width), lambda i, _: (i, 0, 0)),
        ],
        [shape_of((rows, width), BF16), shape_of((2, rows, width), BF16)],
        [act, pl.BlockSpec((1, rows, width), lambda i, _: (i, 0, 0))],
        flops=2 * square,
        nbytes=5 * 10**6,
    )(info, layer_in, x_other, row(pre_gain), row(pre_bias), qkv_w, kv_bias)
    kv_other = swap(kv, 0)
    q = call(
        query_kernel,
        (1,),
        [act, pl.BlockSpec((width, width), lambda i, _: (0, 0)), vec],
        shape_of((rows, width), BF16),
        act,
        flops=square,
        nbytes=3 * 10**6,
    )(info, n1, qkv_w, row(q_bias))

    pair_width = 2 * HEAD_DIM
    blocks = width // pair_width
    col = pl.BlockSpec((rows, pair_width), lambda i, _: (0, i))
    col2 = pl.BlockSpec((2, rows, pair_width), lambda i, _: (0, 0, i))
    att_spec = pl.BlockSpec((2, rows, full), lambda i, _: (i, 0, 0))
    head_flops = 2 * rows * full * pair_width * HEADS
    ctx, att = call(
        attention_kernel,
        (blocks,),
        [col, col2, col2, fixed((1, full))],
        [shape_of((rows, width), BF16), shape_of((HEADS, rows, full), BF16)],
        [col, att_spec],
        flops=4 * head_flops,
        nbytes=12 * 10**6,
        trans=HEADS * rows * full,
    )(info, q, kv, kv_other, mask)

    orders = (order_x, order_y, order_z)
    mlp_out = call(
        functools.partial(mlp_kernel, orders, per, per_down, steps),
        (steps,),
        [
            own_rows,
            fixed((half, width)),
            own_rows,
            fixed((half, width)),
            act,
            fixed((width, width)),
            vec,
            vec,
            vec,
            pl.BlockSpec((width, width), lambda i, _: (0, i)),
            pl.BlockSpec((1, 1, width), lambda i, _: (i, 0, 0)),
            pl.BlockSpec((width, width), lambda i, _: (i, 0)),
            vec,
        ],
        [
            shape_of((half, width), BF16),
            shape_of((half, width), BF16),
            shape_of((rows, width), F32),
            shape_of((rows, width), BF16),
            shape_of((4 + steps, width), F32),
            shape_of((pairs, steps, per, width), BF16),
            shape_of((pairs, steps, per, width), F32),
            shape_of((pairs, per_down, width), BF16),
            shape_of((pairs, per_down, width), F32),
            shape_of((pairs, per, width), BF16),
            shape_of((pairs, per, width), F32),
        ],
        [
            fixed((half, width)),
            fixed((half, width)),
            act,
            act,
            fixed((4 + steps, width)),
            pl.BlockSpec((pairs, 1, per, width), lambda i, _: (0, i, 0, 0)),
            pl.BlockSpec((pairs, 1, per, width), lambda i, _: (0, i, 0, 0)),
            fixed((pairs, per_down, width)),
            fixed((pairs, per_down, width)),
            fixed((pairs, per, width)),
            fixed((pairs, per, width)),
        ],
        scratch=[
            pltpu.VMEM((rows, width), F32),
            pltpu.VMEM((rows, width), BF16),
            pltpu.VMEM((rows, width), F32),
            pltpu.VMEM((rows, width), F32),
            pltpu.VMEM((width, width), F32),
        ],
        flops=(6 * steps + 3) * square,
        nbytes=40 * 10**6,
        trans=2 * rows * ff,
    )(
        info,
        layer_in,
        x_other,
        out_grad,
        g_other,
        ctx,
        out_w,
        row(out_b),
        row(mid_gain),
        row(mid_bias),
        up_w,
        up_b.reshape(steps, 1, width),
        down_w,
        row(down_b),
    )
    out_own, out_other, gmid, gctx, early, s_up, k_up, s_down, k_down, s_out, k_out = mlp_out
    out_back = swap(out_other, 1)

    def reduce(sent, kept, order):
        got = swap(sent, 0)
        for bit in order:
            total = kept + got.astype(F32)
            cut = total.shape[0] // 2
            kept = total[:cut]
            got = swap(total[cut:].astype(BF16), bit)
        return kept, got

    def natural(sent, kept):
        return jnp.stack([kept, sent.astype(F32)], axis=1)

    if halving:
        up_pair = reduce(s_up, k_up, order_x)
        down_pair = reduce(s_down, k_down, order_y)
        out_pair = reduce(s_out, k_out, order_z)

    dq, dbq, dkv_own, dkv_send = call(
        attention_back_kernel,
        (blocks,),
        [att_spec, col, col2, col2, col],
        [
            shape_of((rows, width), BF16),
            shape_of((1, width), F32),
            shape_of((2, rows, width), F32),
            shape_of((2, rows, width), BF16),
        ],
        [col, pl.BlockSpec((1, pair_width), lambda i, _: (0, i)), col2, col2],
        flops=8 * head_flops,
        nbytes=16 * 10**6,
    )(info, att, q, kv, kv_other, gctx)
    dkv_other = swap(dkv_send, 0)
    shard = fixed((pairs, per, width))
    tile = pltpu.VMEM((width, width), F32)
    dn_q, s_q, k_q = call(
        functools.partial(query_back_kernel, order_x, per),
        (1,),
        [act, act, pl.BlockSpec((width, width), lambda i, _: (0, 0))],
        [shape_of((rows, width), F32), shape_of((pairs, per, width), BF16), shape_of((pairs, per, width), F32)],
        [act, shard, shard],
        scratch=[tile],
        flops=2 * square,
        nbytes=6 * 10**6,
    )(info, n1, dq, qkv_w)
    dkv, dbv, s_k, k_k, s_v, k_v = call(
        functools.partial(key_value_back_kernel, (order_x, order_y), per),
        (1,),
        [act, fixed((2, rows, width)), fixed((2, rows, width))],
        [
            shape_of((2, rows, width), BF16),
            shape_of((1, width), F32),
            shape_of((pairs, per, width), BF16),
            shape_of((pairs, per, width), F32),
            shape_of((pairs, per, width), BF16),
            shape_of((pairs, per, width), F32),
        ],
        [fixed((2, rows, width)), vec, shard, shard, shard, shard],
        scratch=[tile],
        flops=2 * square,
        nbytes=10 * 10**6,
    )(info, n1, dkv_own, dkv_other)
    if halving:
        q_pair = reduce(s_q, k_q, order_x)
        k_pair = reduce(s_k, k_k, order_x)
        v_pair = reduce(s_v, k_v, order_y)
    in_own, in_other, late = call(
        input_back_kernel,
        (1,),
        [
            own_rows,
            fixed((half, width)),
            vec,
            fixed((2, rows, width)),
            fixed((width, 3 * width)),
            act,
            act,
            vec,
            vec,
        ],
        [shape_of((half, width), BF16), shape_of((half, width), BF16), shape_of((8, width), F32)],
        [fixed((half, width)), fixed((half, width)), fixed((8, width))],
        flops=2 * square,
        nbytes=10 * 10**6,
    )(info, layer_in, x_other, row(pre_gain), dkv, qkv_w, dn_q, gmid, dbq, dbv)
    in_back = swap(in_other, 1)

    def give_back(own, other):
        first = jnp.where(mine == 0, own, other)
        second = jnp.where(mine == 0, other, own)
        return jnp.stack([first, second])

    layer_out = give_back(out_own, out_back)
    in_grad = give_back(in_own, in_back)

    factor = 1.0 / math.sqrt(seq_here * full * dp)
    vectors = jnp.concatenate([early, late], axis=0)
    if halving:
        for bit in range(bits):
            vectors = vectors + swap(vectors, bit)
    else:
        vectors = lax.psum(vectors, ("dp", "seq"))
    per_vec, per_up = width // devices, ff // devices
    early_rows = 4 + steps
    small, up_bias = call(
        functools.partial(vector_kernel, factor, per_vec, per_up),
        (1,),
        [
            pl.BlockSpec((early_rows, width), lambda i, _: (0, 0)),
            pl.BlockSpec((8, width), lambda i, _: (early_rows // 8, 0)),
        ],
        [shape_of((early_rows + 8, 128), F32), shape_of((8, 128), F32)],
        [fixed((early_rows + 8, 128)), fixed((8, 128))],
    )(info, vectors, vectors)
    pick = lambda i: small[i, :per_vec]
    d_upbias = up_bias[0, :per_up]
    d_outbias, d_midgain, d_midbias, d_downbias = (pick(i) for i in range(4))
    d_pregain, d_prebias, d_qbias, d_vbias = (pick(early_rows + i) for i in range(4))

    if halving:

        def finish(named):
            operands = [v for pair, _ in named for v in pair]
            shapes = [s for _, s in named]
            return call(
                functools.partial(finish_kernel, factor),
                (1,),
                [fixed(v.shape) for v in operands],
                [shape_of(s, F32) for s in shapes],
                [fixed(s) for s in shapes],
            )(info, *operands)

        d_wup, d_wdown, d_wout = finish(
            [(up_pair, (per, ff)), (down_pair, (per_down, width)), (out_pair, (per, width))]
        )
        d_q, d_k, d_v = finish([(pair, (per, width)) for pair in (q_pair, k_pair, v_pair)])
        d_qkv = jnp.concatenate([d_q, d_k, d_v], axis=1)
    else:

        def scatter(value):
            return lax.psum_scatter(value, ("dp", "seq"), scatter_dimension=0, tiled=True) * factor

        d_wup = scatter(
            natural(s_up, k_up).transpose(0, 1, 3, 2, 4).reshape(width, ff)
        )
        d_wdown = scatter(natural(s_down, k_down).reshape(ff, width))
        d_wout = scatter(natural(s_out, k_out).reshape(width, width))
        d_qkv = scatter(
            jnp.concatenate(
                [natural(s, k).reshape(width, width) for s, k in ((s_q, k_q), (s_k, k_k), (s_v, k_v))],
                axis=1,
            )
        )
    return (
        layer_out,
        in_grad,
        d_pregain,
        d_prebias,
        d_qkv,
        d_qbias,
        d_vbias,
        d_wout,
        d_outbias,
        d_midgain,
        d_midbias,
        d_wup,
        d_upbias,
        d_wdown,
        d_downbias,
    )


def solution(mesh):
    both = ("dp", "seq")
    rows = P("dp", "seq", None)
    return jax.shard_map(
        on_device,
        mesh=mesh,
        in_specs=(rows, rows) + (P(),) * 13 + (P("dp", None), P("dp")),
        out_specs=(
            rows,
            rows,
            P(both),
            P(both),
            P(both, None),
            P(both),
            P(both),
            P(both, None),
            P(both),
            P(both),
            P(both),
            P(both, None),
            P(both),
            P(both, None),
            P(both),
        ),
        check_vma=False,
    )
```
